32 devices in a mesh: grp: 2 (over y), row: 16 (over z, x, core), col: 1.
Axes of the slice: x: 2, y: 2, z: 4, core: 2. Of those that a mesh axis runs over, the one named last changes fastest.
Arguments:
- alignment_state: bfloat16 [64, 128, 64], P(('grp', 'row'), 'col'), parts along dimension 0, may hold values from -6 to 6
- pair_state: bfloat16 [256, 128, 128], P(('grp', 'row'), 'col'), parts along dimension 0, may hold values from -6 to 6
- cotangent: bfloat16 [256, 128, 128], P(('grp', 'row'), 'col'), parts along dimension 0, may hold values from -0.046875 to 0.046875
- sequence_row_mask: int32 [64], P('grp'), parts along dimension 0, may hold values 0 or 1
- residue_mask: int32 [256], P('grp'), parts along dimension 0, may hold values 0 or 1
- norm_gain_vector: float32 [64], replicated, may hold values from 0.1 to 1.9
- left_matrix_weight: bfloat16 [64, 32], replicated, may hold values from -3 to 3
- right_matrix_weight: bfloat16 [64, 32], replicated, may hold values from -3 to 3
- output_weight: bfloat16 [1024, 128], replicated, may hold values from -0.1875 to 0.1875
- output_bias: float32 [128], replicated, may hold values from -4 to 4
- gate_matrix: bfloat16 [128, 128], replicated, may hold values from -0.5 to 0.5
Outputs:
- pair_update: bfloat16 [256, 128, 128], P(('grp', 'row'), 'col'), parts along dimension 0
- grad_left: float32 [128, 32], P('grp'), parts along dimension 0
- grad_right: float32 [128, 32], P('grp'), parts along dimension 0
- grad_out: float32 [2048, 128], P('grp'), parts along dimension 0
- grad_gate: float32 [256, 128], P('grp'), parts along dimension 0
The draws below stay inside these ranges and needn't reach their ends.
There are 2 independent parts, one for each index of `grp`. The reference program is written for one: setup_inputs(seed, part) draws one part's arguments, and reference() takes and returns one part's arrays. A program takes and returns all parts, laid end to end along the dimension named above; an argument that names none is the same for every part. Nothing has to cross between parts.
All inputs are finite; a program needn't handle non-finite values.
Results may differ from the reference program's by a relative error of at most 0.0076.
Values may be sent and summed in bfloat16 or wider, within the bound.
A program may use at most 64 MiB of HBM per device.

```python
import jax
import jax.numpy as jnp
from jax import lax

ALIGN_CHANNELS = 64
PROJECT_WIDTH = 32
PAIR_CH = 128
ALIGN_ROWS = 32
CROP_RESIDUES = 128


def place_ends(array, own_key, smallest, largest):
    longest = array.shape.index(max(array.shape))
    spots = []
    for shift in (0, 1):
        where = [jax.random.randint(jax.random.fold_in(own_key, axis), (), 0, length) for axis, length in enumerate(array.shape)]
        where[longest] = (where[longest] + shift) % array.shape[longest]
        spots.append(tuple(where))
    return array.at[spots[0]].set(smallest).at[spots[1]].set(largest)


def block_scale(rng, extent, cuts, low, high):
    def one(axis_at, blocks):
        steps = jax.random.uniform(jax.random.fold_in(jax.random.fold_in(rng, 6), axis_at), (blocks,), jnp.float32, low / len(cuts), high / len(cuts))
        return jnp.repeat(jnp.exp(steps), extent[axis_at] // blocks).reshape((-1,) + (1,) * (len(extent) - axis_at - 1))

    loudness = one(*cuts[0])
    for cut in cuts[1:]:
        loudness = loudness * one(*cut)
    return loudness


def scatter_about(own_key, shape, spread, bound, cuts=(), kind=jnp.bfloat16):
    values = jax.random.normal(own_key, shape, jnp.float32) * spread
    if len(cuts) > 0:
        values = block_scale(own_key, shape, cuts, -0.22, 0.18) * values
    return jnp.clip(values, min=-bound, max=bound).astype(kind)


def setup_inputs(seed: int = 0, part: int = 0) -> dict:
    seeds = jax.random.split(jax.random.key(seed), 12)
    part_keys = jax.random.split(jax.random.fold_in(seeds[11], part), 12)
    alignment_state = scatter_about(part_keys[0], (ALIGN_ROWS, CROP_RESIDUES, ALIGN_CHANNELS), 1.0, 6.0, ((0, 16),))
    pair_state = scatter_about(part_keys[1], (CROP_RESIDUES, CROP_RESIDUES, PAIR_CH), 1.0, 6.0, ((0, 16),))
    cotangent = scatter_about(part_keys[2], (CROP_RESIDUES, CROP_RESIDUES, PAIR_CH), (1.0 / CROP_RESIDUES), 0.046875, ((0, 16),))
    sequence_row_mask = place_ends((jax.random.randint(part_keys[3], (ALIGN_ROWS,), 0, 8) < 7).astype(jnp.int32), jax.random.fold_in(part_keys[3], 1), 0, 1)
    residue_mask = place_ends((jax.random.randint(part_keys[4], (CROP_RESIDUES,), 0, 16) < 15).astype(jnp.int32), jax.random.fold_in(part_keys[4], 1), 0, 1)
    norm_gain_vector = jnp.clip(1.0 + 0.18 * jax.random.normal(seeds[5], (ALIGN_CHANNELS,), jnp.float32), 0.1, 1.9)
    left_matrix_weight = scatter_about(seeds[6], (ALIGN_CHANNELS, PROJECT_WIDTH), 0.5, 3.0)
    right_matrix_weight = scatter_about(seeds[7], (ALIGN_CHANNELS, PROJECT_WIDTH), 0.5, 3.0)
    output_weight = scatter_about(seeds[8], (PROJECT_WIDTH * PROJECT_WIDTH, PAIR_CH), (PROJECT_WIDTH * PROJECT_WIDTH) ** -0.5, 0.1875)
    output_bias = scatter_about(seeds[9], (PAIR_CH,), 1.0, 4.0, (), jnp.float32)
    gate_matrix = scatter_about(seeds[10], (PAIR_CH, PAIR_CH), PAIR_CH ** -0.5, 0.5)
    return dict(alignment_state=alignment_state, pair_state=pair_state, cotangent=cotangent, sequence_row_mask=sequence_row_mask, residue_mask=residue_mask, norm_gain_vector=norm_gain_vector, left_matrix_weight=left_matrix_weight, right_matrix_weight=right_matrix_weight, output_weight=output_weight, output_bias=output_bias, gate_matrix=gate_matrix)


def layer_normalize(alignment_state, norm_gain_vector):
    value_entries = alignment_state.astype(jnp.float32)
    average = lax.optimization_barrier(jnp.mean(value_entries, axis=-1, keepdims=True))
    centred = value_entries - average
    variance = lax.optimization_barrier(jnp.mean(centred * centred, axis=-1, keepdims=True))
    return (centred * lax.rsqrt(variance + 1e-05) * norm_gain_vector).astype(jnp.bfloat16)

def reference(alignment_state, pair_state, cotangent, sequence_row_mask, residue_mask, norm_gain_vector, left_matrix_weight, right_matrix_weight, output_weight, output_bias, gate_matrix):
    feature_values = layer_normalize(alignment_state, norm_gain_vector)
    seq_flags = sequence_row_mask.astype(jnp.float32)
    res_flags = residue_mask.astype(jnp.float32)
    both_mask = seq_flags[:, None] * res_flags[None, :]
    flattened_features = feature_values.reshape(ALIGN_ROWS * CROP_RESIDUES, ALIGN_CHANNELS)
    left_proj = (jnp.dot(flattened_features, left_matrix_weight, preferred_element_type=jnp.float32).reshape(ALIGN_ROWS, CROP_RESIDUES, PROJECT_WIDTH) * both_mask[:, :, None]).astype(jnp.bfloat16)
    right_proj = (jnp.dot(flattened_features, right_matrix_weight, preferred_element_type=jnp.float32).reshape(ALIGN_ROWS, CROP_RESIDUES, PROJECT_WIDTH) * both_mask[:, :, None]).astype(jnp.bfloat16)
    left_rows = left_proj.transpose(1, 2, 0)
    right_flat = right_proj.reshape(ALIGN_ROWS, CROP_RESIDUES * PROJECT_WIDTH)
    row_total = jnp.sum(seq_flags)
    row_block = 32 if CROP_RESIDUES % 32 == 0 else CROP_RESIDUES
    n_blocks = CROP_RESIDUES // row_block
    contract_first = (((0,), (0,)), ((), ()))
    contract_second = (((1,), (1,)), ((), ()))

    def one_block(carry, block_idx):
        grad_out, grad_gate, grad_right_acc = carry
        first_row = block_idx * row_block
        left_blk = lax.dynamic_slice_in_dim(left_rows, first_row, row_block, 0).reshape(row_block * PROJECT_WIDTH, ALIGN_ROWS)
        outer_prod = jnp.dot(left_blk, right_flat, preferred_element_type=jnp.float32)
        outer_prod = outer_prod.reshape(row_block, PROJECT_WIDTH, CROP_RESIDUES, PROJECT_WIDTH).transpose(0, 2, 1, 3)
        outer_prod = outer_prod.reshape(row_block * CROP_RESIDUES, PROJECT_WIDTH * PROJECT_WIDTH).astype(jnp.bfloat16)
        linear = jnp.dot(outer_prod, output_weight, preferred_element_type=jnp.float32) + output_bias
        pair_blk = lax.dynamic_slice_in_dim(pair_state, first_row, row_block, 0).reshape(row_block * CROP_RESIDUES, PAIR_CH)
        gate_val = jax.nn.sigmoid(jnp.dot(pair_blk, gate_matrix, preferred_element_type=jnp.float32))
        blk_flags = lax.dynamic_slice_in_dim(res_flags, first_row, row_block, 0)
        divisor = jnp.maximum(row_total * blk_flags[:, None] * res_flags[None, :], 1.0).reshape(row_block * CROP_RESIDUES, 1)
        cot_blk = lax.dynamic_slice_in_dim(cotangent, first_row, row_block, 0).reshape(row_block * CROP_RESIDUES, PAIR_CH).astype(jnp.float32)
        new_pair = (gate_val * linear / divisor).astype(jnp.bfloat16)
        grad_lin = (cot_blk * gate_val / divisor).astype(jnp.bfloat16)
        grad_pre = (cot_blk * linear / divisor * gate_val * (1.0 - gate_val)).astype(jnp.bfloat16)
        grad_out = grad_out + lax.dot_general(outer_prod, grad_lin, contract_first, preferred_element_type=jnp.float32)
        grad_gate = grad_gate + lax.dot_general(pair_blk, grad_pre, contract_first, preferred_element_type=jnp.float32)
        grad_outer = lax.dot_general(grad_lin, output_weight, contract_second, preferred_element_type=jnp.float32).astype(jnp.bfloat16)
        outer_turned = grad_outer.reshape(row_block, CROP_RESIDUES, PROJECT_WIDTH, PROJECT_WIDTH).transpose(0, 2, 1, 3).reshape(row_block * PROJECT_WIDTH, CROP_RESIDUES * PROJECT_WIDTH)
        left_part = lax.dot_general(outer_turned, right_flat, contract_second, preferred_element_type=jnp.float32)
        grad_right_acc = grad_right_acc + lax.dot_general(left_blk, outer_turned, contract_first, preferred_element_type=jnp.float32)
        return ((grad_out, grad_gate, grad_right_acc), (new_pair.reshape(row_block, CROP_RESIDUES, PAIR_CH), left_part))
    start_carry = (jnp.zeros((PROJECT_WIDTH * PROJECT_WIDTH, PAIR_CH), jnp.float32), jnp.zeros((PAIR_CH, PAIR_CH), jnp.float32), jnp.zeros((ALIGN_ROWS, CROP_RESIDUES * PROJECT_WIDTH), jnp.float32))
    final_carry, stacked = lax.scan(one_block, start_carry, jnp.arange(n_blocks, dtype=jnp.int32))
    grad_out, grad_gate, grad_right_acc = final_carry
    pair_blocks, left_blocks = stacked
    pair_update = pair_blocks.reshape(CROP_RESIDUES, CROP_RESIDUES, PAIR_CH)
    grad_left_act = left_blocks.reshape(CROP_RESIDUES, PROJECT_WIDTH, ALIGN_ROWS).transpose(2, 0, 1) * both_mask[:, :, None]
    grad_right_act = grad_right_acc.reshape(ALIGN_ROWS, CROP_RESIDUES, PROJECT_WIDTH) * both_mask[:, :, None]
    feats_wide = flattened_features.astype(jnp.float32)
    grad_left = jnp.dot(feats_wide.T, grad_left_act.reshape(ALIGN_ROWS * CROP_RESIDUES, PROJECT_WIDTH), precision=lax.Precision.HIGHEST)
    grad_right = jnp.dot(feats_wide.T, grad_right_act.reshape(ALIGN_ROWS * CROP_RESIDUES, PROJECT_WIDTH), precision=lax.Precision.HIGHEST)
    return (pair_update, grad_left, grad_right, grad_out, grad_gate)
```

```python
import jax
import jax.numpy as jnp
from jax import lax
from jax.experimental import pallas as pl
from jax.experimental.pallas import tpu as pltpu
from jax.sharding import PartitionSpec as P


def layer_normalize(alignment_state, norm_gain_vector):
    value_entries = alignment_state.astype(jnp.float32)
    average = jnp.mean(value_entries, axis=-1, keepdims=True)
    centred = value_entries - average
    variance = jnp.mean(centred * centred, axis=-1, keepdims=True)
    return (centred * lax.rsqrt(variance + 1e-05) * norm_gain_vector).astype(jnp.bfloat16)


def general_device(
    alignment_state,
    pair_state,
    cotangent,
    sequence_row_mask,
    residue_mask,
    norm_gain_vector,
    left_matrix_weight,
    right_matrix_weight,
    output_weight,
    output_bias,
    gate_matrix,
):
    sequence_resident, column_count, alignment_channel_count = alignment_state.shape
    count_of_rows = pair_state.shape[0]
    pair_chans = pair_state.shape[2]
    projection_width = left_matrix_weight.shape[1]
    every_sequence = sequence_row_mask.shape[0]
    row_at = lax.axis_index("row")
    col_at = lax.axis_index("col")
    number_of_rows = lax.axis_size("row")
    contract_first = (((0,), (0,)), ((), ()))
    contract_second = (((1,), (1,)), ((), ()))
    resident_features = layer_normalize(alignment_state, norm_gain_vector)
    seq_flags = sequence_row_mask.astype(jnp.float32)
    res_flags = residue_mask.astype(jnp.float32)
    my_cols = lax.dynamic_slice_in_dim(res_flags, col_at * column_count, column_count, 0)
    my_rows = lax.dynamic_slice_in_dim(res_flags, row_at * count_of_rows, count_of_rows, 0)
    panel_mask = seq_flags[:, None] * my_rows[None, :]
    column_mask = seq_flags[:, None] * my_cols[None, :]
    broadcast_features = lax.all_gather(
        resident_features.reshape(sequence_resident, column_count * alignment_channel_count),
        "col",
        axis=1,
        tiled=True,
    )
    row_portions = broadcast_features.reshape(
        sequence_resident, number_of_rows, count_of_rows * alignment_channel_count
    )
    row_feats = lax.all_to_all(
        row_portions, "row", split_axis=1, concat_axis=0, tiled=True
    ).reshape(every_sequence * count_of_rows, alignment_channel_count)
    left_panel = (
        jnp.dot(row_feats, left_matrix_weight, preferred_element_type=jnp.float32).reshape(
            every_sequence, count_of_rows, projection_width
        )
        * panel_mask[:, :, None]
    ).astype(jnp.bfloat16)
    left_matrix = left_panel.transpose(1, 2, 0).reshape(
        count_of_rows * projection_width, every_sequence
    )
    column_features = lax.all_gather(
        resident_features.reshape(sequence_resident, column_count * alignment_channel_count),
        "row",
        axis=0,
        tiled=True,
    ).reshape(every_sequence, column_count, alignment_channel_count)
    right_panel = (
        jnp.dot(
            column_features.reshape(every_sequence * column_count, alignment_channel_count),
            right_matrix_weight,
            preferred_element_type=jnp.float32,
        ).reshape(every_sequence, column_count, projection_width)
        * column_mask[:, :, None]
    ).astype(jnp.bfloat16)
    surplus_offset = jnp.zeros((alignment_channel_count, projection_width), jnp.float32)

    def absorb(extra, first_col, width_columns, right_part):
        feat_blk = (
            lax.dynamic_slice_in_dim(column_features, first_col, width_columns, 1)
            .reshape(every_sequence * width_columns, alignment_channel_count)
            .astype(jnp.float32)
        )
        mask_blk = lax.dynamic_slice_in_dim(column_mask, first_col, width_columns, 1)
        masked_part = (
            right_part.reshape(every_sequence, width_columns, projection_width)
            * mask_blk[:, :, None]
        ).reshape(every_sequence * width_columns, projection_width)
        return extra + jnp.dot(feat_blk.T, masked_part, precision=lax.Precision.HIGHEST)

    right_flat = right_panel.reshape(every_sequence, column_count * projection_width)
    row_total = jnp.sum(seq_flags)
    col_block = 128
    n_blocks = column_count // col_block

    def one_block(block_idx, carry):
        new_update, grad_out, grad_gate, left_acc, extra = carry
        first_col = block_idx * col_block
        right_blk = lax.dynamic_slice_in_dim(
            right_flat, first_col * projection_width, col_block * projection_width, 1
        )
        outer_prod = jnp.dot(left_matrix, right_blk, preferred_element_type=jnp.float32)
        outer_prod = outer_prod.reshape(
            count_of_rows, projection_width, col_block, projection_width
        ).transpose(0, 2, 1, 3)
        outer_prod = outer_prod.reshape(
            count_of_rows * col_block, projection_width * projection_width
        ).astype(jnp.bfloat16)
        linear = (
            jnp.dot(outer_prod, output_weight, preferred_element_type=jnp.float32) + output_bias
        )
        pair_blk = lax.dynamic_slice_in_dim(pair_state, first_col, col_block, 1).reshape(
            count_of_rows * col_block, pair_chans
        )
        gate_val = jax.nn.sigmoid(
            jnp.dot(pair_blk, gate_matrix, preferred_element_type=jnp.float32)
        )
        blk_flags = lax.dynamic_slice_in_dim(my_cols, first_col, col_block, 0)
        divisor = jnp.maximum(row_total * my_rows[:, None] * blk_flags[None, :], 1.0).reshape(
            count_of_rows * col_block, 1
        )
        cot_blk = (
            lax.dynamic_slice_in_dim(cotangent, first_col, col_block, 1)
            .reshape(count_of_rows * col_block, pair_chans)
            .astype(jnp.float32)
        )
        new_pair = (gate_val * linear / divisor).astype(jnp.bfloat16)
        new_update = lax.dynamic_update_slice_in_dim(
            new_update, new_pair.reshape(count_of_rows, col_block, pair_chans), first_col, 1
        )
        grad_lin = (cot_blk * gate_val / divisor).astype(jnp.bfloat16)
        grad_pre = (cot_blk * linear / divisor * gate_val * (1.0 - gate_val)).astype(jnp.bfloat16)
        grad_out = grad_out + lax.dot_general(
            outer_prod, grad_lin, contract_first, preferred_element_type=jnp.float32
        )
        grad_gate = grad_gate + lax.dot_general(
            pair_blk, grad_pre, contract_first, preferred_element_type=jnp.float32
        )
        grad_outer = lax.dot_general(
            grad_lin, output_weight, contract_second, preferred_element_type=jnp.float32
        ).astype(jnp.bfloat16)
        outer_turned = (
            grad_outer.reshape(count_of_rows, col_block, projection_width, projection_width)
            .transpose(0, 2, 1, 3)
            .reshape(count_of_rows * projection_width, col_block * projection_width)
        )
        left_acc = left_acc + lax.dot_general(
            outer_turned, right_blk, contract_second, preferred_element_type=jnp.float32
        )
        right_part = lax.dot_general(
            left_matrix, outer_turned, contract_first, preferred_element_type=jnp.float32
        )
        extra = absorb(extra, first_col, col_block, right_part)
        return (new_update, grad_out, grad_gate, left_acc, extra)

    start_carry = (
        jnp.zeros((count_of_rows, column_count, pair_chans), jnp.bfloat16),
        jnp.zeros((projection_width * projection_width, pair_chans), jnp.float32),
        jnp.zeros((pair_chans, pair_chans), jnp.float32),
        jnp.zeros((count_of_rows * projection_width, every_sequence), jnp.float32),
        surplus_offset,
    )
    new_update, grad_out, grad_gate, left_acc, extra = lax.fori_loop(
        0, n_blocks, one_block, start_carry
    )
    grad_left_act = (
        left_acc.reshape(count_of_rows, projection_width, every_sequence).transpose(2, 0, 1)
        * panel_mask[:, :, None]
    )
    grad_left = jnp.dot(
        row_feats.astype(jnp.float32).T,
        grad_left_act.reshape(every_sequence * count_of_rows, projection_width),
        precision=lax.Precision.HIGHEST,
    )
    summed_left, summed_right, summed_out, summed_gate = lax.psum(
        (grad_left, extra, grad_out, grad_gate), ("row", "col")
    )
    return (new_update, summed_left, summed_right, summed_out, summed_gate)


F32 = jnp.float32
BF16 = jnp.bfloat16
MESH = pl.DeviceIdType.MESH
NT = (((1,), (1,)), ((), ()))
TN = (((0,), (0,)), ((), ()))
NN = (((1,), (0,)), ((), ()))


def mm(a, b, dims=NN):
    return lax.dot_general(a, b, dims, preferred_element_type=F32)


def split2(x):
    high = x.astype(BF16)
    return high, (x - high.astype(F32)).astype(BF16)


def gather_start(buf, me, core, chip, chips, send, recv):
    copies = []
    for k in range(chips):
        if k == 0:
            target = chip * 2 + (1 - core)
        else:
            target = lax.rem(chip + k, chips) * 2 + core
        copy = pltpu.make_async_remote_copy(
            src_ref=buf.at[me],
            dst_ref=buf.at[me],
            send_sem=send.at[k],
            recv_sem=recv.at[k],
            device_id={"row": target},
            device_id_type=MESH,
        )
        copy.start()
        copies.append(copy)
    return copies


def gather_finish(copies, buf, core, chip, chips, send, recv):
    partner = chip * 2 + (1 - core)
    passed = []
    for k in range(1, chips):
        copies[k].wait_recv()
        slot = lax.rem(chip - k + chips, chips) * 2 + core
        copy = pltpu.make_async_remote_copy(
            src_ref=buf.at[slot],
            dst_ref=buf.at[slot],
            send_sem=send.at[chips + k],
            recv_sem=recv.at[chips + k],
            device_id={"row": partner},
            device_id_type=MESH,
        )
        copy.start()
        passed.append(copy)
    copies[0].wait_recv()
    for copy in passed:
        copy.wait_recv()
    return copies + passed


def fused_kernel(
    seq_ref, res_ref, *inputs_and_rest,
):
    hbm, rest = inputs_and_rest[:10], inputs_and_rest[10:]
    outs_and_scratch, vmem, load_sem = rest[:-11], rest[-11:-1], rest[-1]
    loads = [
        pltpu.make_async_copy(src, dst, load_sem.at[n])
        for n, (src, dst) in enumerate(zip(hbm, vmem))
    ]
    for n in (0, 2, 1, 3, 4, 5, 6, 7, 8, 9):
        loads[n].start()
    fused_body(loads, seq_ref, res_ref, *vmem, *outs_and_scratch)


def fused_body(
    loads, seq_ref, res_ref, align_ref, gain_ref, pair_ref, gm_ref, w_ref, resrow_ref, wl_ref,
    wr_ref, cot_ref, bias_ref,
    upd_ref, gt_s,
    feat, gate_s, w2_s, w32_s, rt_s, fr_s, m_s, g_s, pre_s, n2_s, gr2_s,
    pk_s, sa_s, ra_s, sb_s, rb_s,
    send_f, recv_f, send_a, recv_a, send_b, recv_b, send_g, recv_g,
):
    me = lax.axis_index("row")
    core = lax.rem(me, 2)
    chip = lax.div(me, 2)
    devices, residues, lanes = feat.shape
    chips = devices // 2
    s_loc, ch, _ = align_ref.shape
    rows, _, pc = pair_ref.shape
    width = wl_ref.shape[0]
    seqs = s_loc * devices
    partner = chip * 2 + (1 - core)

    barrier = pltpu.get_barrier_semaphore()
    for k in range(chips):
        target = partner if k == 0 else lax.rem(chip + k, chips) * 2 + core
        pl.semaphore_signal(barrier, inc=1, device_id={"row": target}, device_id_type=MESH)

    loads[0].wait()
    loads[1].wait()
    parts = []
    for s in range(s_loc):
        value = align_ref[s].astype(F32)
        centred = value - jnp.mean(value, axis=0, keepdims=True)
        variance = jnp.mean(centred * centred, axis=0, keepdims=True)
        parts.append(centred * lax.rsqrt(variance + 1e-05))
    gain = jnp.concatenate([gain_ref[...]] * s_loc, axis=1)
    feat[me] = (jnp.transpose(jnp.concatenate(parts, axis=0)) * gain).astype(BF16)
    pl.semaphore_wait(barrier, chips)
    copies = gather_start(feat, me, core, chip, chips, send_f, recv_f)

    for load in loads[2:]:
        load.wait()
    gm = gm_ref[...]
    for i in range(rows):
        gate_s[i] = jax.nn.sigmoid(mm(pair_ref[i], gm))
    w32_s[...] = w_ref[...].astype(F32)
    for e in range(width):
        w2_s[:, e * pc : (e + 1) * pc] = w32_s[pl.ds(e, width, stride=width), :].astype(BF16)
    resrow = resrow_ref[...].astype(F32)
    rescol = jnp.transpose(jnp.broadcast_to(resrow, (pc, residues)))
    seq = [seq_ref[s].astype(F32) for s in range(seqs)]
    mine = [res_ref[me * rows + i].astype(F32) for i in range(rows)]
    row_total = seq[0]
    for s in range(1, seqs):
        row_total = row_total + seq[s]
    lane = lax.broadcasted_iota(jnp.int32, (1, rows * seqs), 1)
    maskrow = jnp.zeros((1, rows * seqs), F32)
    for s in range(s_loc):
        for d in range(devices):
            maskrow = jnp.where(lax.rem(lane, seqs) == s * devices + d, seq[d * s_loc + s], maskrow)
    resl = jnp.zeros((1, rows * seqs), F32)
    for i in range(rows):
        resl = jnp.where(lax.div(lane, seqs) == i, mine[i], resl)
    maskrow = maskrow * resl
    wlt = wl_ref[...].astype(F32)
    wlt2 = jnp.concatenate([wlt] * s_loc, axis=1).astype(BF16)
    wrt = wr_ref[...].astype(F32)
    wrt2 = jnp.concatenate([wrt] * s_loc, axis=1)
    lane_s = lax.div(lax.broadcasted_iota(jnp.int32, (width, lanes), 1), ch)
    wr_bd = jnp.concatenate(
        [jnp.where(lane_s == s, wrt2, 0.0) for s in range(s_loc)], axis=0
    ).astype(BF16)

    done = gather_finish(copies, feat, core, chip, chips, send_f, recv_f)

    feats = feat[...].reshape(devices * residues, lanes)
    right = mm(wr_bd, feats, NT)
    for d in range(devices):
        for s in range(s_loc):
            rt_s[pl.ds(s * devices + d, width, stride=seqs), :] = right[
                s * width : (s + 1) * width, d * residues : (d + 1) * residues
            ] * (seq[d * s_loc + s] * resrow)
    rtt = rt_s[...].astype(BF16)
    rt = jnp.transpose(rt_s[...]).astype(BF16)

    for d in range(devices):
        block = feat[d, pl.ds(pl.multiple_of(chip * 2 * rows, 2 * rows), 2 * rows), :].astype(F32)
        fr_s[d * rows : (d + 1) * rows, :] = jnp.where(core == 0, block[:rows], block[rows:])
    lane_d = lax.div(lax.broadcasted_iota(jnp.int32, (devices, lanes), 1), ch)
    pieces = []
    for i in range(rows):
        block = fr_s[pl.ds(i, devices, stride=rows), :]
        for s in range(s_loc):
            pieces.append(jnp.where(lane_d == s, block, 0.0))
    fr = jnp.concatenate(pieces, axis=0).astype(BF16)
    left_t = mm(wlt2, fr, NT) * maskrow
    left = jnp.transpose(left_t).astype(BF16)
    left_t = left_t.astype(BF16)

    for e in range(0, width, 2):
        part = mm(left, w2_s[:, e * pc : (e + 2) * pc]).astype(BF16)
        for h in range(2):
            for i in range(rows):
                m_s[(e + h) * seqs : (e + h + 1) * seqs, i * pc : (i + 1) * pc] = part[
                    i * seqs : (i + 1) * seqs, h * pc : (h + 1) * pc
                ]

    bias = bias_ref[...]
    for i in range(0, rows, 2):
        lin2 = mm(rt, m_s[:, i * pc : (i + 2) * pc])
        for h in range(2):
            linear = lin2[:, h * pc : (h + 1) * pc] + bias
            gate = gate_s[i + h]
            inverse = 1.0 / jnp.maximum(row_total * mine[i + h] * rescol, 1.0)
            cot = cot_ref[i + h].astype(F32)
            scaled = gate * inverse
            upd_ref[i + h] = (scaled * linear).astype(BF16)
            glin = cot * scaled
            g_s[:, (i + h) * pc : (i + h + 1) * pc] = glin.astype(BF16)
            pre_s[(i + h) * residues : (i + h + 1) * residues, :] = (
                glin * linear * (1.0 - gate)
            ).astype(BF16)

    step = 8
    for e in range(0, width, step):
        part = mm(rtt[e * seqs : (e + step) * seqs], g_s[...]).astype(BF16)
        for h in range(step):
            for i in range(rows):
                n2_s[i * seqs : (i + 1) * seqs, (e + h) * pc : (e + h + 1) * pc] = part[
                    h * seqs : (h + 1) * seqs, i * pc : (i + 1) * pc
                ]
    go = mm(left_t, n2_s[...])
    per = width // devices
    g_rows = pc // devices
    top = per * width
    for k in range(devices):
        for h in range(per):
            e = k * per + h
            pk_s[k % 2, k // 2, h * width : (h + 1) * width, :] = go[:, e * pc : (e + 1) * pc]

    def pair(part, first, size):
        window = pl.ds(first, size)
        sa_s[:, window, :] = pk_s[1 - core, :, window, :].astype(BF16)
        copy = pltpu.make_async_remote_copy(
            src_ref=sa_s.at[:, window], dst_ref=ra_s.at[:, window],
            send_sem=send_a.at[part], recv_sem=recv_a.at[part],
            device_id={"row": partner}, device_id_type=MESH,
        )
        copy.start()
        return copy

    def scatter_part(part, first, size):
        window = pl.ds(first, size)
        sb_s[:, window, :] = (
            pk_s[core, :, window, :] + ra_s[:, window, :].astype(F32)
        ).astype(BF16)
        copies = []
        for k in range(1, chips):
            to = lax.rem(chip + k, chips)
            at = part * (chips - 1) + k - 1
            copy = pltpu.make_async_remote_copy(
                src_ref=sb_s.at[to, window], dst_ref=rb_s.at[k - 1, window],
                send_sem=send_b.at[at], recv_sem=recv_b.at[at],
                device_id={"row": to * 2 + core}, device_id_type=MESH,
            )
            copy.start()
            copies.append(copy)
        return copies

    first = pair(0, 0, top)
    act = mm(w2_s[...], n2_s[...], NT) * maskrow
    act_hi, act_lo = split2(act)
    gl2 = mm(act_hi, fr) + mm(act_lo, fr)
    gl = gl2[:, :ch]
    for s in range(1, s_loc):
        gl = gl + gl2[:, s * ch : (s + 1) * ch]

    rt_s[...] = mm(m_s[...], g_s[...], NT)
    first.wait_recv()
    scatter = scatter_part(0, 0, top)
    for d in range(devices):
        for s in range(s_loc):
            gr2_s[s * width : (s + 1) * width, d * residues : (d + 1) * residues] = rt_s[
                pl.ds(s * devices + d, width, stride=seqs), :
            ] * (seq[d * s_loc + s] * resrow)
    gr_hi, gr_lo = split2(gr2_s[...])
    gr2 = mm(gr_hi, feats) + mm(gr_lo, feats)
    gr = gr2[:width, :ch]
    for s in range(1, s_loc):
        gr = gr + gr2[s * width : (s + 1) * width, s * ch : (s + 1) * ch]
    gg = mm(pair_ref[...].reshape(rows * residues, pc), pre_s[...], TN)

    both = jnp.concatenate([gl, gr], axis=1)
    for k in range(devices):
        rest = pk_s.at[k % 2, k // 2]
        rest[top : top + g_rows, :] = gg[k * g_rows : (k + 1) * g_rows]
        if k < width // 8:
            tail = both[k * 8 : (k + 1) * 8]
        else:
            tail = jnp.zeros((8, 2 * ch), F32)
        rest[top + g_rows : top + g_rows + 8, :] = tail

    second = pair(1, top, g_rows + 8)
    second.wait_recv()
    small = scatter_part(1, top, g_rows + 8)
    total = pk_s[core, chip] + ra_s[chip].astype(F32)
    for k in range(1, chips):
        scatter[k - 1].wait_recv()
        small[k - 1].wait_recv()
        total = total + rb_s[k - 1].astype(F32)
    gt_s[me] = total.astype(BF16)
    copies = gather_start(gt_s, me, core, chip, chips, send_g, recv_g)
    done2 = gather_finish(copies, gt_s, core, chip, chips, send_g, recv_g)

    for copy in done + [first, second] + scatter + small + done2:
        copy.wait_send()


def unpack_kernel(mid_ref, sum_ref, upd_ref, gl_ref, gr_ref, go_ref, gg_ref, sem):
    devices = sum_ref.shape[0]
    width, ch = gl_ref.shape
    per = width // devices
    pc = gg_ref.shape[0]
    g_rows = pc // devices
    top = per * width
    copy = pltpu.make_async_copy(mid_ref, upd_ref, sem)
    copy.start()
    for k in range(devices):
        block = sum_ref[k].astype(F32)
        for h in range(per):
            go_ref[pl.ds(k * per + h, width, stride=width), :] = block[h * width : (h + 1) * width]
        gg_ref[k * g_rows : (k + 1) * g_rows, :] = block[top : top + g_rows]
        if k < width // 8:
            tail = block[top + g_rows : top + g_rows + 8]
            gl_ref[k * 8 : (k + 1) * 8, :] = tail[:, :ch]
            gr_ref[k * 8 : (k + 1) * 8, :] = tail[:, ch:]
    copy.wait()


def fused_device(
    alignment_state, pair_state, cotangent, sequence_row_mask, residue_mask, norm_gain_vector,
    left_matrix_weight, right_matrix_weight, output_weight, output_bias, gate_matrix,
):
    s_loc, residues, ch = alignment_state.shape
    rows, _, pc = pair_state.shape
    width = left_matrix_weight.shape[1]
    devices = lax.axis_size("row")
    seqs = s_loc * devices
    chips = devices // 2
    lanes = s_loc * ch
    chunk = (width // devices) * width + pc // devices + 8
    smem = pl.BlockSpec(memory_space=pltpu.SMEM)
    vmem = pl.BlockSpec(memory_space=pltpu.VMEM)
    dma = pltpu.SemaphoreType.DMA
    inputs = (
        alignment_state.transpose(0, 2, 1),
        norm_gain_vector.reshape(1, ch),
        pair_state,
        gate_matrix,
        output_weight,
        residue_mask.reshape(1, residues),
        left_matrix_weight.T,
        right_matrix_weight.T,
        cotangent,
        output_bias.reshape(1, pc),
    )
    middle, sums = pl.pallas_call(
        fused_kernel,
        name="fused",
        out_shape=(
            pltpu.VMEM((rows, residues, pc), BF16),
            pltpu.VMEM((devices, chunk, pc), BF16),
        ),
        in_specs=[smem, smem] + [pl.BlockSpec(memory_space=pltpu.HBM)] * 10,
        out_specs=(vmem,) * 2,
        scratch_shapes=[
            pltpu.VMEM((devices, residues, lanes), BF16),
            pltpu.VMEM((rows, residues, pc), F32),
            pltpu.VMEM((width, width * pc), BF16),
            pltpu.VMEM((width * width, pc), F32),
            pltpu.VMEM((width * seqs, residues), F32),
            pltpu.VMEM((devices * rows, lanes), F32),
            pltpu.VMEM((width * seqs, rows * pc), BF16),
            pltpu.VMEM((residues, rows * pc), BF16),
            pltpu.VMEM((rows * residues, pc), BF16),
            pltpu.VMEM((rows * seqs, width * pc), BF16),
            pltpu.VMEM((s_loc * width, devices * residues), F32),
            pltpu.VMEM((2, chips, chunk, pc), F32),
            pltpu.VMEM((chips, chunk, pc), BF16),
            pltpu.VMEM((chips, chunk, pc), BF16),
            pltpu.VMEM((chips, chunk, pc), BF16),
            pltpu.VMEM((chips - 1, chunk, pc), BF16),
            dma((2 * chips,)),
            dma((2 * chips,)),
            dma((2,)),
            dma((2,)),
            dma((2 * (chips - 1),)),
            dma((2 * (chips - 1),)),
            dma((2 * chips,)),
            dma((2 * chips,)),
        ]
        + [pltpu.VMEM(value.shape, value.dtype) for value in inputs]
        + [dma((len(inputs),))],
        compiler_params=pltpu.CompilerParams(
            collective_id=0, has_side_effects=True, vmem_limit_bytes=61 * 1024 * 1024
        ),
    )(sequence_row_mask, residue_mask, *inputs)
    update, left_t, right_t, grad_out, grad_gate = pl.pallas_call(
        unpack_kernel,
        name="unpack",
        out_shape=(
            jax.ShapeDtypeStruct((rows, residues, pc), BF16),
            jax.ShapeDtypeStruct((width, ch), F32),
            jax.ShapeDtypeStruct((width, ch), F32),
            jax.ShapeDtypeStruct((width * width, pc), F32),
            jax.ShapeDtypeStruct((pc, pc), F32),
        ),
        in_specs=[vmem] * 2,
        out_specs=(pl.BlockSpec(memory_space=pltpu.HBM),) + (vmem,) * 4,
        scratch_shapes=[dma],
        compiler_params=pltpu.CompilerParams(vmem_limit_bytes=32 * 1024 * 1024),
    )(middle, sums)
    return update, left_t.T, right_t.T, grad_out, grad_gate


def per_device(*arrays):
    alignment_state, pair_state = arrays[0], arrays[1]
    s_loc, residues, ch = alignment_state.shape
    rows, _, pc = pair_state.shape
    width = arrays[6].shape[1]
    devices = lax.axis_size("row")
    fits = (
        lax.axis_size("col") == 1
        and devices % 2 == 0
        and (s_loc * ch, pc, residues) == (128, 128, 128)
        and rows == 8
        and width % devices == 0
        and pc == devices * 8
        and s_loc * devices == 32
    )
    return fused_device(*arrays) if fits else general_device(*arrays)


def solution(mesh):
    return jax.shard_map(
        per_device,
        mesh=mesh,
        in_specs=(
            P(("grp", "row"), "col", None),
            P(("grp", "row"), "col", None),
            P(("grp", "row"), "col", None),
            P("grp"),
            P("grp"),
            P(),
            P(),
            P(),
            P(),
            P(),
            P(),
        ),
        out_specs=(
            P(("grp", "row"), "col", None),
            P("grp", None),
            P("grp", None),
            P("grp", None),
            P("grp", None),
        ),
        check_vma=False,
    )
```

```python
import jax
import jax.numpy as jnp
from jax import lax
from jax.experimental import pallas as pl
from jax.experimental.pallas import tpu as pltpu
from jax.sharding import PartitionSpec as P


def layer_normalize(alignment_state, norm_gain_vector):
    value_entries = alignment_state.astype(jnp.float32)
    average = jnp.mean(value_entries, axis=-1, keepdims=True)
    centred = value_entries - average
    variance = jnp.mean(centred * centred, axis=-1, keepdims=True)
    return (centred * lax.rsqrt(variance + 1e-05) * norm_gain_vector).astype(jnp.bfloat16)


def general_device(
    alignment_state,
    pair_state,
    cotangent,
    sequence_row_mask,
    residue_mask,
    norm_gain_vector,
    left_matrix_weight,
    right_matrix_weight,
    output_weight,
    output_bias,
    gate_matrix,
):
    sequence_resident, column_count, alignment_channel_count = alignment_state.shape
    count_of_rows = pair_state.shape[0]
    pair_chans = pair_state.shape[2]
    projection_width = left_matrix_weight.shape[1]
    every_sequence = sequence_row_mask.shape[0]
    row_at = lax.axis_index("row")
    col_at = lax.axis_index("col")
    number_of_rows = lax.axis_size("row")
    contract_first = (((0,), (0,)), ((), ()))
    contract_second = (((1,), (1,)), ((), ()))
    resident_features = layer_normalize(alignment_state, norm_gain_vector)
    seq_flags = sequence_row_mask.astype(jnp.float32)
    res_flags = residue_mask.astype(jnp.float32)
    my_cols = lax.dynamic_slice_in_dim(res_flags, col_at * column_count, column_count, 0)
    my_rows = lax.dynamic_slice_in_dim(res_flags, row_at * count_of_rows, count_of_rows, 0)
    panel_mask = seq_flags[:, None] * my_rows[None, :]
    column_mask = seq_flags[:, None] * my_cols[None, :]
    broadcast_features = lax.all_gather(
        resident_features.reshape(sequence_resident, column_count * alignment_channel_count),
        "col",
        axis=1,
        tiled=True,
    )
    row_portions = broadcast_features.reshape(
        sequence_resident, number_of_rows, count_of_rows * alignment_channel_count
    )
    row_feats = lax.all_to_all(
        row_portions, "row", split_axis=1, concat_axis=0, tiled=True
    ).reshape(every_sequence * count_of_rows, alignment_channel_count)
    left_panel = (
        jnp.dot(row_feats, left_matrix_weight, preferred_element_type=jnp.float32).reshape(
            every_sequence, count_of_rows, projection_width
        )
        * panel_mask[:, :, None]
    ).astype(jnp.bfloat16)
    left_matrix = left_panel.transpose(1, 2, 0).reshape(
        count_of_rows * projection_width, every_sequence
    )
    column_features = lax.all_gather(
        resident_features.reshape(sequence_resident, column_count * alignment_channel_count),
        "row",
        axis=0,
        tiled=True,
    ).reshape(every_sequence, column_count, alignment_channel_count)
    right_panel = (
        jnp.dot(
            column_features.reshape(every_sequence * column_count, alignment_channel_count),
            right_matrix_weight,
            preferred_element_type=jnp.float32,
        ).reshape(every_sequence, column_count, projection_width)
        * column_mask[:, :, None]
    ).astype(jnp.bfloat16)
    surplus_offset = jnp.zeros((alignment_channel_count, projection_width), jnp.float32)

    def absorb(extra, first_col, width_columns, right_part):
        feat_blk = (
            lax.dynamic_slice_in_dim(column_features, first_col, width_columns, 1)
            .reshape(every_sequence * width_columns, alignment_channel_count)
            .astype(jnp.float32)
        )
        mask_blk = lax.dynamic_slice_in_dim(column_mask, first_col, width_columns, 1)
        masked_part = (
            right_part.reshape(every_sequence, width_columns, projection_width)
            * mask_blk[:, :, None]
        ).reshape(every_sequence * width_columns, projection_width)
        return extra + jnp.dot(feat_blk.T, masked_part, precision=lax.Precision.HIGHEST)

    right_flat = right_panel.reshape(every_sequence, column_count * projection_width)
    row_total = jnp.sum(seq_flags)
    col_block = 128
    n_blocks = column_count // col_block

    def one_block(block_idx, carry):
        new_update, grad_out, grad_gate, left_acc, extra = carry
        first_col = block_idx * col_block
        right_blk = lax.dynamic_slice_in_dim(
            right_flat, first_col * projection_width, col_block * projection_width, 1
        )
        outer_prod = jnp.dot(left_matrix, right_blk, preferred_element_type=jnp.float32)
        outer_prod = outer_prod.reshape(
            count_of_rows, projection_width, col_block, projection_width
        ).transpose(0, 2, 1, 3)
        outer_prod = outer_prod.reshape(
            count_of_rows * col_block, projection_width * projection_width
        ).astype(jnp.bfloat16)
        linear = (
            jnp.dot(outer_prod, output_weight, preferred_element_type=jnp.float32) + output_bias
        )
        pair_blk = lax.dynamic_slice_in_dim(pair_state, first_col, col_block, 1).reshape(
            count_of_rows * col_block, pair_chans
        )
        gate_val = jax.nn.sigmoid(
            jnp.dot(pair_blk, gate_matrix, preferred_element_type=jnp.float32)
        )
        blk_flags = lax.dynamic_slice_in_dim(my_cols, first_col, col_block, 0)
        divisor = jnp.maximum(row_total * my_rows[:, None] * blk_flags[None, :], 1.0).reshape(
            count_of_rows * col_block, 1
        )
        cot_blk = (
            lax.dynamic_slice_in_dim(cotangent, first_col, col_block, 1)
            .reshape(count_of_rows * col_block, pair_chans)
            .astype(jnp.float32)
        )
        new_pair = (gate_val * linear / divisor).astype(jnp.bfloat16)
        new_update = lax.dynamic_update_slice_in_dim(
            new_update, new_pair.reshape(count_of_rows, col_block, pair_chans), first_col, 1
        )
        grad_lin = (cot_blk * gate_val / divisor).astype(jnp.bfloat16)
        grad_pre = (cot_blk * linear / divisor * gate_val * (1.0 - gate_val)).astype(jnp.bfloat16)
        grad_out = grad_out + lax.dot_general(
            outer_prod, grad_lin, contract_first, preferred_element_type=jnp.float32
        )
        grad_gate = grad_gate + lax.dot_general(
            pair_blk, grad_pre, contract_first, preferred_element_type=jnp.float32
        )
        grad_outer = lax.dot_general(
            grad_lin, output_weight, contract_second, preferred_element_type=jnp.float32
        ).astype(jnp.bfloat16)
        outer_turned = (
            grad_outer.reshape(count_of_rows, col_block, projection_width, projection_width)
            .transpose(0, 2, 1, 3)
            .reshape(count_of_rows * projection_width, col_block * projection_width)
        )
        left_acc = left_acc + lax.dot_general(
            outer_turned, right_blk, contract_second, preferred_element_type=jnp.float32
        )
        right_part = lax.dot_general(
            left_matrix, outer_turned, contract_first, preferred_element_type=jnp.float32
        )
        extra = absorb(extra, first_col, col_block, right_part)
        return (new_update, grad_out, grad_gate, left_acc, extra)

    start_carry = (
        jnp.zeros((count_of_rows, column_count, pair_chans), jnp.bfloat16),
        jnp.zeros((projection_width * projection_width, pair_chans), jnp.float32),
        jnp.zeros((pair_chans, pair_chans), jnp.float32),
        jnp.zeros((count_of_rows * projection_width, every_sequence), jnp.float32),
        surplus_offset,
    )
    new_update, grad_out, grad_gate, left_acc, extra = lax.fori_loop(
        0, n_blocks, one_block, start_carry
    )
    grad_left_act = (
        left_acc.reshape(count_of_rows, projection_width, every_sequence).transpose(2, 0, 1)
        * panel_mask[:, :, None]
    )
    grad_left = jnp.dot(
        row_feats.astype(jnp.float32).T,
        grad_left_act.reshape(every_sequence * count_of_rows, projection_width),
        precision=lax.Precision.HIGHEST,
    )
    summed_left, summed_right, summed_out, summed_gate = lax.psum(
        (grad_left, extra, grad_out, grad_gate), ("row", "col")
    )
    return (new_update, summed_left, summed_right, summed_out, summed_gate)


F32 = jnp.float32
BF16 = jnp.bfloat16
MESH = pl.DeviceIdType.MESH
NT = (((1,), (1,)), ((), ()))
TN = (((0,), (0,)), ((), ()))
NN = (((1,), (0,)), ((), ()))


def mm(a, b, dims=NN):
    return lax.dot_general(a, b, dims, preferred_element_type=F32)


def split2(x):
    high = x.astype(BF16)
    return high, (x - high.astype(F32)).astype(BF16)


def send(src, dst, send_sem, recv_sem, target):
    copy = pltpu.make_async_remote_copy(
        src_ref=src, dst_ref=dst, send_sem=send_sem, recv_sem=recv_sem,
        device_id={"row": target}, device_id_type=MESH,
    )
    copy.start()
    return copy


def gather_start(buf, me, core, chip, chips, send_sem, recv_sem):
    block = buf.at[me]
    copies = [send(block, block, send_sem.at[0], recv_sem.at[0], chip * 2 + 1 - core)]
    for k in range(1, chips):
        target = lax.rem(chip + k, chips) * 2 + 1 - core
        copies.append(send(block, block, send_sem.at[k], recv_sem.at[k], target))
    return copies


def gather_finish(copies, buf, core, chip, chips, send_sem, recv_sem):
    partner = chip * 2 + 1 - core
    passed = []
    for k in range(1, chips):
        copies[k].wait_recv()
        block = buf.at[lax.rem(chip - k + chips, chips) * 2 + 1 - core]
        at = chips + k
        passed.append(send(block, block, send_sem.at[at], recv_sem.at[at], partner))
    copies[0].wait_recv()
    for copy in passed:
        copy.wait_recv()
    return copies + passed


def fused_kernel(
    seq_ref, res_ref, *inputs_and_rest,
):
    hbm, rest = inputs_and_rest[:10], inputs_and_rest[10:]
    outs_and_scratch, vmem, load_sem = rest[:-11], rest[-11:-1], rest[-1]
    loads = [
        pltpu.make_async_copy(src, dst, load_sem.at[n])
        for n, (src, dst) in enumerate(zip(hbm, vmem))
    ]
    for n in (0, 1, 2, 3, 8, 4, 5, 6, 7, 9):
        loads[n].start()
    fused_body(loads, seq_ref, res_ref, *vmem, *outs_and_scratch)


def fused_body(
    loads, seq_ref, res_ref, align_ref, gain_ref, pair_ref, gm_ref, w_ref, resrow_ref, wl_ref,
    wr_ref, cot_ref, bias_ref,
    upd_ref, gt_s, gs_s,
    feat, gate_s, w2_s, w32_s, wr32_s, rt_s, fr_s, lt_s, m_s, g_s, pre_s, n2_s, gr2_s,
    sb_s, rb_s, sm_s, rm_s,
    send_f, recv_f, send_x, recv_x, send_b, recv_b, send_m, recv_m, send_g, recv_g, send_h, recv_h,
):
    me = lax.axis_index("row")
    core = lax.rem(me, 2)
    chip = lax.div(me, 2)
    half = 1 - core
    devices, residues, lanes = feat.shape
    chips = devices // 2
    s_loc, ch, _ = align_ref.shape
    rows, _, pc = pair_ref.shape
    width = wl_ref.shape[0]
    seqs = s_loc * devices
    partner = chip * 2 + 1 - core
    wide = width // 2
    mine_wide = rows * seqs

    barrier = pltpu.get_barrier_semaphore()
    for k in range(1, devices):
        pl.semaphore_signal(
            barrier, inc=1, device_id={"row": lax.rem(me + k, devices)}, device_id_type=MESH
        )

    loads[0].wait()
    loads[1].wait()
    parts = []
    for s in range(s_loc):
        value = align_ref[s].astype(F32)
        centred = value - jnp.mean(value, axis=0, keepdims=True)
        variance = jnp.mean(centred * centred, axis=0, keepdims=True)
        parts.append(centred * lax.rsqrt(variance + 1e-05))
    gain = jnp.concatenate([gain_ref[...]] * s_loc, axis=1)
    feat[me] = (jnp.transpose(jnp.concatenate(parts, axis=0)) * gain).astype(BF16)
    pl.semaphore_wait(barrier, devices - 1)
    copies = gather_start(feat, me, core, chip, chips, send_f, recv_f)

    for load in loads[2:]:
        load.wait()
    gm = gm_ref[...]
    resrow = resrow_ref[...].astype(F32)
    rescol = jnp.transpose(jnp.broadcast_to(resrow, (pc, residues)))
    seq = [seq_ref[s].astype(F32) for s in range(seqs)]
    both_rows = [res_ref[chip * 2 * rows + i].astype(F32) for i in range(2 * rows)]
    mine = [res_ref[me * rows + i].astype(F32) for i in range(rows)]
    row_total = seq[0]
    for s in range(1, seqs):
        row_total = row_total + seq[s]
    present = 1.0 / jnp.maximum(row_total * rescol, 1.0)
    inverse = [present * mine[i] + (1.0 - mine[i]) for i in range(rows)]
    for i in range(rows):
        gate = jax.nn.sigmoid(mm(pair_ref[i], gm))
        gate_s[i] = gate
        g_s[core, :, i * pc : (i + 1) * pc] = (
            cot_ref[i].astype(F32) * (gate * inverse[i])
        ).astype(BF16)
    crossing = send(g_s.at[core], g_s.at[core], send_x, recv_x, partner)

    w32_s[...] = w_ref[...].astype(F32)
    for h in range(2):
        for t in range(2):
            for k in range(chips):
                e, q = 4 * k + 2 * h + t, t * chips + k
                w2_s[h, :, q * pc : (q + 1) * pc] = w32_s[
                    pl.ds(e, width, stride=width), :
                ].astype(BF16)
    lane = lax.broadcasted_iota(jnp.int32, (1, 2 * mine_wide), 1)
    maskrow = jnp.zeros((1, 2 * mine_wide), F32)
    for s in range(s_loc):
        for d in range(devices):
            maskrow = jnp.where(lax.rem(lane, seqs) == s * devices + d, seq[d * s_loc + s], maskrow)
    resl = jnp.zeros((1, 2 * mine_wide), F32)
    for i in range(2 * rows):
        resl = jnp.where(lax.div(lane, seqs) == i, both_rows[i], resl)
    maskrow = maskrow * resl
    wlt = wl_ref[...].astype(F32)
    wlt2 = jnp.concatenate([wlt] * s_loc, axis=1).astype(BF16)
    wr32_s[...] = jnp.concatenate([wr_ref[...].astype(F32)] * s_loc, axis=1)
    wrt2 = jnp.concatenate(
        [wr32_s[pl.ds(n, chips, stride=4), :] for n in range(4)], axis=0
    )
    lane_s = lax.div(lax.broadcasted_iota(jnp.int32, (width, lanes), 1), ch)
    wr_bd = jnp.concatenate(
        [jnp.where(lane_s == s, wrt2, 0.0) for s in range(s_loc)], axis=0
    ).astype(BF16)

    done = gather_finish(copies, feat, core, chip, chips, send_f, recv_f)

    feats = feat[...].reshape(devices * residues, lanes)
    right = mm(wr_bd, feats, NT)
    for d in range(devices):
        for s in range(s_loc):
            rt_s[pl.ds(s * devices + d, width, stride=seqs), :] = right[
                s * width : (s + 1) * width, d * residues : (d + 1) * residues
            ] * (seq[d * s_loc + s] * resrow)
    own_half = pl.ds(pl.multiple_of(half * (wide * seqs), wide * seqs), wide * seqs)
    rtt = rt_s[own_half, :].astype(BF16)

    for d in range(devices):
        fr_s[d * 2 * rows : (d + 1) * 2 * rows, :] = feat[
            d, pl.ds(pl.multiple_of(chip * 2 * rows, 2 * rows), 2 * rows), :
        ].astype(F32)
    lane_d = lax.div(lax.broadcasted_iota(jnp.int32, (devices, lanes), 1), ch)
    pieces = []
    for i in range(2 * rows):
        block = fr_s[pl.ds(i, devices, stride=2 * rows), :]
        for s in range(s_loc):
            pieces.append(jnp.where(lane_d == s, block, 0.0))
    fr = jnp.concatenate(pieces, axis=0).astype(BF16)
    left_t = mm(wlt2, fr, NT) * maskrow
    for c in range(2):
        lt_s[c] = left_t[:, c * mine_wide : (c + 1) * mine_wide]
    left_t = left_t.astype(BF16)

    crossing.wait_recv()
    step = 4
    for e in range(0, wide, step):
        for c in range(2):
            part = mm(rtt[e * seqs : (e + step) * seqs], g_s[c]).astype(BF16)
            for h in range(step):
                for i in range(rows):
                    at = (c * rows + i) * seqs
                    n2_s[at : at + seqs, (e + h) * pc : (e + h + 1) * pc] = part[
                        h * seqs : (h + 1) * seqs, i * pc : (i + 1) * pc
                    ]
    go = mm(left_t, n2_s[...])
    for k in range(chips):
        for t in range(2):
            q = t * chips + k
            sb_s[k, t * width : (t + 1) * width, :] = go[:, q * pc : (q + 1) * pc].astype(BF16)
    scatter = []
    for k in range(chips):
        to = lax.rem(chip + k, chips)
        scatter.append(
            send(sb_s.at[to], rb_s.at[k], send_b.at[k], recv_b.at[k], to * 2 + 1 - core)
        )

    left = jnp.transpose(lt_s[core]).astype(BF16)
    for h in range(2):
        for e in range(0, wide, 2):
            part = mm(left, w2_s[h, :, e * pc : (e + 2) * pc]).astype(BF16)
            for n in range(2):
                at = (h * wide + e + n) * seqs
                for i in range(rows):
                    m_s[at : at + seqs, i * pc : (i + 1) * pc] = part[
                        i * seqs : (i + 1) * seqs, n * pc : (n + 1) * pc
                    ]
    rt = jnp.transpose(rt_s[...]).astype(BF16)

    bias = bias_ref[...]
    for i in range(0, rows, 2):
        lin2 = mm(rt, m_s[:, i * pc : (i + 2) * pc])
        for h in range(2):
            linear = lin2[:, h * pc : (h + 1) * pc] + bias
            gate = gate_s[i + h]
            scaled = gate * inverse[i + h]
            upd_ref[i + h] = (scaled * linear).astype(BF16)
            pre_s[(i + h) * residues : (i + h + 1) * residues, :] = (
                cot_ref[i + h].astype(F32) * scaled * linear * (1.0 - gate)
            ).astype(BF16)
    gg = mm(pair_ref[...].reshape(rows * residues, pc), pre_s[...], TN)

    act = mm(w2_s[half], n2_s[...], NT) * maskrow
    act_hi, act_lo = split2(act)
    gl2 = mm(act_hi, fr) + mm(act_lo, fr)
    gl = gl2[:, :ch]
    for s in range(1, s_loc):
        gl = gl + gl2[:, s * ch : (s + 1) * ch]

    rt_s[...] = mm(m_s[...], g_s[core], NT)
    for d in range(devices):
        for s in range(s_loc):
            gr2_s[s * width : (s + 1) * width, d * residues : (d + 1) * residues] = rt_s[
                pl.ds(s * devices + d, width, stride=seqs), :
            ] * (seq[d * s_loc + s] * resrow)
    gr_hi, gr_lo = split2(gr2_s[...])
    gr2 = mm(gr_hi, feats) + mm(gr_lo, feats)
    gr = gr2[:width, :ch]
    for s in range(1, s_loc):
        gr = gr + gr2[s * width : (s + 1) * width, s * ch : (s + 1) * ch]

    both = jnp.concatenate([gl, gr], axis=1)
    g_rows = pc // devices
    for k in range(devices):
        tail = both[k * 8 : (k + 1) * 8] if k < width // 8 else jnp.zeros((8, 2 * ch), F32)
        sm_s[k] = jnp.concatenate([gg[k * g_rows : (k + 1) * g_rows], tail], axis=0).astype(BF16)
    small = []
    for k in range(1, devices):
        to = lax.rem(me + k, devices)
        small.append(send(sm_s.at[to], rm_s.at[k - 1], send_m.at[k - 1], recv_m.at[k - 1], to))

    scatter[0].wait_recv()
    total = rb_s[0].astype(F32)
    for k in range(1, chips):
        scatter[k].wait_recv()
        total = total + rb_s[k].astype(F32)
    gt_s[me] = total.astype(BF16)
    copies = gather_start(gt_s, me, core, chip, chips, send_g, recv_g)

    total = sm_s[me].astype(F32)
    for k in range(1, devices):
        small[k - 1].wait_recv()
        total = total + rm_s[k - 1].astype(F32)
    gs_s[me] = total.astype(BF16)
    spread = []
    for k in range(1, devices):
        block = gs_s.at[me]
        spread.append(
            send(block, block, send_h.at[k - 1], recv_h.at[k - 1], lax.rem(me + k, devices))
        )
    done2 = gather_finish(copies, gt_s, core, chip, chips, send_g, recv_g)
    for copy in spread:
        copy.wait_recv()
    for copy in done + [crossing] + scatter + small + done2 + spread:
        copy.wait_send()


def unpack_kernel(mid_ref, sum_ref, rest_ref, upd_ref, gl_ref, gr_ref, go_ref, gg_ref, sem):
    devices = sum_ref.shape[0]
    width, ch = gl_ref.shape
    per = width // devices
    pc = gg_ref.shape[0]
    g_rows = pc // devices
    copy = pltpu.make_async_copy(mid_ref, upd_ref, sem)
    copy.start()
    for k in range(devices):
        for h in range(per):
            go_ref[pl.ds(k * per + h, width, stride=width), :] = sum_ref[
                k, h * width : (h + 1) * width, :
            ].astype(F32)
        block = rest_ref[k].astype(F32)
        gg_ref[k * g_rows : (k + 1) * g_rows, :] = block[:g_rows]
        if k < width // 8:
            gl_ref[k * 8 : (k + 1) * 8, :] = block[g_rows:, :ch]
            gr_ref[pl.ds(k, 8, stride=4), :] = block[g_rows:, ch:]
    copy.wait()


def fused_device(
    alignment_state, pair_state, cotangent, sequence_row_mask, residue_mask, norm_gain_vector,
    left_matrix_weight, right_matrix_weight, output_weight, output_bias, gate_matrix,
):
    s_loc, residues, ch = alignment_state.shape
    rows, _, pc = pair_state.shape
    width = left_matrix_weight.shape[1]
    devices = lax.axis_size("row")
    seqs = s_loc * devices
    chips = devices // 2
    lanes = s_loc * ch
    top = (width // devices) * width
    small = pc // devices + 8
    smem = pl.BlockSpec(memory_space=pltpu.SMEM)
    vmem = pl.BlockSpec(memory_space=pltpu.VMEM)
    dma = pltpu.SemaphoreType.DMA
    inputs = (
        alignment_state.transpose(0, 2, 1),
        norm_gain_vector.reshape(1, ch),
        pair_state,
        gate_matrix,
        output_weight,
        residue_mask.reshape(1, residues),
        left_matrix_weight.T,
        right_matrix_weight.T,
        cotangent,
        output_bias.reshape(1, pc),
    )
    middle, sums, rest = pl.pallas_call(
        fused_kernel,
        name="fused",
        out_shape=(
            pltpu.VMEM((rows, residues, pc), BF16),
            pltpu.VMEM((devices, top, pc), BF16),
            pltpu.VMEM((devices, small, pc), BF16),
        ),
        in_specs=[smem, smem] + [pl.BlockSpec(memory_space=pltpu.HBM)] * 10,
        out_specs=(vmem,) * 3,
        scratch_shapes=[
            pltpu.VMEM((devices, residues, lanes), BF16),
            pltpu.VMEM((rows, residues, pc), F32),
            pltpu.VMEM((2, width, width // 2 * pc), BF16),
            pltpu.VMEM((width * width, pc), F32),
            pltpu.VMEM((width, lanes), F32),
            pltpu.VMEM((width * seqs, residues), F32),
            pltpu.VMEM((devices * 2 * rows, lanes), F32),
            pltpu.VMEM((2, width, rows * seqs), F32),
            pltpu.VMEM((width * seqs, rows * pc), BF16),
            pltpu.VMEM((2, residues, rows * pc), BF16),
            pltpu.VMEM((rows * residues, pc), BF16),
            pltpu.VMEM((2 * rows * seqs, width // 2 * pc), BF16),
            pltpu.VMEM((s_loc * width, devices * residues), F32),
            pltpu.VMEM((chips, top, pc), BF16),
            pltpu.VMEM((chips, top, pc), BF16),
            pltpu.VMEM((devices, small, pc), BF16),
            pltpu.VMEM((devices - 1, small, pc), BF16),
            dma((2 * chips,)),
            dma((2 * chips,)),
            dma,
            dma,
            dma((chips,)),
            dma((chips,)),
            dma((devices - 1,)),
            dma((devices - 1,)),
            dma((2 * chips,)),
            dma((2 * chips,)),
            dma((devices - 1,)),
            dma((devices - 1,)),
        ]
        + [pltpu.VMEM(value.shape, value.dtype) for value in inputs]
        + [dma((len(inputs),))],
        compiler_params=pltpu.CompilerParams(
            collective_id=0, has_side_effects=True, vmem_limit_bytes=61 * 1024 * 1024
        ),
    )(sequence_row_mask, residue_mask, *inputs)
    update, left_t, right_t, grad_out, grad_gate = pl.pallas_call(
        unpack_kernel,
        name="unpack",
        out_shape=(
            jax.ShapeDtypeStruct((rows, residues, pc), BF16),
            jax.ShapeDtypeStruct((width, ch), F32),
            jax.ShapeDtypeStruct((width, ch), F32),
            jax.ShapeDtypeStruct((width * width, pc), F32),
            jax.ShapeDtypeStruct((pc, pc), F32),
        ),
        in_specs=[vmem] * 3,
        out_specs=(pl.BlockSpec(memory_space=pltpu.HBM),) + (vmem,) * 4,
        scratch_shapes=[dma],
        compiler_params=pltpu.CompilerParams(vmem_limit_bytes=32 * 1024 * 1024),
    )(middle, sums, rest)
    return update, left_t.T, right_t.T, grad_out, grad_gate


def per_device(*arrays):
    alignment_state, pair_state = arrays[0], arrays[1]
    s_loc, residues, ch = alignment_state.shape
    rows, _, pc = pair_state.shape
    width = arrays[6].shape[1]
    devices = lax.axis_size("row")
    fits = (
        lax.axis_size("col") == 1
        and devices % 2 == 0
        and (s_loc * ch, pc, residues) == (128, 128, 128)
        and rows == 8
        and width % devices == 0
        and pc == devices * 8
        and s_loc * devices == 32
    )
    return fused_device(*arrays) if fits else general_device(*arrays)


def solution(mesh):
    return jax.shard_map(
        per_device,
        mesh=mesh,
        in_specs=(
            P(("grp", "row"), "col", None),
            P(("grp", "row"), "col", None),
            P(("grp", "row"), "col", None),
            P("grp"),
            P("grp"),
            P(),
            P(),
            P(),
            P(),
            P(),
            P(),
        ),
        out_specs=(
            P(("grp", "row"), "col", None),
            P("grp", None),
            P("grp", None),
            P("grp", None),
            P("grp", None),
        ),
        check_vma=False,
    )
```

```python
import jax
import jax.numpy as jnp
from jax import lax
from jax.experimental import pallas as pl
from jax.experimental.pallas import tpu as pltpu
from jax.sharding import PartitionSpec as P


def layer_normalize(alignment_state, norm_gain_vector):
    value_entries = alignment_state.astype(jnp.float32)
    average = jnp.mean(value_entries, axis=-1, keepdims=True)
    centred = value_entries - average
    variance = jnp.mean(centred * centred, axis=-1, keepdims=True)
    return (centred * lax.rsqrt(variance + 1e-05) * norm_gain_vector).astype(jnp.bfloat16)


def general_device(
    alignment_state,
    pair_state,
    cotangent,
    sequence_row_mask,
    residue_mask,
    norm_gain_vector,
    left_matrix_weight,
    right_matrix_weight,
    output_weight,
    output_bias,
    gate_matrix,
):
    sequence_resident, column_count, alignment_channel_count = alignment_state.shape
    count_of_rows = pair_state.shape[0]
    pair_chans = pair_state.shape[2]
    projection_width = left_matrix_weight.shape[1]
    every_sequence = sequence_row_mask.shape[0]
    row_at = lax.axis_index("row")
    col_at = lax.axis_index("col")
    number_of_rows = lax.axis_size("row")
    contract_first = (((0,), (0,)), ((), ()))
    contract_second = (((1,), (1,)), ((), ()))
    resident_features = layer_normalize(alignment_state, norm_gain_vector)
    seq_flags = sequence_row_mask.astype(jnp.float32)
    res_flags = residue_mask.astype(jnp.float32)
    my_cols = lax.dynamic_slice_in_dim(res_flags, col_at * column_count, column_count, 0)
    my_rows = lax.dynamic_slice_in_dim(res_flags, row_at * count_of_rows, count_of_rows, 0)
    panel_mask = seq_flags[:, None] * my_rows[None, :]
    column_mask = seq_flags[:, None] * my_cols[None, :]
    broadcast_features = lax.all_gather(
        resident_features.reshape(sequence_resident, column_count * alignment_channel_count),
        "col",
        axis=1,
        tiled=True,
    )
    row_portions = broadcast_features.reshape(
        sequence_resident, number_of_rows, count_of_rows * alignment_channel_count
    )
    row_feats = lax.all_to_all(
        row_portions, "row", split_axis=1, concat_axis=0, tiled=True
    ).reshape(every_sequence * count_of_rows, alignment_channel_count)
    left_panel = (
        jnp.dot(row_feats, left_matrix_weight, preferred_element_type=jnp.float32).reshape(
            every_sequence, count_of_rows, projection_width
        )
        * panel_mask[:, :, None]
    ).astype(jnp.bfloat16)
    left_matrix = left_panel.transpose(1, 2, 0).reshape(
        count_of_rows * projection_width, every_sequence
    )
    column_features = lax.all_gather(
        resident_features.reshape(sequence_resident, column_count * alignment_channel_count),
        "row",
        axis=0,
        tiled=True,
    ).reshape(every_sequence, column_count, alignment_channel_count)
    right_panel = (
        jnp.dot(
            column_features.reshape(every_sequence * column_count, alignment_channel_count),
            right_matrix_weight,
            preferred_element_type=jnp.float32,
        ).reshape(every_sequence, column_count, projection_width)
        * column_mask[:, :, None]
    ).astype(jnp.bfloat16)
    surplus_offset = jnp.zeros((alignment_channel_count, projection_width), jnp.float32)

    def absorb(extra, first_col, width_columns, right_part):
        feat_blk = (
            lax.dynamic_slice_in_dim(column_features, first_col, width_columns, 1)
            .reshape(every_sequence * width_columns, alignment_channel_count)
            .astype(jnp.float32)
        )
        mask_blk = lax.dynamic_slice_in_dim(column_mask, first_col, width_columns, 1)
        masked_part = (
            right_part.reshape(every_sequence, width_columns, projection_width)
            * mask_blk[:, :, None]
        ).reshape(every_sequence * width_columns, projection_width)
        return extra + jnp.dot(feat_blk.T, masked_part, precision=lax.Precision.HIGHEST)

    right_flat = right_panel.reshape(every_sequence, column_count * projection_width)
    row_total = jnp.sum(seq_flags)
    col_block = 128
    n_blocks = column_count // col_block

    def one_block(block_idx, carry):
        new_update, grad_out, grad_gate, left_acc, extra = carry
        first_col = block_idx * col_block
        right_blk = lax.dynamic_slice_in_dim(
            right_flat, first_col * projection_width, col_block * projection_width, 1
        )
        outer_prod = jnp.dot(left_matrix, right_blk, preferred_element_type=jnp.float32)
        outer_prod = outer_prod.reshape(
            count_of_rows, projection_width, col_block, projection_width
        ).transpose(0, 2, 1, 3)
        outer_prod = outer_prod.reshape(
            count_of_rows * col_block, projection_width * projection_width
        ).astype(jnp.bfloat16)
        linear = (
            jnp.dot(outer_prod, output_weight, preferred_element_type=jnp.float32) + output_bias
        )
        pair_blk = lax.dynamic_slice_in_dim(pair_state, first_col, col_block, 1).reshape(
            count_of_rows * col_block, pair_chans
        )
        gate_val = jax.nn.sigmoid(
            jnp.dot(pair_blk, gate_matrix, preferred_element_type=jnp.float32)
        )
        blk_flags = lax.dynamic_slice_in_dim(my_cols, first_col, col_block, 0)
        divisor = jnp.maximum(row_total * my_rows[:, None] * blk_flags[None, :], 1.0).reshape(
            count_of_rows * col_block, 1
        )
        cot_blk = (
            lax.dynamic_slice_in_dim(cotangent, first_col, col_block, 1)
            .reshape(count_of_rows * col_block, pair_chans)
            .astype(jnp.float32)
        )
        new_pair = (gate_val * linear / divisor).astype(jnp.bfloat16)
        new_update = lax.dynamic_update_slice_in_dim(
            new_update, new_pair.reshape(count_of_rows, col_block, pair_chans), first_col, 1
        )
        grad_lin = (cot_blk * gate_val / divisor).astype(jnp.bfloat16)
        grad_pre = (cot_blk * linear / divisor * gate_val * (1.0 - gate_val)).astype(jnp.bfloat16)
        grad_out = grad_out + lax.dot_general(
            outer_prod, grad_lin, contract_first, preferred_element_type=jnp.float32
        )
        grad_gate = grad_gate + lax.dot_general(
            pair_blk, grad_pre, contract_first, preferred_element_type=jnp.float32
        )
        grad_outer = lax.dot_general(
            grad_lin, output_weight, contract_second, preferred_element_type=jnp.float32
        ).astype(jnp.bfloat16)
        outer_turned = (
            grad_outer.reshape(count_of_rows, col_block, projection_width, projection_width)
            .transpose(0, 2, 1, 3)
            .reshape(count_of_rows * projection_width, col_block * projection_width)
        )
        left_acc = left_acc + lax.dot_general(
            outer_turned, right_blk, contract_second, preferred_element_type=jnp.float32
        )
        right_part = lax.dot_general(
            left_matrix, outer_turned, contract_first, preferred_element_type=jnp.float32
        )
        extra = absorb(extra, first_col, col_block, right_part)
        return (new_update, grad_out, grad_gate, left_acc, extra)

    start_carry = (
        jnp.zeros((count_of_rows, column_count, pair_chans), jnp.bfloat16),
        jnp.zeros((projection_width * projection_width, pair_chans), jnp.float32),
        jnp.zeros((pair_chans, pair_chans), jnp.float32),
        jnp.zeros((count_of_rows * projection_width, every_sequence), jnp.float32),
        surplus_offset,
    )
    new_update, grad_out, grad_gate, left_acc, extra = lax.fori_loop(
        0, n_blocks, one_block, start_carry
    )
    grad_left_act = (
        left_acc.reshape(count_of_rows, projection_width, every_sequence).transpose(2, 0, 1)
        * panel_mask[:, :, None]
    )
    grad_left = jnp.dot(
        row_feats.astype(jnp.float32).T,
        grad_left_act.reshape(every_sequence * count_of_rows, projection_width),
        precision=lax.Precision.HIGHEST,
    )
    summed_left, summed_right, summed_out, summed_gate = lax.psum(
        (grad_left, extra, grad_out, grad_gate), ("row", "col")
    )
    return (new_update, summed_left, summed_right, summed_out, summed_gate)


F32 = jnp.float32
BF16 = jnp.bfloat16
MESH = pl.DeviceIdType.MESH
NT = (((1,), (1,)), ((), ()))
TN = (((0,), (0,)), ((), ()))
NN = (((1,), (0,)), ((), ()))


def mm(a, b, dims=NN):
    return lax.dot_general(a, b, dims, preferred_element_type=F32)


def send(src, dst, send_sem, recv_sem, target):
    copy = pltpu.make_async_remote_copy(
        src_ref=src, dst_ref=dst, send_sem=send_sem, recv_sem=recv_sem,
        device_id={"row": target}, device_id_type=MESH,
    )
    copy.start()
    return copy


def gather_start(buf, me, core, chip, chips, send_sem, recv_sem):
    block = buf.at[me]
    copies = [send(block, block, send_sem.at[0], recv_sem.at[0], chip * 2 + 1 - core)]
    for k in range(1, chips):
        target = lax.rem(chip + k, chips) * 2 + 1 - core
        copies.append(send(block, block, send_sem.at[k], recv_sem.at[k], target))
    return copies


def gather_finish(copies, buf, core, chip, chips, send_sem, recv_sem):
    partner = chip * 2 + 1 - core
    passed = []
    for k in range(1, chips):
        copies[k].wait_recv()
        block = buf.at[lax.rem(chip - k + chips, chips) * 2 + 1 - core]
        at = chips + k
        passed.append(send(block, block, send_sem.at[at], recv_sem.at[at], partner))
    copies[0].wait_recv()
    for copy in passed:
        copy.wait_recv()
    return copies + passed


def fused_kernel(
    seq_ref, res_ref, *inputs_and_rest,
):
    hbm, rest = inputs_and_rest[:10], inputs_and_rest[10:]
    outs_and_scratch, vmem, load_sem = rest[:-11], rest[-11:-1], rest[-1]
    loads = [
        pltpu.make_async_copy(src, dst, load_sem.at[n])
        for n, (src, dst) in enumerate(zip(hbm, vmem))
    ]
    for n in (0, 1, 5, 7, 2, 3, 8, 4, 6, 9):
        loads[n].start()
    fused_body(loads, seq_ref, res_ref, *vmem, *outs_and_scratch)


def fused_body(
    loads, seq_ref, res_ref, align_ref, gain_ref, pair_ref, gm_ref, w_ref, resrow_ref, wl_ref,
    wr_ref, cot_ref, bias_ref,
    upd_ref, gt_s, gs_s, ps_s,
    feat, near, gate_s, w2_s, w32_s, wr32_s, own_s, rin_s, rt_s, fr_s, lt_s, m_s, g_s, pre_s, n2_s,
    gr2_s, sb_s, rb_s, sm_s, rm_s, pk_s, pr_s,
    send_r, recv_r, send_n, recv_n, send_f, recv_f, send_x, recv_x, send_b, recv_b, send_m, recv_m,
    send_g, recv_g, send_h, recv_h, send_p, recv_p,
):
    me = lax.axis_index("row")
    core = lax.rem(me, 2)
    chip = lax.div(me, 2)
    x_at = lax.rem(chip, 2)
    z_at = lax.div(chip, 2)
    half = 1 - core
    _, chips, residues, lanes = feat.shape
    devices = 2 * chips
    planes = chips // 2
    s_loc, ch, _ = align_ref.shape
    rows, _, pc = pair_ref.shape
    width = wl_ref.shape[0]
    seqs = s_loc * devices
    partner = chip * 2 + 1 - core
    across = (z_at * 2 + 1 - x_at) * 2 + core
    wide = width // 2
    mine_wide = rows * seqs

    barrier = pltpu.get_barrier_semaphore()
    for k in range(1, devices):
        pl.semaphore_signal(
            barrier, inc=1, device_id={"row": lax.rem(me + k, devices)}, device_id_type=MESH
        )

    for n in (0, 1, 5, 7):
        loads[n].wait()
    parts = []
    for s in range(s_loc):
        value = align_ref[s].astype(F32)
        centred = value - jnp.mean(value, axis=0, keepdims=True)
        variance = jnp.mean(centred * centred, axis=0, keepdims=True)
        parts.append(centred * lax.rsqrt(variance + 1e-05))
    gain = jnp.concatenate([gain_ref[...]] * s_loc, axis=1)
    own = (jnp.transpose(jnp.concatenate(parts, axis=0)) * gain).astype(BF16)
    feat[core, x_at * planes + z_at] = own

    resrow = resrow_ref[...].astype(F32)
    wr32_s[...] = jnp.concatenate([wr_ref[...].astype(F32)] * s_loc, axis=1)
    lane_s = lax.div(lax.broadcasted_iota(jnp.int32, (wide, lanes), 1), ch)
    wr_parts = []
    for h in range(2):
        block = jnp.concatenate(
            [wr32_s[pl.ds(2 * h + t, chips, stride=4), :] for t in range(2)], axis=0
        )
        for s in range(s_loc):
            wr_parts.append(jnp.where(lane_s == s, block, 0.0))
    right = mm(jnp.concatenate(wr_parts, axis=0).astype(BF16), own, NT)
    flags = [seq_ref[me * s_loc + s].astype(F32) * resrow for s in range(s_loc)]
    for h in range(2):
        for s in range(s_loc):
            at = (h * s_loc + s) * wide
            own_s[h, s * wide : (s + 1) * wide, :] = (
                right[at : at + wide] * flags[s]
            ).astype(BF16)
    rin_s[half, me] = own_s[half]
    pl.semaphore_wait(barrier, devices - 1)

    rights = []
    nears = []
    mine_at = feat.at[core, x_at * planes + z_at]
    for k in range(chips):
        to = lax.rem(chip + k, chips)
        window = pl.ds(pl.multiple_of(to * 2 * rows, 2 * rows), 2 * rows)
        nears.append(
            send(
                mine_at.at[window], near.at[core, chip], send_n.at[k], recv_n.at[k],
                to * 2 + 1 - core,
            )
        )
    for k in range(1, devices):
        to = lax.rem(me + k, devices)
        h = 1 - lax.rem(to, 2)
        rights.append(
            send(own_s.at[h], rin_s.at[h, me], send_r.at[k - 1], recv_r.at[k - 1], to)
        )
    column = []
    for k in range(1, planes):
        to = (lax.rem(z_at + k, planes) * 2 + x_at) * 2 + core
        column.append(send(mine_at, mine_at, send_f.at[k], recv_f.at[k], to))
    sideways = [send(mine_at, mine_at, send_f.at[0], recv_f.at[0], across)]

    for n in (2, 3, 4, 6, 8, 9):
        loads[n].wait()
    gm = gm_ref[...]
    rescol = jnp.transpose(jnp.broadcast_to(resrow, (pc, residues)))
    seq = [seq_ref[s].astype(F32) for s in range(seqs)]
    both_rows = [res_ref[chip * 2 * rows + i].astype(F32) for i in range(2 * rows)]
    mine = [res_ref[me * rows + i].astype(F32) for i in range(rows)]
    row_total = seq[0]
    for s in range(1, seqs):
        row_total = row_total + seq[s]
    present = 1.0 / jnp.maximum(row_total * rescol, 1.0)
    inverse = [present * mine[i] + (1.0 - mine[i]) for i in range(rows)]
    for i in range(rows):
        gate = jax.nn.sigmoid(mm(pair_ref[i], gm))
        gate_s[i] = gate
        g_s[core, :, i * pc : (i + 1) * pc] = (
            cot_ref[i].astype(F32) * (gate * inverse[i])
        ).astype(BF16)
    crossing = send(g_s.at[core], g_s.at[core], send_x, recv_x, partner)

    w32_s[...] = w_ref[...].astype(F32)
    for h in range(2):
        for t in range(2):
            for k in range(chips):
                e, q = 4 * k + 2 * h + t, t * chips + k
                w2_s[h, :, q * pc : (q + 1) * pc] = w32_s[
                    pl.ds(e, width, stride=width), :
                ].astype(BF16)
    lane = lax.broadcasted_iota(jnp.int32, (1, 2 * mine_wide), 1)
    maskrow = jnp.zeros((1, 2 * mine_wide), F32)
    for s in range(s_loc):
        for d in range(devices):
            maskrow = jnp.where(lax.rem(lane, seqs) == s * devices + d, seq[d * s_loc + s], maskrow)
    resl = jnp.zeros((1, 2 * mine_wide), F32)
    for i in range(2 * rows):
        resl = jnp.where(lax.div(lane, seqs) == i, both_rows[i], resl)
    maskrow = maskrow * resl
    wlt = wl_ref[...].astype(F32)
    wlt2 = jnp.concatenate([wlt] * s_loc, axis=1).astype(BF16)

    for copy in nears:
        copy.wait_recv()
    near_pass = send(near.at[half], near.at[half], send_n.at[chips], recv_n.at[chips], partner)
    near_pass.wait_recv()
    for d in range(devices):
        fr_s[d * 2 * rows : (d + 1) * 2 * rows, :] = near[d % 2, d // 2].astype(F32)
    lane_d = lax.div(lax.broadcasted_iota(jnp.int32, (devices, lanes), 1), ch)
    pieces = []
    for i in range(2 * rows):
        block = fr_s[pl.ds(i, devices, stride=2 * rows), :]
        for s in range(s_loc):
            pieces.append(jnp.where(lane_d == s, block, 0.0))
    fr = jnp.concatenate(pieces, axis=0).astype(BF16)
    left_t = mm(wlt2, fr, NT) * maskrow
    for c in range(2):
        lt_s[c] = left_t[:, c * mine_wide : (c + 1) * mine_wide]
    left_t = left_t.astype(BF16)

    left = jnp.transpose(lt_s[core]).astype(BF16)
    for h in range(2):
        for e in range(0, wide, 2):
            part = mm(left, w2_s[h, :, e * pc : (e + 2) * pc]).astype(BF16)
            for n in range(2):
                at = (h * wide + e + n) * seqs
                for i in range(rows):
                    m_s[at : at + seqs, i * pc : (i + 1) * pc] = part[
                        i * seqs : (i + 1) * seqs, n * pc : (n + 1) * pc
                    ]

    def lay_out(h):
        for d in range(devices):
            for s in range(s_loc):
                rt_s[h, pl.ds(s * devices + d, wide, stride=seqs), :] = rin_s[
                    h, d, s * wide : (s + 1) * wide, :
                ].astype(F32)

    crossing.wait_recv()
    for copy in rights:
        copy.wait_recv()
    right_pass = send(
        rin_s.at[half], rin_s.at[half], send_r.at[devices - 1], recv_r.at[devices - 1], partner
    )
    lay_out(half)
    rtt = rt_s[half].astype(BF16)
    step = 4
    for e in range(0, wide, step):
        for c in range(2):
            part = mm(rtt[e * seqs : (e + step) * seqs], g_s[c]).astype(BF16)
            for h in range(step):
                for i in range(rows):
                    at = (c * rows + i) * seqs
                    n2_s[at : at + seqs, (e + h) * pc : (e + h + 1) * pc] = part[
                        h * seqs : (h + 1) * seqs, i * pc : (i + 1) * pc
                    ]
    go = mm(left_t, n2_s[...])
    for k in range(chips):
        for t in range(2):
            q = t * chips + k
            sb_s[k, t * width : (t + 1) * width, :] = go[:, q * pc : (q + 1) * pc].astype(BF16)
    scatter = []
    for k in range(chips):
        to = lax.rem(chip + k, chips)
        scatter.append(
            send(sb_s.at[to], rb_s.at[k], send_b.at[k], recv_b.at[k], to * 2 + 1 - core)
        )

    for k in range(1, planes):
        column[k - 1].wait_recv()
        block = feat.at[core, x_at * planes + lax.rem(z_at - k + planes, planes)]
        at = planes + k
        sideways.append(send(block, block, send_f.at[at], recv_f.at[at], across))
    block = feat.at[core, pl.ds(x_at * planes, planes)]
    feat_pass = [send(block, block, send_f.at[planes], recv_f.at[planes], partner)]

    right_pass.wait_recv()
    lay_out(core)
    rt = jnp.transpose(rt_s[...].reshape(width * seqs, residues)).astype(BF16)

    bias = bias_ref[...]
    for i in range(0, rows, 2):
        lin2 = mm(rt, m_s[:, i * pc : (i + 2) * pc])
        for h in range(2):
            linear = lin2[:, h * pc : (h + 1) * pc] + bias
            gate = gate_s[i + h]
            scaled = gate * inverse[i + h]
            upd_ref[i + h] = (scaled * linear).astype(BF16)
            pre_s[(i + h) * residues : (i + h + 1) * residues, :] = (
                cot_ref[i + h].astype(F32) * scaled * linear * (1.0 - gate)
            ).astype(BF16)
    gg = mm(pair_ref[...].reshape(rows * residues, pc), pre_s[...], TN)
    g_rows = pc // chips
    sm_s[...] = gg.reshape(chips, g_rows, pc).astype(BF16)

    def portion(k):
        to = lax.rem(chip + k, chips)
        return pltpu.make_async_remote_copy(
            src_ref=sm_s.at[to], dst_ref=rm_s.at[2 * k + core], send_sem=send_m.at[k],
            recv_sem=recv_m.at[2 * k + core], device_id={"row": to * 2 + 1}, device_id_type=MESH,
        )

    def arrived(k, c):
        return pltpu.make_async_remote_copy(
            src_ref=sm_s.at[0], dst_ref=rm_s.at[2 * k + c], send_sem=send_m.at[k],
            recv_sem=recv_m.at[2 * k + c], device_id={"row": partner}, device_id_type=MESH,
        )

    @pl.when(core == 0)
    def _():
        portion(0).start()

    for k in range(1, chips):
        portion(k).start()

    act = mm(w2_s[half], n2_s[...], NT) * maskrow
    gl2 = mm(act.astype(BF16), fr)
    gl = gl2[:, :ch]
    for s in range(1, s_loc):
        gl = gl + gl2[:, s * ch : (s + 1) * ch]

    back = mm(m_s[...], g_s[core], NT)
    rt_s[...] = back.reshape(2, wide * seqs, residues)
    for p in range(2):
        for n in range(chips):
            b = p * chips + n
            d = (n % planes) * 4 + (n // planes) * 2 + p
            for s in range(s_loc):
                flag = seq[d * s_loc + s] * resrow
                for h in range(2):
                    at = s * width + h * wide
                    gr2_s[at : at + wide, b * residues : (b + 1) * residues] = (
                        rt_s[h, pl.ds(s * devices + d, wide, stride=seqs), :] * flag
                    )
    scatter[0].wait_recv()
    total = rb_s[0].astype(F32)
    for k in range(1, chips):
        scatter[k].wait_recv()
        total = total + rb_s[k].astype(F32)
    gt_s[me] = total.astype(BF16)
    copies = gather_start(gt_s, me, core, chip, chips, send_g, recv_g)

    for copy in sideways:
        copy.wait_recv()
    block = feat.at[core, pl.ds((1 - x_at) * planes, planes)]
    at = 2 * planes
    feat_pass.append(send(block, block, send_f.at[at], recv_f.at[at], partner))

    for copy in feat_pass:
        copy.wait_recv()
    feats = feat[...].reshape(devices * residues, lanes)
    gr2 = mm(gr2_s[...].astype(BF16), feats)
    gr = gr2[:width, :ch]
    for s in range(1, s_loc):
        gr = gr + gr2[s * width : (s + 1) * width, s * ch : (s + 1) * ch]

    pk_s[0] = jnp.concatenate([gl[:wide], gl[wide:]], axis=1)
    pk_s[1] = jnp.concatenate([gr[:wide], gr[wide:]], axis=1)
    twin = send(pk_s.at[half], pr_s, send_p.at[0], recv_p.at[0], partner)

    twin.wait_recv()
    ps_s[me] = (pk_s[core] + pr_s[...]).astype(BF16)
    last = []
    for k in range(1, devices):
        block = ps_s.at[me]
        last.append(
            send(block, block, send_p.at[k], recv_p.at[k], lax.rem(me + k, devices))
        )

    def spread(k, c):
        block = gs_s.at[chip]
        return pltpu.make_async_remote_copy(
            src_ref=block, dst_ref=block, send_sem=send_h.at[2 * k + c], recv_sem=recv_h.at[k],
            device_id={"row": lax.rem(chip + k, chips) * 2 + c}, device_id_type=MESH,
        )

    def landed(k):
        block = gs_s.at[lax.rem(chip - k + chips, chips)]
        return pltpu.make_async_remote_copy(
            src_ref=block, dst_ref=block, send_sem=send_h.at[2 * k], recv_sem=recv_h.at[k],
            device_id={"row": partner}, device_id_type=MESH,
        )

    @pl.when(core == 1)
    def _():
        total = sm_s[chip].astype(F32)
        arrived(0, 0).wait_recv()
        total = total + rm_s[0].astype(F32)
        for k in range(1, chips):
            for c in range(2):
                arrived(k, c).wait_recv()
                total = total + rm_s[2 * k + c].astype(F32)
        gs_s[chip] = total.astype(BF16)
        spread(0, 0).start()
        for k in range(1, chips):
            for c in range(2):
                spread(k, c).start()

    done2 = gather_finish(copies, gt_s, core, chip, chips, send_g, recv_g)
    for copy in last:
        copy.wait_recv()

    @pl.when(core == 0)
    def _():
        landed(0).wait_recv()
        portion(0).wait_send()

    for k in range(1, chips):
        landed(k).wait_recv()
        portion(k).wait_send()

    @pl.when(core == 1)
    def _():
        spread(0, 0).wait_send()
        for k in range(1, chips):
            for c in range(2):
                spread(k, c).wait_send()

    for copy in (
        nears + [near_pass] + rights + [right_pass] + column + sideways + feat_pass + [crossing]
        + scatter + [twin] + done2 + last
    ):
        copy.wait_send()


def unpack_kernel(
    mid_ref, sum_ref, gate_ref, rest_ref, upd_ref, gl_ref, gr_ref, go_ref, gg_ref, sem,
):
    devices = sum_ref.shape[0]
    width, ch = gl_ref.shape
    per = width // devices
    wide = width // 2
    copy = pltpu.make_async_copy(mid_ref, upd_ref, sem.at[0])
    copy.start()
    for k in range(devices):
        for h in range(per):
            go_ref[pl.ds(k * per + h, width, stride=width), :] = sum_ref[
                k, h * width : (h + 1) * width, :
            ].astype(F32)
    gg_ref[...] = gate_ref[...].reshape(gg_ref.shape).astype(F32)
    left, right = rest_ref[0].astype(F32), rest_ref[1].astype(F32)
    for k in range(2, devices, 2):
        left = left + rest_ref[k].astype(F32)
        right = right + rest_ref[k + 1].astype(F32)
    for h in range(2):
        gl_ref[h * wide : (h + 1) * wide, :] = left[:, h * ch : (h + 1) * ch]
        for t in range(2):
            gr_ref[pl.ds(2 * h + t, wide // 2, stride=4), :] = right[
                t * (wide // 2) : (t + 1) * (wide // 2), h * ch : (h + 1) * ch
            ]
    copy.wait()


def fused_device(
    alignment_state, pair_state, cotangent, sequence_row_mask, residue_mask, norm_gain_vector,
    left_matrix_weight, right_matrix_weight, output_weight, output_bias, gate_matrix,
):
    s_loc, residues, ch = alignment_state.shape
    rows, _, pc = pair_state.shape
    width = left_matrix_weight.shape[1]
    devices = lax.axis_size("row")
    seqs = s_loc * devices
    chips = devices // 2
    lanes = s_loc * ch
    top = (width // devices) * width
    smem = pl.BlockSpec(memory_space=pltpu.SMEM)
    vmem = pl.BlockSpec(memory_space=pltpu.VMEM)
    dma = pltpu.SemaphoreType.DMA
    inputs = (
        alignment_state.transpose(0, 2, 1),
        norm_gain_vector.reshape(1, ch),
        pair_state,
        gate_matrix,
        output_weight,
        residue_mask.reshape(1, residues),
        left_matrix_weight.T,
        right_matrix_weight.T,
        cotangent,
        output_bias.reshape(1, pc),
    )
    middle, sums, gates, rest = pl.pallas_call(
        fused_kernel,
        name="fused",
        out_shape=(
            pltpu.VMEM((rows, residues, pc), BF16),
            pltpu.VMEM((devices, top, pc), BF16),
            pltpu.VMEM((chips, pc // chips, pc), BF16),
            pltpu.VMEM((devices, width // 2, 2 * ch), BF16),
        ),
        in_specs=[smem, smem] + [pl.BlockSpec(memory_space=pltpu.HBM)] * 10,
        out_specs=(vmem,) * 4,
        scratch_shapes=[
            pltpu.VMEM((2, chips, residues, lanes), BF16),
            pltpu.VMEM((2, chips, 2 * rows, lanes), BF16),
            pltpu.VMEM((rows, residues, pc), F32),
            pltpu.VMEM((2, width, width // 2 * pc), BF16),
            pltpu.VMEM((width * width, pc), F32),
            pltpu.VMEM((width, lanes), F32),
            pltpu.VMEM((2, s_loc * width // 2, residues), BF16),
            pltpu.VMEM((2, devices, s_loc * width // 2, residues), BF16),
            pltpu.VMEM((2, width // 2 * seqs, residues), F32),
            pltpu.VMEM((devices * 2 * rows, lanes), F32),
            pltpu.VMEM((2, width, rows * seqs), F32),
            pltpu.VMEM((width * seqs, rows * pc), BF16),
            pltpu.VMEM((2, residues, rows * pc), BF16),
            pltpu.VMEM((rows * residues, pc), BF16),
            pltpu.VMEM((2 * rows * seqs, width // 2 * pc), BF16),
            pltpu.VMEM((s_loc * width, devices * residues), F32),
            pltpu.VMEM((chips, top, pc), BF16),
            pltpu.VMEM((chips, top, pc), BF16),
            pltpu.VMEM((chips, pc // chips, pc), BF16),
            pltpu.VMEM((devices, pc // chips, pc), BF16),
            pltpu.VMEM((2, width // 2, 2 * ch), F32),
            pltpu.VMEM((width // 2, 2 * ch), F32),
            dma((devices,)),
            dma((devices,)),
            dma((chips + 1,)),
            dma((chips + 1,)),
            dma((chips + 1,)),
            dma((chips + 1,)),
            dma,
            dma,
            dma((chips,)),
            dma((chips,)),
            dma((chips,)),
            dma((devices,)),
            dma((2 * chips,)),
            dma((2 * chips,)),
            dma((devices,)),
            dma((chips,)),
            dma((devices,)),
            dma((devices,)),
        ]
        + [pltpu.VMEM(value.shape, value.dtype) for value in inputs]
        + [dma((len(inputs),))],
        compiler_params=pltpu.CompilerParams(
            collective_id=0, has_side_effects=True, vmem_limit_bytes=61 * 1024 * 1024
        ),
    )(sequence_row_mask, residue_mask, *inputs)
    update, left_t, right_t, grad_out, grad_gate = pl.pallas_call(
        unpack_kernel,
        name="unpack",
        out_shape=(
            jax.ShapeDtypeStruct((rows, residues, pc), BF16),
            jax.ShapeDtypeStruct((width, ch), F32),
            jax.ShapeDtypeStruct((width, ch), F32),
            jax.ShapeDtypeStruct((width * width, pc), F32),
            jax.ShapeDtypeStruct((pc, pc), F32),
        ),
        in_specs=[vmem] * 4,
        out_specs=(pl.BlockSpec(memory_space=pltpu.HBM),) + (vmem,) * 4,
        scratch_shapes=[dma((1,))],
        compiler_params=pltpu.CompilerParams(vmem_limit_bytes=32 * 1024 * 1024),
    )(middle, sums, gates, rest)
    return update, left_t.T, right_t.T, grad_out, grad_gate


def per_device(*arrays):
    alignment_state, pair_state = arrays[0], arrays[1]
    s_loc, residues, ch = alignment_state.shape
    rows, _, pc = pair_state.shape
    width = arrays[6].shape[1]
    devices = lax.axis_size("row")
    fits = (
        lax.axis_size("col") == 1
        and devices % 2 == 0
        and (s_loc * ch, pc, residues) == (128, 128, 128)
        and rows == 8
        and width % devices == 0
        and pc == devices * 8
        and s_loc * devices == 32
    )
    return fused_device(*arrays) if fits else general_device(*arrays)


def solution(mesh):
    return jax.shard_map(
        per_device,
        mesh=mesh,
        in_specs=(
            P(("grp", "row"), "col", None),
            P(("grp", "row"), "col", None),
            P(("grp", "row"), "col", None),
            P("grp"),
            P("grp"),
            P(),
            P(),
            P(),
            P(),
            P(),
            P(),
        ),
        out_specs=(
            P(("grp", "row"), "col", None),
            P("grp", None),
            P("grp", None),
            P("grp", None),
            P("grp", None),
        ),
        check_vma=False,
    )
```

```python
import jax
import jax.numpy as jnp
from jax import lax
from jax.experimental import pallas as pl
from jax.experimental.pallas import tpu as pltpu
from jax.sharding import PartitionSpec as P


def layer_normalize(alignment_state, norm_gain_vector):
    value_entries = alignment_state.astype(jnp.float32)
    average = jnp.mean(value_entries, axis=-1, keepdims=True)
    centred = value_entries - average
    variance = jnp.mean(centred * centred, axis=-1, keepdims=True)
    return (centred * lax.rsqrt(variance + 1e-05) * norm_gain_vector).astype(jnp.bfloat16)


def general_device(
    alignment_state,
    pair_state,
    cotangent,
    sequence_row_mask,
    residue_mask,
    norm_gain_vector,
    left_matrix_weight,
    right_matrix_weight,
    output_weight,
    output_bias,
    gate_matrix,
):
    sequence_resident, column_count, alignment_channel_count = alignment_state.shape
    count_of_rows = pair_state.shape[0]
    pair_chans = pair_state.shape[2]
    projection_width = left_matrix_weight.shape[1]
    every_sequence = sequence_row_mask.shape[0]
    row_at = lax.axis_index("row")
    col_at = lax.axis_index("col")
    number_of_rows = lax.axis_size("row")
    contract_first = (((0,), (0,)), ((), ()))
    contract_second = (((1,), (1,)), ((), ()))
    resident_features = layer_normalize(alignment_state, norm_gain_vector)
    seq_flags = sequence_row_mask.astype(jnp.float32)
    res_flags = residue_mask.astype(jnp.float32)
    my_cols = lax.dynamic_slice_in_dim(res_flags, col_at * column_count, column_count, 0)
    my_rows = lax.dynamic_slice_in_dim(res_flags, row_at * count_of_rows, count_of_rows, 0)
    panel_mask = seq_flags[:, None] * my_rows[None, :]
    column_mask = seq_flags[:, None] * my_cols[None, :]
    broadcast_features = lax.all_gather(
        resident_features.reshape(sequence_resident, column_count * alignment_channel_count),
        "col",
        axis=1,
        tiled=True,
    )
    row_portions = broadcast_features.reshape(
        sequence_resident, number_of_rows, count_of_rows * alignment_channel_count
    )
    row_feats = lax.all_to_all(
        row_portions, "row", split_axis=1, concat_axis=0, tiled=True
    ).reshape(every_sequence * count_of_rows, alignment_channel_count)
    left_panel = (
        jnp.dot(row_feats, left_matrix_weight, preferred_element_type=jnp.float32).reshape(
            every_sequence, count_of_rows, projection_width
        )
        * panel_mask[:, :, None]
    ).astype(jnp.bfloat16)
    left_matrix = left_panel.transpose(1, 2, 0).reshape(
        count_of_rows * projection_width, every_sequence
    )
    column_features = lax.all_gather(
        resident_features.reshape(sequence_resident, column_count * alignment_channel_count),
        "row",
        axis=0,
        tiled=True,
    ).reshape(every_sequence, column_count, alignment_channel_count)
    right_panel = (
        jnp.dot(
            column_features.reshape(every_sequence * column_count, alignment_channel_count),
            right_matrix_weight,
            preferred_element_type=jnp.float32,
        ).reshape(every_sequence, column_count, projection_width)
        * column_mask[:, :, None]
    ).astype(jnp.bfloat16)
    surplus_offset = jnp.zeros((alignment_channel_count, projection_width), jnp.float32)

    def absorb(extra, first_col, width_columns, right_part):
        feat_blk = (
            lax.dynamic_slice_in_dim(column_features, first_col, width_columns, 1)
            .reshape(every_sequence * width_columns, alignment_channel_count)
            .astype(jnp.float32)
        )
        mask_blk = lax.dynamic_slice_in_dim(column_mask, first_col, width_columns, 1)
        masked_part = (
            right_part.reshape(every_sequence, width_columns, projection_width)
            * mask_blk[:, :, None]
        ).reshape(every_sequence * width_columns, projection_width)
        return extra + jnp.dot(feat_blk.T, masked_part, precision=lax.Precision.HIGHEST)

    right_flat = right_panel.reshape(every_sequence, column_count * projection_width)
    row_total = jnp.sum(seq_flags)
    col_block = 128
    n_blocks = column_count // col_block

    def one_block(block_idx, carry):
        new_update, grad_out, grad_gate, left_acc, extra = carry
        first_col = block_idx * col_block
        right_blk = lax.dynamic_slice_in_dim(
            right_flat, first_col * projection_width, col_block * projection_width, 1
        )
        outer_prod = jnp.dot(left_matrix, right_blk, preferred_element_type=jnp.float32)
        outer_prod = outer_prod.reshape(
            count_of_rows, projection_width, col_block, projection_width
        ).transpose(0, 2, 1, 3)
        outer_prod = outer_prod.reshape(
            count_of_rows * col_block, projection_width * projection_width
        ).astype(jnp.bfloat16)
        linear = (
            jnp.dot(outer_prod, output_weight, preferred_element_type=jnp.float32) + output_bias
        )
        pair_blk = lax.dynamic_slice_in_dim(pair_state, first_col, col_block, 1).reshape(
            count_of_rows * col_block, pair_chans
        )
        gate_val = jax.nn.sigmoid(
            jnp.dot(pair_blk, gate_matrix, preferred_element_type=jnp.float32)
        )
        blk_flags = lax.dynamic_slice_in_dim(my_cols, first_col, col_block, 0)
        divisor = jnp.maximum(row_total * my_rows[:, None] * blk_flags[None, :], 1.0).reshape(
            count_of_rows * col_block, 1
        )
        cot_blk = (
            lax.dynamic_slice_in_dim(cotangent, first_col, col_block, 1)
            .reshape(count_of_rows * col_block, pair_chans)
            .astype(jnp.float32)
        )
        new_pair = (gate_val * linear / divisor).astype(jnp.bfloat16)
        new_update = lax.dynamic_update_slice_in_dim(
            new_update, new_pair.reshape(count_of_rows, col_block, pair_chans), first_col, 1
        )
        grad_lin = (cot_blk * gate_val / divisor).astype(jnp.bfloat16)
        grad_pre = (cot_blk * linear / divisor * gate_val * (1.0 - gate_val)).astype(jnp.bfloat16)
        grad_out = grad_out + lax.dot_general(
            outer_prod, grad_lin, contract_first, preferred_element_type=jnp.float32
        )
        grad_gate = grad_gate + lax.dot_general(
            pair_blk, grad_pre, contract_first, preferred_element_type=jnp.float32
        )
        grad_outer = lax.dot_general(
            grad_lin, output_weight, contract_second, preferred_element_type=jnp.float32
        ).astype(jnp.bfloat16)
        outer_turned = (
            grad_outer.reshape(count_of_rows, col_block, projection_width, projection_width)
            .transpose(0, 2, 1, 3)
            .reshape(count_of_rows * projection_width, col_block * projection_width)
        )
        left_acc = left_acc + lax.dot_general(
            outer_turned, right_blk, contract_second, preferred_element_type=jnp.float32
        )
        right_part = lax.dot_general(
            left_matrix, outer_turned, contract_first, preferred_element_type=jnp.float32
        )
        extra = absorb(extra, first_col, col_block, right_part)
        return (new_update, grad_out, grad_gate, left_acc, extra)

    start_carry = (
        jnp.zeros((count_of_rows, column_count, pair_chans), jnp.bfloat16),
        jnp.zeros((projection_width * projection_width, pair_chans), jnp.float32),
        jnp.zeros((pair_chans, pair_chans), jnp.float32),
        jnp.zeros((count_of_rows * projection_width, every_sequence), jnp.float32),
        surplus_offset,
    )
    new_update, grad_out, grad_gate, left_acc, extra = lax.fori_loop(
        0, n_blocks, one_block, start_carry
    )
    grad_left_act = (
        left_acc.reshape(count_of_rows, projection_width, every_sequence).transpose(2, 0, 1)
        * panel_mask[:, :, None]
    )
    grad_left = jnp.dot(
        row_feats.astype(jnp.float32).T,
        grad_left_act.reshape(every_sequence * count_of_rows, projection_width),
        precision=lax.Precision.HIGHEST,
    )
    summed_left, summed_right, summed_out, summed_gate = lax.psum(
        (grad_left, extra, grad_out, grad_gate), ("row", "col")
    )
    return (new_update, summed_left, summed_right, summed_out, summed_gate)


F32 = jnp.float32
BF16 = jnp.bfloat16
MESH = pl.DeviceIdType.MESH
NT = (((1,), (1,)), ((), ()))
TN = (((0,), (0,)), ((), ()))
NN = (((1,), (0,)), ((), ()))


def mm(a, b, dims=NN):
    return lax.dot_general(a, b, dims, preferred_element_type=F32)


def send(src, dst, send_sem, recv_sem, target):
    copy = pltpu.make_async_remote_copy(
        src_ref=src, dst_ref=dst, send_sem=send_sem, recv_sem=recv_sem,
        device_id={"row": target}, device_id_type=MESH,
    )
    copy.start()
    return copy


FAR_FIRST = (6, 7, 4, 5, 2, 3, 1)
NEAR_FIRST = (1, 2, 3, 4, 5, 6, 7)


def other_chip(chip, n):
    z_at, x_at = lax.div(chip, 2), lax.rem(chip, 2)
    z_to = (z_at, z_at + 1 - 2 * lax.rem(z_at, 2), lax.rem(z_at + 2, 4), 3 - z_at)[n // 2]
    return z_to * 2 + (1 - x_at if n % 2 else x_at)


def gather_start(buf, me, core, chip, send_sem, recv_sem):
    block = buf.at[me]
    return {
        n: send(
            block, block, send_sem.at[n], recv_sem.at[n], other_chip(chip, n) * 2 + 1 - core
        )
        for n in FAR_FIRST + (0,)
    }


def gather_finish(copies, buf, core, chip, chips, send_sem, recv_sem, use):
    partner = chip * 2 + 1 - core
    passed = []
    for n in NEAR_FIRST:
        copies[n].wait_recv()
        source = other_chip(chip, n) * 2 + 1 - core
        block = buf.at[source]
        at = chips + n
        passed.append(send(block, block, send_sem.at[at], recv_sem.at[at], partner))
        use(source)
    copies[0].wait_recv()
    use(partner)
    for n, copy in zip(NEAR_FIRST, passed):
        copy.wait_recv()
        use(other_chip(chip, n) * 2 + core)
    return list(copies.values()) + passed


def fused_kernel(
    seq_ref, res_ref, *inputs_and_rest,
):
    hbm, rest = inputs_and_rest[:10], inputs_and_rest[10:]
    outs_and_scratch, vmem, load_sem = rest[:-11], rest[-11:-1], rest[-1]
    loads = [
        pltpu.make_async_copy(src, dst, load_sem.at[n])
        for n, (src, dst) in enumerate(zip(hbm, vmem))
    ]
    for n in (0, 1, 5, 7, 2, 3, 8, 4, 6, 9):
        loads[n].start()
    fused_body(loads, seq_ref, res_ref, *vmem, *outs_and_scratch)


def fused_body(
    loads, seq_ref, res_ref, align_ref, gain_ref, pair_ref, gm_ref, w_ref, resrow_ref, wl_ref,
    wr_ref, cot_ref, bias_ref,
    upd_ref, gl_ref, gr_ref, go_ref, gg_ref,
    gt_s, gs_s, ps_s, feat, near, gate_s, w2_s, w32_s, wr32_s, own_s, rin_s, rt_s, fr_s, lt_s, m_s, g_s, pre_s, n2_s,
    gr2_s, sb_s, rb_s, sm_s, rm_s, pk_s, pr_s,
    send_r, recv_r, send_n, recv_n, send_f, recv_f, send_x, recv_x, send_b, recv_b, send_m, recv_m,
    send_g, recv_g, send_h, recv_h, send_p, recv_p,
):
    me = lax.axis_index("row")
    core = lax.rem(me, 2)
    chip = lax.div(me, 2)
    x_at = lax.rem(chip, 2)
    z_at = lax.div(chip, 2)
    half = 1 - core
    _, chips, residues, lanes = feat.shape
    devices = 2 * chips
    planes = chips // 2
    s_loc, ch, _ = align_ref.shape
    rows, _, pc = pair_ref.shape
    width = wl_ref.shape[0]
    seqs = s_loc * devices
    partner = chip * 2 + 1 - core
    across = (z_at * 2 + 1 - x_at) * 2 + core
    wide = width // 2
    mine_wide = rows * seqs

    barrier = pltpu.get_barrier_semaphore()
    for k in range(1, devices):
        pl.semaphore_signal(
            barrier, inc=1, device_id={"row": lax.rem(me + k, devices)}, device_id_type=MESH
        )

    for n in (0, 1, 5, 7):
        loads[n].wait()
    parts = []
    for s in range(s_loc):
        value = align_ref[s].astype(F32)
        centred = value - jnp.mean(value, axis=0, keepdims=True)
        variance = jnp.mean(centred * centred, axis=0, keepdims=True)
        parts.append(centred * lax.rsqrt(variance + 1e-05))
    gain = jnp.concatenate([gain_ref[...]] * s_loc, axis=1)
    own = (jnp.transpose(jnp.concatenate(parts, axis=0)) * gain).astype(BF16)
    feat[core, x_at * planes + z_at] = own

    resrow = resrow_ref[...].astype(F32)
    wr32_s[...] = jnp.concatenate([wr_ref[...].astype(F32)] * s_loc, axis=1)
    lane_s = lax.div(lax.broadcasted_iota(jnp.int32, (wide, lanes), 1), ch)
    wr_parts = []
    for h in range(2):
        block = jnp.concatenate(
            [wr32_s[pl.ds(2 * h + t, chips, stride=4), :] for t in range(2)], axis=0
        )
        for s in range(s_loc):
            wr_parts.append(jnp.where(lane_s == s, block, 0.0))
    right = mm(jnp.concatenate(wr_parts, axis=0).astype(BF16), own, NT)
    flags = [seq_ref[me * s_loc + s].astype(F32) * resrow for s in range(s_loc)]
    for h in range(2):
        for s in range(s_loc):
            at = (h * s_loc + s) * wide
            own_s[h, s * wide : (s + 1) * wide, :] = (
                right[at : at + wide] * flags[s]
            ).astype(BF16)
    rin_s[half, me] = own_s[half]
    pl.semaphore_wait(barrier, devices - 1)

    rights = []
    nears = []
    mine_at = feat.at[core, x_at * planes + z_at]
    for n in FAR_FIRST + (0,):
        to = other_chip(chip, n)
        window = pl.ds(pl.multiple_of(to * 2 * rows, 2 * rows), 2 * rows)
        nears.append(
            send(
                mine_at.at[window], near.at[core, chip], send_n.at[n], recv_n.at[n],
                to * 2 + 1 - core,
            )
        )
    for n in FAR_FIRST + (0,):
        to = other_chip(chip, n)
        if n > 0:
            at = 2 * n + 1
            rights.append(
                send(
                    own_s.at[half], rin_s.at[half, me], send_r.at[at], recv_r.at[at],
                    to * 2 + core,
                )
            )
        at = 2 * n
        rights.append(
            send(
                own_s.at[core], rin_s.at[core, me], send_r.at[at], recv_r.at[at],
                to * 2 + 1 - core,
            )
        )
    column = []
    for k in range(1, planes):
        to = (lax.rem(z_at + k, planes) * 2 + x_at) * 2 + core
        column.append(send(mine_at, mine_at, send_f.at[k], recv_f.at[k], to))
    sideways = [send(mine_at, mine_at, send_f.at[0], recv_f.at[0], across)]

    for n in (2, 3, 4, 6, 8, 9):
        loads[n].wait()
    gm = gm_ref[...]
    rescol = jnp.transpose(jnp.broadcast_to(resrow, (pc, residues)))
    seq = [seq_ref[s].astype(F32) for s in range(seqs)]
    both_rows = [res_ref[chip * 2 * rows + i].astype(F32) for i in range(2 * rows)]
    mine = [res_ref[me * rows + i].astype(F32) for i in range(rows)]
    row_total = seq[0]
    for s in range(1, seqs):
        row_total = row_total + seq[s]
    present = 1.0 / jnp.maximum(row_total * rescol, 1.0)
    inverse = [present * mine[i] + (1.0 - mine[i]) for i in range(rows)]
    for i in range(rows):
        gate = jax.nn.sigmoid(mm(pair_ref[i], gm))
        gate_s[i] = gate
        g_s[core, :, i * pc : (i + 1) * pc] = (
            cot_ref[i].astype(F32) * (gate * inverse[i])
        ).astype(BF16)
    crossing = send(g_s.at[core], g_s.at[core], send_x, recv_x, partner)

    w32_s[...] = w_ref[...].astype(F32)
    for h in range(2):
        for t in range(2):
            for k in range(chips):
                e, q = 4 * k + 2 * h + t, t * chips + k
                w2_s[h, :, q * pc : (q + 1) * pc] = w32_s[
                    pl.ds(e, width, stride=width), :
                ].astype(BF16)
    lane = lax.broadcasted_iota(jnp.int32, (1, 2 * mine_wide), 1)
    maskrow = jnp.zeros((1, 2 * mine_wide), F32)
    for s in range(s_loc):
        for d in range(devices):
            maskrow = jnp.where(lax.rem(lane, seqs) == s * devices + d, seq[d * s_loc + s], maskrow)
    resl = jnp.zeros((1, 2 * mine_wide), F32)
    for i in range(2 * rows):
        resl = jnp.where(lax.div(lane, seqs) == i, both_rows[i], resl)
    maskrow = maskrow * resl
    wlt = wl_ref[...].astype(F32)
    wlt2 = jnp.concatenate([wlt] * s_loc, axis=1).astype(BF16)

    for copy in nears:
        copy.wait_recv()
    near_pass = send(near.at[half], near.at[half], send_n.at[chips], recv_n.at[chips], partner)
    near_pass.wait_recv()
    for d in range(devices):
        fr_s[d * 2 * rows : (d + 1) * 2 * rows, :] = near[d % 2, d // 2].astype(F32)
    lane_d = lax.div(lax.broadcasted_iota(jnp.int32, (devices, lanes), 1), ch)
    pieces = []
    for i in range(2 * rows):
        block = fr_s[pl.ds(i, devices, stride=2 * rows), :]
        for s in range(s_loc):
            pieces.append(jnp.where(lane_d == s, block, 0.0))
    fr = jnp.concatenate(pieces, axis=0).astype(BF16)
    left_t = mm(wlt2, fr, NT) * maskrow
    for c in range(2):
        lt_s[c] = left_t[:, c * mine_wide : (c + 1) * mine_wide]
    left_t = left_t.astype(BF16)

    left = jnp.transpose(lt_s[core]).astype(BF16)
    for h in range(2):
        for e in range(0, wide, 2):
            part = mm(left, w2_s[h, :, e * pc : (e + 2) * pc]).astype(BF16)
            for n in range(2):
                at = (h * wide + e + n) * seqs
                for i in range(rows):
                    m_s[at : at + seqs, i * pc : (i + 1) * pc] = part[
                        i * seqs : (i + 1) * seqs, n * pc : (n + 1) * pc
                    ]

    def lay_out(h):
        for d in range(devices):
            for s in range(s_loc):
                rt_s[h, pl.ds(s * devices + d, wide, stride=seqs), :] = rin_s[
                    h, d, s * wide : (s + 1) * wide, :
                ].astype(F32)

    crossing.wait_recv()
    for copy in rights:
        copy.wait_recv()
    right_pass = send(
        rin_s.at[half], rin_s.at[half], send_r.at[1], recv_r.at[1], partner
    )
    lay_out(half)
    rtt = rt_s[half].astype(BF16)
    step = 4
    for e in range(0, wide, step):
        for c in range(2):
            part = mm(rtt[e * seqs : (e + step) * seqs], g_s[c]).astype(BF16)
            for h in range(step):
                for i in range(rows):
                    at = (c * rows + i) * seqs
                    n2_s[at : at + seqs, (e + h) * pc : (e + h + 1) * pc] = part[
                        h * seqs : (h + 1) * seqs, i * pc : (i + 1) * pc
                    ]
    go = mm(left_t, n2_s[...])
    for k in range(chips):
        for t in range(2):
            q = t * chips + k
            sb_s[k, t * width : (t + 1) * width, :] = go[:, q * pc : (q + 1) * pc].astype(BF16)
    scatter = {}
    for n in FAR_FIRST + (0,):
        to = other_chip(chip, n)
        scatter[n] = send(sb_s.at[to], rb_s.at[n], send_b.at[n], recv_b.at[n], to * 2 + 1 - core)

    for k in range(1, planes):
        column[k - 1].wait_recv()
        block = feat.at[core, x_at * planes + lax.rem(z_at - k + planes, planes)]
        at = planes + k
        sideways.append(send(block, block, send_f.at[at], recv_f.at[at], across))
    block = feat.at[core, pl.ds(x_at * planes, planes)]
    feat_pass = [send(block, block, send_f.at[planes], recv_f.at[planes], partner)]

    right_pass.wait_recv()
    lay_out(core)
    rt = jnp.transpose(rt_s[...].reshape(width * seqs, residues)).astype(BF16)

    bias = bias_ref[...]
    for i in range(0, rows, 2):
        lin2 = mm(rt, m_s[:, i * pc : (i + 2) * pc])
        for h in range(2):
            linear = lin2[:, h * pc : (h + 1) * pc] + bias
            gate = gate_s[i + h]
            scaled = gate * inverse[i + h]
            upd_ref[i + h] = (scaled * linear).astype(BF16)
            pre_s[(i + h) * residues : (i + h + 1) * residues, :] = (
                cot_ref[i + h].astype(F32) * scaled * linear * (1.0 - gate)
            ).astype(BF16)
    gg = mm(pair_ref[...].reshape(rows * residues, pc), pre_s[...], TN)
    g_rows = pc // chips
    sm_s[...] = gg.reshape(chips, g_rows, pc).astype(BF16)

    def portion(k):
        to = lax.rem(chip + k, chips)
        return pltpu.make_async_remote_copy(
            src_ref=sm_s.at[to], dst_ref=rm_s.at[2 * k + core], send_sem=send_m.at[k],
            recv_sem=recv_m.at[2 * k + core], device_id={"row": to * 2 + 1}, device_id_type=MESH,
        )

    def arrived(k, c):
        return pltpu.make_async_remote_copy(
            src_ref=sm_s.at[0], dst_ref=rm_s.at[2 * k + c], send_sem=send_m.at[k],
            recv_sem=recv_m.at[2 * k + c], device_id={"row": partner}, device_id_type=MESH,
        )

    @pl.when(core == 0)
    def _():
        portion(0).start()

    for k in range(1, chips):
        portion(k).start()

    act = mm(w2_s[half], n2_s[...], NT) * maskrow
    gl2 = mm(act.astype(BF16), fr)
    gl = gl2[:, :ch]
    for s in range(1, s_loc):
        gl = gl + gl2[:, s * ch : (s + 1) * ch]

    back = mm(m_s[...], g_s[core], NT)
    rt_s[...] = back.reshape(2, wide * seqs, residues)
    for p in range(2):
        for n in range(chips):
            b = p * chips + n
            d = (n % planes) * 4 + (n // planes) * 2 + p
            for s in range(s_loc):
                flag = seq[d * s_loc + s] * resrow
                for h in range(2):
                    at = s * width + h * wide
                    gr2_s[at : at + wide, b * residues : (b + 1) * residues] = (
                        rt_s[h, pl.ds(s * devices + d, wide, stride=seqs), :] * flag
                    )
    scatter[0].wait_recv()
    total = rb_s[0].astype(F32)
    for k in range(1, chips):
        scatter[k].wait_recv()
        total = total + rb_s[k].astype(F32)
    gt_s[me] = total.astype(BF16)
    copies = gather_start(gt_s, me, core, chip, send_g, recv_g)

    for copy in sideways:
        copy.wait_recv()
    block = feat.at[core, pl.ds((1 - x_at) * planes, planes)]
    at = 2 * planes
    feat_pass.append(send(block, block, send_f.at[at], recv_f.at[at], partner))

    for copy in feat_pass:
        copy.wait_recv()
    feats = feat[...].reshape(devices * residues, lanes)
    gr2 = mm(gr2_s[...].astype(BF16), feats)
    gr = gr2[:width, :ch]
    for s in range(1, s_loc):
        gr = gr + gr2[s * width : (s + 1) * width, s * ch : (s + 1) * ch]

    pk_s[0] = jnp.concatenate([gl[:wide], gl[wide:]], axis=1)
    pk_s[1] = jnp.concatenate([gr[:wide], gr[wide:]], axis=1)
    twin = send(pk_s.at[half], pr_s, send_p.at[1], recv_p.at[1], partner)

    twin.wait_recv()
    ps_s[me] = (pk_s[core] + pr_s[...]).astype(BF16)
    last = []
    block = ps_s.at[me]
    for n in FAR_FIRST + (0,):
        to = other_chip(chip, n) * 2
        if n > 0:
            at = 2 * n + 1
            last.append(send(block, block, send_p.at[at], recv_p.at[at], to + core))
        at = 2 * n
        last.append(send(block, block, send_p.at[at], recv_p.at[at], to + 1 - core))

    def spread(k, c):
        block = gs_s.at[chip]
        return pltpu.make_async_remote_copy(
            src_ref=block, dst_ref=block, send_sem=send_h.at[2 * k + c], recv_sem=recv_h.at[k],
            device_id={"row": lax.rem(chip + k, chips) * 2 + c}, device_id_type=MESH,
        )

    def landed(k):
        block = gs_s.at[lax.rem(chip - k + chips, chips)]
        return pltpu.make_async_remote_copy(
            src_ref=block, dst_ref=block, send_sem=send_h.at[2 * k], recv_sem=recv_h.at[k],
            device_id={"row": partner}, device_id_type=MESH,
        )

    @pl.when(core == 1)
    def _():
        total = sm_s[chip].astype(F32)
        arrived(0, 0).wait_recv()
        total = total + rm_s[0].astype(F32)
        for k in range(1, chips):
            for c in range(2):
                arrived(k, c).wait_recv()
                total = total + rm_s[2 * k + c].astype(F32)
        gs_s[chip] = total.astype(BF16)
        spread(0, 0).start()
        for k in range(1, chips):
            for c in range(2):
                spread(k, c).start()

    def place(d):
        for t in range(2):
            go_ref[pl.ds(2 * d + t, width, stride=width), :] = gt_s[
                d, t * width : (t + 1) * width, :
            ].astype(F32)

    place(me)
    done2 = gather_finish(copies, gt_s, core, chip, chips, send_g, recv_g, place)
    for copy in last:
        copy.wait_recv()

    @pl.when(core == 0)
    def _():
        landed(0).wait_recv()
        portion(0).wait_send()

    for k in range(1, chips):
        landed(k).wait_recv()
        portion(k).wait_send()

    @pl.when(core == 1)
    def _():
        spread(0, 0).wait_send()
        for k in range(1, chips):
            for c in range(2):
                spread(k, c).wait_send()

    for k in range(chips):
        gg_ref[k * g_rows : (k + 1) * g_rows, :] = gs_s[k].astype(F32)
    gl, gr = ps_s[0].astype(F32), ps_s[1].astype(F32)
    for d in range(2, devices, 2):
        gl = gl + ps_s[d].astype(F32)
        gr = gr + ps_s[d + 1].astype(F32)
    for h in range(2):
        gl_ref[h * wide : (h + 1) * wide, :] = gl[:, h * ch : (h + 1) * ch]
        for t in range(2):
            gr_ref[pl.ds(2 * h + t, chips, stride=4), :] = gr[
                t * chips : (t + 1) * chips, h * ch : (h + 1) * ch
            ]
    for copy in (
        nears + [near_pass] + rights + [right_pass] + column + sideways + feat_pass + [crossing]
        + list(scatter.values()) + [twin] + done2 + last
    ):
        copy.wait_send()


def store_kernel(*refs):
    copies = [
        pltpu.make_async_copy(refs[n], refs[5 + n], refs[10].at[n]) for n in (3, 0, 4, 1, 2)
    ]
    for copy in copies:
        copy.start()
    for copy in copies:
        copy.wait()


def fused_device(
    alignment_state, pair_state, cotangent, sequence_row_mask, residue_mask, norm_gain_vector,
    left_matrix_weight, right_matrix_weight, output_weight, output_bias, gate_matrix,
):
    s_loc, residues, ch = alignment_state.shape
    rows, _, pc = pair_state.shape
    width = left_matrix_weight.shape[1]
    devices = lax.axis_size("row")
    seqs = s_loc * devices
    chips = devices // 2
    lanes = s_loc * ch
    top = (width // devices) * width
    smem = pl.BlockSpec(memory_space=pltpu.SMEM)
    vmem = pl.BlockSpec(memory_space=pltpu.VMEM)
    dma = pltpu.SemaphoreType.DMA
    inputs = (
        alignment_state.transpose(0, 2, 1),
        norm_gain_vector.reshape(1, ch),
        pair_state,
        gate_matrix,
        output_weight,
        residue_mask.reshape(1, residues),
        left_matrix_weight.T,
        right_matrix_weight.T,
        cotangent,
        output_bias.reshape(1, pc),
    )
    results = pl.pallas_call(
        fused_kernel,
        name="fused",
        out_shape=(
            pltpu.VMEM((rows, residues, pc), BF16),
            pltpu.VMEM((width, ch), F32),
            pltpu.VMEM((width, ch), F32),
            pltpu.VMEM((width * width, pc), F32),
            pltpu.VMEM((pc, pc), F32),
        ),
        in_specs=[smem, smem] + [pl.BlockSpec(memory_space=pltpu.HBM)] * 10,
        out_specs=(vmem,) * 5,
        scratch_shapes=[
            pltpu.VMEM((devices, top, pc), BF16),
            pltpu.VMEM((chips, pc // chips, pc), BF16),
            pltpu.VMEM((devices, width // 2, 2 * ch), BF16),
            pltpu.VMEM((2, chips, residues, lanes), BF16),
            pltpu.VMEM((2, chips, 2 * rows, lanes), BF16),
            pltpu.VMEM((rows, residues, pc), F32),
            pltpu.VMEM((2, width, width // 2 * pc), BF16),
            pltpu.VMEM((width * width, pc), F32),
            pltpu.VMEM((width, lanes), F32),
            pltpu.VMEM((2, s_loc * width // 2, residues), BF16),
            pltpu.VMEM((2, devices, s_loc * width // 2, residues), BF16),
            pltpu.VMEM((2, width // 2 * seqs, residues), F32),
            pltpu.VMEM((devices * 2 * rows, lanes), F32),
            pltpu.VMEM((2, width, rows * seqs), F32),
            pltpu.VMEM((width * seqs, rows * pc), BF16),
            pltpu.VMEM((2, residues, rows * pc), BF16),
            pltpu.VMEM((rows * residues, pc), BF16),
            pltpu.VMEM((2 * rows * seqs, width // 2 * pc), BF16),
            pltpu.VMEM((s_loc * width, devices * residues), F32),
            pltpu.VMEM((chips, top, pc), BF16),
            pltpu.VMEM((chips, top, pc), BF16),
            pltpu.VMEM((chips, pc // chips, pc), BF16),
            pltpu.VMEM((devices, pc // chips, pc), BF16),
            pltpu.VMEM((2, width // 2, 2 * ch), F32),
            pltpu.VMEM((width // 2, 2 * ch), F32),
            dma((devices,)),
            dma((devices,)),
            dma((chips + 1,)),
            dma((chips + 1,)),
            dma((chips + 1,)),
            dma((chips + 1,)),
            dma,
            dma,
            dma((chips,)),
            dma((chips,)),
            dma((chips,)),
            dma((devices,)),
            dma((2 * chips,)),
            dma((2 * chips,)),
            dma((devices,)),
            dma((chips,)),
            dma((devices,)),
            dma((devices,)),
        ]
        + [pltpu.VMEM(value.shape, value.dtype) for value in inputs]
        + [dma((len(inputs),))],
        compiler_params=pltpu.CompilerParams(
            collective_id=0, has_side_effects=True, vmem_limit_bytes=61 * 1024 * 1024
        ),
    )(sequence_row_mask, residue_mask, *inputs)
    update, left_t, right_t, grad_out, grad_gate = pl.pallas_call(
        store_kernel,
        name="store",
        out_shape=(
            jax.ShapeDtypeStruct((rows, residues, pc), BF16),
            jax.ShapeDtypeStruct((width, ch), F32),
            jax.ShapeDtypeStruct((width, ch), F32),
            jax.ShapeDtypeStruct((width * width, pc), F32),
            jax.ShapeDtypeStruct((pc, pc), F32),
        ),
        in_specs=[vmem] * 5,
        out_specs=(pl.BlockSpec(memory_space=pltpu.HBM),) * 5,
        scratch_shapes=[dma((5,))],
        compiler_params=pltpu.CompilerParams(vmem_limit_bytes=32 * 1024 * 1024),
    )(*results)
    return update, left_t.T, right_t.T, grad_out, grad_gate


def per_device(*arrays):
    alignment_state, pair_state = arrays[0], arrays[1]
    s_loc, residues, ch = alignment_state.shape
    rows, _, pc = pair_state.shape
    width = arrays[6].shape[1]
    devices = lax.axis_size("row")
    fits = (
        lax.axis_size("col") == 1
        and devices % 2 == 0
        and (s_loc * ch, pc, residues) == (128, 128, 128)
        and rows == 8
        and width % devices == 0
        and pc == devices * 8
        and s_loc * devices == 32
    )
    return fused_device(*arrays) if fits else general_device(*arrays)


def solution(mesh):
    return jax.shard_map(
        per_device,
        mesh=mesh,
        in_specs=(
            P(("grp", "row"), "col", None),
            P(("grp", "row"), "col", None),
            P(("grp", "row"), "col", None),
            P("grp"),
            P("grp"),
            P(),
            P(),
            P(),
            P(),
            P(),
            P(),
        ),
        out_specs=(
            P(("grp", "row"), "col", None),
            P("grp", None),
            P("grp", None),
            P("grp", None),
            P("grp", None),
        ),
        check_vma=False,
    )
```

```python
import jax
import jax.numpy as jnp
from jax import lax
from jax.experimental import pallas as pl
from jax.experimental.pallas import tpu as pltpu
from jax.sharding import PartitionSpec as P


def layer_normalize(alignment_state, norm_gain_vector):
    value_entries = alignment_state.astype(jnp.float32)
    average = jnp.mean(value_entries, axis=-1, keepdims=True)
    centred = value_entries - average
    variance = jnp.mean(centred * centred, axis=-1, keepdims=True)
    return (centred * lax.rsqrt(variance + 1e-05) * norm_gain_vector).astype(jnp.bfloat16)


def general_device(
    alignment_state,
    pair_state,
    cotangent,
    sequence_row_mask,
    residue_mask,
    norm_gain_vector,
    left_matrix_weight,
    right_matrix_weight,
    output_weight,
    output_bias,
    gate_matrix,
):
    sequence_resident, column_count, alignment_channel_count = alignment_state.shape
    count_of_rows = pair_state.shape[0]
    pair_chans = pair_state.shape[2]
    projection_width = left_matrix_weight.shape[1]
    every_sequence = sequence_row_mask.shape[0]
    row_at = lax.axis_index("row")
    col_at = lax.axis_index("col")
    number_of_rows = lax.axis_size("row")
    contract_first = (((0,), (0,)), ((), ()))
    contract_second = (((1,), (1,)), ((), ()))
    resident_features = layer_normalize(alignment_state, norm_gain_vector)
    seq_flags = sequence_row_mask.astype(jnp.float32)
    res_flags = residue_mask.astype(jnp.float32)
    my_cols = lax.dynamic_slice_in_dim(res_flags, col_at * column_count, column_count, 0)
    my_rows = lax.dynamic_slice_in_dim(res_flags, row_at * count_of_rows, count_of_rows, 0)
    panel_mask = seq_flags[:, None] * my_rows[None, :]
    column_mask = seq_flags[:, None] * my_cols[None, :]
    broadcast_features = lax.all_gather(
        resident_features.reshape(sequence_resident, column_count * alignment_channel_count),
        "col",
        axis=1,
        tiled=True,
    )
    row_portions = broadcast_features.reshape(
        sequence_resident, number_of_rows, count_of_rows * alignment_channel_count
    )
    row_feats = lax.all_to_all(
        row_portions, "row", split_axis=1, concat_axis=0, tiled=True
    ).reshape(every_sequence * count_of_rows, alignment_channel_count)
    left_panel = (
        jnp.dot(row_feats, left_matrix_weight, preferred_element_type=jnp.float32).reshape(
            every_sequence, count_of_rows, projection_width
        )
        * panel_mask[:, :, None]
    ).astype(jnp.bfloat16)
    left_matrix = left_panel.transpose(1, 2, 0).reshape(
        count_of_rows * projection_width, every_sequence
    )
    column_features = lax.all_gather(
        resident_features.reshape(sequence_resident, column_count * alignment_channel_count),
        "row",
        axis=0,
        tiled=True,
    ).reshape(every_sequence, column_count, alignment_channel_count)
    right_panel = (
        jnp.dot(
            column_features.reshape(every_sequence * column_count, alignment_channel_count),
            right_matrix_weight,
            preferred_element_type=jnp.float32,
        ).reshape(every_sequence, column_count, projection_width)
        * column_mask[:, :, None]
    ).astype(jnp.bfloat16)
    surplus_offset = jnp.zeros((alignment_channel_count, projection_width), jnp.float32)

    def absorb(extra, first_col, width_columns, right_part):
        feat_blk = (
            lax.dynamic_slice_in_dim(column_features, first_col, width_columns, 1)
            .reshape(every_sequence * width_columns, alignment_channel_count)
            .astype(jnp.float32)
        )
        mask_blk = lax.dynamic_slice_in_dim(column_mask, first_col, width_columns, 1)
        masked_part = (
            right_part.reshape(every_sequence, width_columns, projection_width)
            * mask_blk[:, :, None]
        ).reshape(every_sequence * width_columns, projection_width)
        return extra + jnp.dot(feat_blk.T, masked_part, precision=lax.Precision.HIGHEST)

    right_flat = right_panel.reshape(every_sequence, column_count * projection_width)
    row_total = jnp.sum(seq_flags)
    col_block = 128
    n_blocks = column_count // col_block

    def one_block(block_idx, carry):
        new_update, grad_out, grad_gate, left_acc, extra = carry
        first_col = block_idx * col_block
        right_blk = lax.dynamic_slice_in_dim(
            right_flat, first_col * projection_width, col_block * projection_width, 1
        )
        outer_prod = jnp.dot(left_matrix, right_blk, preferred_element_type=jnp.float32)
        outer_prod = outer_prod.reshape(
            count_of_rows, projection_width, col_block, projection_width
        ).transpose(0, 2, 1, 3)
        outer_prod = outer_prod.reshape(
            count_of_rows * col_block, projection_width * projection_width
        ).astype(jnp.bfloat16)
        linear = (
            jnp.dot(outer_prod, output_weight, preferred_element_type=jnp.float32) + output_bias
        )
        pair_blk = lax.dynamic_slice_in_dim(pair_state, first_col, col_block, 1).reshape(
            count_of_rows * col_block, pair_chans
        )
        gate_val = jax.nn.sigmoid(
            jnp.dot(pair_blk, gate_matrix, preferred_element_type=jnp.float32)
        )
        blk_flags = lax.dynamic_slice_in_dim(my_cols, first_col, col_block, 0)
        divisor = jnp.maximum(row_total * my_rows[:, None] * blk_flags[None, :], 1.0).reshape(
            count_of_rows * col_block, 1
        )
        cot_blk = (
            lax.dynamic_slice_in_dim(cotangent, first_col, col_block, 1)
            .reshape(count_of_rows * col_block, pair_chans)
            .astype(jnp.float32)
        )
        new_pair = (gate_val * linear / divisor).astype(jnp.bfloat16)
        new_update = lax.dynamic_update_slice_in_dim(
            new_update, new_pair.reshape(count_of_rows, col_block, pair_chans), first_col, 1
        )
        grad_lin = (cot_blk * gate_val / divisor).astype(jnp.bfloat16)
        grad_pre = (cot_blk * linear / divisor * gate_val * (1.0 - gate_val)).astype(jnp.bfloat16)
        grad_out = grad_out + lax.dot_general(
            outer_prod, grad_lin, contract_first, preferred_element_type=jnp.float32
        )
        grad_gate = grad_gate + lax.dot_general(
            pair_blk, grad_pre, contract_first, preferred_element_type=jnp.float32
        )
        grad_outer = lax.dot_general(
            grad_lin, output_weight, contract_second, preferred_element_type=jnp.float32
        ).astype(jnp.bfloat16)
        outer_turned = (
            grad_outer.reshape(count_of_rows, col_block, projection_width, projection_width)
            .transpose(0, 2, 1, 3)
            .reshape(count_of_rows * projection_width, col_block * projection_width)
        )
        left_acc = left_acc + lax.dot_general(
            outer_turned, right_blk, contract_second, preferred_element_type=jnp.float32
        )
        right_part = lax.dot_general(
            left_matrix, outer_turned, contract_first, preferred_element_type=jnp.float32
        )
        extra = absorb(extra, first_col, col_block, right_part)
        return (new_update, grad_out, grad_gate, left_acc, extra)

    start_carry = (
        jnp.zeros((count_of_rows, column_count, pair_chans), jnp.bfloat16),
        jnp.zeros((projection_width * projection_width, pair_chans), jnp.float32),
        jnp.zeros((pair_chans, pair_chans), jnp.float32),
        jnp.zeros((count_of_rows * projection_width, every_sequence), jnp.float32),
        surplus_offset,
    )
    new_update, grad_out, grad_gate, left_acc, extra = lax.fori_loop(
        0, n_blocks, one_block, start_carry
    )
    grad_left_act = (
        left_acc.reshape(count_of_rows, projection_width, every_sequence).transpose(2, 0, 1)
        * panel_mask[:, :, None]
    )
    grad_left = jnp.dot(
        row_feats.astype(jnp.float32).T,
        grad_left_act.reshape(every_sequence * count_of_rows, projection_width),
        precision=lax.Precision.HIGHEST,
    )
    summed_left, summed_right, summed_out, summed_gate = lax.psum(
        (grad_left, extra, grad_out, grad_gate), ("row", "col")
    )
    return (new_update, summed_left, summed_right, summed_out, summed_gate)


F32 = jnp.float32
BF16 = jnp.bfloat16
MESH = pl.DeviceIdType.MESH
NT = (((1,), (1,)), ((), ()))
TN = (((0,), (0,)), ((), ()))
NN = (((1,), (0,)), ((), ()))


def mm(a, b, dims=NN):
    return lax.dot_general(a, b, dims, preferred_element_type=F32)


def send(src, dst, send_sem, recv_sem, target):
    copy = pltpu.make_async_remote_copy(
        src_ref=src, dst_ref=dst, send_sem=send_sem, recv_sem=recv_sem,
        device_id={"row": target}, device_id_type=MESH,
    )
    copy.start()
    return copy


FAR_FIRST = (6, 7, 4, 5, 2, 3, 1)
NEAR_FIRST = (1, 2, 3, 4, 5, 6, 7)


def other_chip(chip, n):
    z_at, x_at = lax.div(chip, 2), lax.rem(chip, 2)
    z_to = (z_at, z_at + 1 - 2 * lax.rem(z_at, 2), lax.rem(z_at + 2, 4), 3 - z_at)[n // 2]
    return z_to * 2 + (1 - x_at if n % 2 else x_at)


def gather_start(buf, me, core, chip, send_sem, recv_sem):
    block = buf.at[me]
    return {
        n: send(
            block, block, send_sem.at[n], recv_sem.at[n], other_chip(chip, n) * 2 + 1 - core
        )
        for n in FAR_FIRST + (0,)
    }


def gather_finish(copies, buf, core, chip, chips, send_sem, recv_sem, use):
    partner = chip * 2 + 1 - core
    passed = []
    for n in NEAR_FIRST:
        copies[n].wait_recv()
        source = other_chip(chip, n) * 2 + 1 - core
        block = buf.at[source]
        at = chips + n
        passed.append(send(block, block, send_sem.at[at], recv_sem.at[at], partner))
        use(source)
    copies[0].wait_recv()
    use(partner)
    for n, copy in zip(NEAR_FIRST, passed):
        copy.wait_recv()
        use(other_chip(chip, n) * 2 + core)
    return list(copies.values()) + passed


def fused_kernel(
    seq_ref, res_ref, *inputs_and_rest,
):
    hbm, rest = inputs_and_rest[:10], inputs_and_rest[10:]
    outs_and_scratch, vmem, load_sem = rest[:-11], rest[-11:-1], rest[-1]
    loads = [
        pltpu.make_async_copy(src, dst, load_sem.at[n])
        for n, (src, dst) in enumerate(zip(hbm, vmem))
    ]
    for n in (0, 1, 5, 7, 2, 3, 8, 4, 6, 9):
        loads[n].start()
    fused_body(loads, seq_ref, res_ref, *vmem, *outs_and_scratch)


def fused_body(
    loads, seq_ref, res_ref, align_ref, gain_ref, pair_ref, gm_ref, w_ref, resrow_ref, wl_ref,
    wr_ref, cot_ref, bias_ref,
    upd_ref, gl_ref, gr_ref, go_ref, gg_ref,
    gt_s, gs_s, ps_s, feat, near, gate_s, w2_s, w32_s, wr32_s, own_s, rin_s, rt_s, fr_s, lt_s, m_s, g_s, pre_s, n2_s,
    gr2_s, sb_s, rb_s, sm_s, rm_s, pk_s, pr_s,
    send_r, recv_r, send_n, recv_n, send_f, recv_f, send_x, recv_x, send_b, recv_b, send_m, recv_m,
    send_g, recv_g, send_h, recv_h, send_p, recv_p,
):
    me = lax.axis_index("row")
    core = lax.rem(me, 2)
    chip = lax.div(me, 2)
    x_at = lax.rem(chip, 2)
    z_at = lax.div(chip, 2)
    half = 1 - core
    _, chips, residues, lanes = feat.shape
    devices = 2 * chips
    planes = chips // 2
    s_loc, ch, _ = align_ref.shape
    rows, _, pc = pair_ref.shape
    width = wl_ref.shape[0]
    seqs = s_loc * devices
    partner = chip * 2 + 1 - core
    across = (z_at * 2 + 1 - x_at) * 2 + core
    wide = width // 2
    mine_wide = rows * seqs

    barrier = pltpu.get_barrier_semaphore()
    for k in range(1, devices):
        pl.semaphore_signal(
            barrier, inc=1, device_id={"row": lax.rem(me + k, devices)}, device_id_type=MESH
        )

    for n in (0, 1, 5, 7):
        loads[n].wait()
    parts = []
    for s in range(s_loc):
        value = align_ref[s].astype(F32)
        centred = value - jnp.mean(value, axis=0, keepdims=True)
        variance = jnp.mean(centred * centred, axis=0, keepdims=True)
        parts.append(centred * lax.rsqrt(variance + 1e-05))
    gain = jnp.concatenate([gain_ref[...]] * s_loc, axis=1)
    own = (jnp.transpose(jnp.concatenate(parts, axis=0)) * gain).astype(BF16)
    feat[core, x_at * planes + z_at] = own

    resrow = resrow_ref[...].astype(F32)
    wr32_s[...] = jnp.concatenate([wr_ref[...].astype(F32)] * s_loc, axis=1)
    lane_s = lax.div(lax.broadcasted_iota(jnp.int32, (wide, lanes), 1), ch)
    wr_parts = []
    for h in range(2):
        block = jnp.concatenate(
            [wr32_s[pl.ds(2 * h + t, chips, stride=4), :] for t in range(2)], axis=0
        )
        for s in range(s_loc):
            wr_parts.append(jnp.where(lane_s == s, block, 0.0))
    right = mm(jnp.concatenate(wr_parts, axis=0).astype(BF16), own, NT)
    flags = [seq_ref[me * s_loc + s].astype(F32) * resrow for s in range(s_loc)]
    for h in range(2):
        for s in range(s_loc):
            at = (h * s_loc + s) * wide
            own_s[h, s * wide : (s + 1) * wide, :] = (
                right[at : at + wide] * flags[s]
            ).astype(BF16)
    rin_s[half, me] = own_s[half]
    pl.semaphore_wait(barrier, devices - 1)

    rights = {}
    nears = []
    mine_at = feat.at[core, x_at * planes + z_at]
    for n in FAR_FIRST + (0,):
        to = other_chip(chip, n)
        window = pl.ds(pl.multiple_of(to * 2 * rows, 2 * rows), 2 * rows)
        nears.append(
            send(
                mine_at.at[window], near.at[core, chip], send_n.at[n], recv_n.at[n],
                to * 2 + 1 - core,
            )
        )
    for n in FAR_FIRST + (0,):
        to = other_chip(chip, n)
        if n > 0:
            at = 2 * n + 1
            rights[at] = send(
                own_s.at[half], rin_s.at[half, me], send_r.at[at], recv_r.at[at], to * 2 + core
            )
        at = 2 * n
        rights[at] = send(
            own_s.at[core], rin_s.at[core, me], send_r.at[at], recv_r.at[at], to * 2 + 1 - core
        )
    column = []
    for k in range(1, planes):
        to = (lax.rem(z_at + k, planes) * 2 + x_at) * 2 + core
        column.append(send(mine_at, mine_at, send_f.at[k], recv_f.at[k], to))
    sideways = [send(mine_at, mine_at, send_f.at[0], recv_f.at[0], across)]

    for n in (2, 3, 4, 6, 8, 9):
        loads[n].wait()
    gm = gm_ref[...]
    rescol = jnp.transpose(jnp.broadcast_to(resrow, (pc, residues)))
    seq = [seq_ref[s].astype(F32) for s in range(seqs)]
    both_rows = [res_ref[chip * 2 * rows + i].astype(F32) for i in range(2 * rows)]
    mine = [res_ref[me * rows + i].astype(F32) for i in range(rows)]
    row_total = seq[0]
    for s in range(1, seqs):
        row_total = row_total + seq[s]
    present = 1.0 / jnp.maximum(row_total * rescol, 1.0)
    inverse = [present * mine[i] + (1.0 - mine[i]) for i in range(rows)]
    for i in range(rows):
        gate = jax.nn.sigmoid(mm(pair_ref[i], gm))
        gate_s[i] = gate
        g_s[core, :, i * pc : (i + 1) * pc] = (
            cot_ref[i].astype(F32) * (gate * inverse[i])
        ).astype(BF16)
    crossing = send(g_s.at[core], g_s.at[core], send_x, recv_x, partner)

    w32_s[...] = w_ref[...].astype(F32)
    for h in range(2):
        for t in range(2):
            for k in range(chips):
                e, q = 4 * k + 2 * h + t, t * chips + k
                w2_s[h, :, q * pc : (q + 1) * pc] = w32_s[
                    pl.ds(e, width, stride=width), :
                ].astype(BF16)
    lane = lax.broadcasted_iota(jnp.int32, (1, 2 * mine_wide), 1)
    maskrow = jnp.zeros((1, 2 * mine_wide), F32)
    for s in range(s_loc):
        for d in range(devices):
            maskrow = jnp.where(lax.rem(lane, seqs) == s * devices + d, seq[d * s_loc + s], maskrow)
    resl = jnp.zeros((1, 2 * mine_wide), F32)
    for i in range(2 * rows):
        resl = jnp.where(lax.div(lane, seqs) == i, both_rows[i], resl)
    maskrow = maskrow * resl
    wlt = wl_ref[...].astype(F32)
    wlt2 = jnp.concatenate([wlt] * s_loc, axis=1).astype(BF16)

    for copy in nears:
        copy.wait_recv()
    near_pass = send(near.at[half], near.at[half], send_n.at[chips], recv_n.at[chips], partner)
    near_pass.wait_recv()
    for d in range(devices):
        fr_s[d * 2 * rows : (d + 1) * 2 * rows, :] = near[d % 2, d // 2].astype(F32)
    lane_d = lax.div(lax.broadcasted_iota(jnp.int32, (devices, lanes), 1), ch)
    pieces = []
    for i in range(2 * rows):
        block = fr_s[pl.ds(i, devices, stride=2 * rows), :]
        for s in range(s_loc):
            pieces.append(jnp.where(lane_d == s, block, 0.0))
    fr = jnp.concatenate(pieces, axis=0).astype(BF16)
    left_t = mm(wlt2, fr, NT) * maskrow
    for c in range(2):
        lt_s[c] = left_t[:, c * mine_wide : (c + 1) * mine_wide]
    left_t = left_t.astype(BF16)

    left = jnp.transpose(lt_s[core]).astype(BF16)
    for h in range(2):
        for e in range(0, wide, 2):
            part = mm(left, w2_s[h, :, e * pc : (e + 2) * pc]).astype(BF16)
            for n in range(2):
                at = (h * wide + e + n) * seqs
                for i in range(rows):
                    m_s[at : at + seqs, i * pc : (i + 1) * pc] = part[
                        i * seqs : (i + 1) * seqs, n * pc : (n + 1) * pc
                    ]

    def lay_out(h, d):
        for s in range(s_loc):
            rt_s[h, pl.ds(s * devices + d, wide, stride=seqs), :] = rin_s[
                h, d, s * wide : (s + 1) * wide, :
            ].astype(F32)

    crossing.wait_recv()
    lay_out(half, me)
    for n in (0,) + NEAR_FIRST:
        source = other_chip(chip, n) * 2
        rights[2 * n].wait_recv()
        lay_out(half, source + 1 - core)
        if n > 0:
            rights[2 * n + 1].wait_recv()
            lay_out(half, source + core)
    right_pass = send(
        rin_s.at[half], rin_s.at[half], send_r.at[1], recv_r.at[1], partner
    )
    rtt = rt_s[half].astype(BF16)
    scatter = {}
    group = 4
    for first in range(0, chips, group):
        for t in range(2):
            at = t * chips + first
            for c in range(2):
                part = mm(rtt[at * seqs : (at + group) * seqs], g_s[c]).astype(BF16)
                for h in range(group):
                    for i in range(rows):
                        to = (c * rows + i) * seqs
                        n2_s[to : to + seqs, (at + h) * pc : (at + h + 1) * pc] = part[
                            h * seqs : (h + 1) * seqs, i * pc : (i + 1) * pc
                        ]
        for t in range(2):
            at = t * chips + first
            go = mm(left_t, n2_s[:, at * pc : (at + group) * pc])
            for h in range(group):
                sb_s[first + h, t * width : (t + 1) * width, :] = go[
                    :, h * pc : (h + 1) * pc
                ].astype(BF16)
        for k in range(first, first + group):
            n = lax.rem(k - chip + chips, chips)
            scatter[k] = send(
                sb_s.at[k], rb_s.at[n], send_b.at[n], recv_b.at[n], k * 2 + 1 - core
            )

    for k in range(1, planes):
        column[k - 1].wait_recv()
        block = feat.at[core, x_at * planes + lax.rem(z_at - k + planes, planes)]
        at = planes + k
        sideways.append(send(block, block, send_f.at[at], recv_f.at[at], across))
    block = feat.at[core, pl.ds(x_at * planes, planes)]
    feat_pass = [send(block, block, send_f.at[planes], recv_f.at[planes], partner)]

    right_pass.wait_recv()
    for d in range(devices):
        lay_out(core, d)
    rt = jnp.transpose(rt_s[...].reshape(width * seqs, residues)).astype(BF16)

    bias = bias_ref[...]
    for i in range(0, rows, 2):
        lin2 = mm(rt, m_s[:, i * pc : (i + 2) * pc])
        for h in range(2):
            linear = lin2[:, h * pc : (h + 1) * pc] + bias
            gate = gate_s[i + h]
            scaled = gate * inverse[i + h]
            upd_ref[i + h] = (scaled * linear).astype(BF16)
            pre_s[(i + h) * residues : (i + h + 1) * residues, :] = (
                cot_ref[i + h].astype(F32) * scaled * linear * (1.0 - gate)
            ).astype(BF16)
    gg = mm(pair_ref[...].reshape(rows * residues, pc), pre_s[...], TN)
    g_rows = pc // chips
    sm_s[...] = gg.reshape(chips, g_rows, pc).astype(BF16)

    def portion(k):
        to = lax.rem(chip + k, chips)
        return pltpu.make_async_remote_copy(
            src_ref=sm_s.at[to], dst_ref=rm_s.at[2 * k + core], send_sem=send_m.at[k],
            recv_sem=recv_m.at[2 * k + core], device_id={"row": to * 2 + 1}, device_id_type=MESH,
        )

    def arrived(k, c):
        return pltpu.make_async_remote_copy(
            src_ref=sm_s.at[0], dst_ref=rm_s.at[2 * k + c], send_sem=send_m.at[k],
            recv_sem=recv_m.at[2 * k + c], device_id={"row": partner}, device_id_type=MESH,
        )

    @pl.when(core == 0)
    def _():
        portion(0).start()

    for k in range(1, chips):
        portion(k).start()

    act = mm(w2_s[half], n2_s[...], NT) * maskrow
    gl2 = mm(act.astype(BF16), fr)
    gl = gl2[:, :ch]
    for s in range(1, s_loc):
        gl = gl + gl2[:, s * ch : (s + 1) * ch]

    back = mm(m_s[...], g_s[core], NT)
    rt_s[...] = back.reshape(2, wide * seqs, residues)
    for p in range(2):
        for n in range(chips):
            b = p * chips + n
            d = (n % planes) * 4 + (n // planes) * 2 + p
            for s in range(s_loc):
                flag = seq[d * s_loc + s] * resrow
                for h in range(2):
                    at = s * width + h * wide
                    gr2_s[at : at + wide, b * residues : (b + 1) * residues] = (
                        rt_s[h, pl.ds(s * devices + d, wide, stride=seqs), :] * flag
                    )
    total = jnp.zeros(rb_s.shape[1:], F32)
    for n in range(chips):
        pltpu.make_async_remote_copy(
            src_ref=sb_s.at[0], dst_ref=rb_s.at[n], send_sem=send_b.at[n], recv_sem=recv_b.at[n],
            device_id={"row": partner}, device_id_type=MESH,
        ).wait_recv()
        total = total + rb_s[n].astype(F32)
    gt_s[me] = total.astype(BF16)
    copies = gather_start(gt_s, me, core, chip, send_g, recv_g)

    for copy in sideways:
        copy.wait_recv()
    block = feat.at[core, pl.ds((1 - x_at) * planes, planes)]
    at = 2 * planes
    feat_pass.append(send(block, block, send_f.at[at], recv_f.at[at], partner))

    def spread(k, c):
        block = gs_s.at[chip]
        return pltpu.make_async_remote_copy(
            src_ref=block, dst_ref=block, send_sem=send_h.at[2 * k + c], recv_sem=recv_h.at[k],
            device_id={"row": lax.rem(chip + k, chips) * 2 + c}, device_id_type=MESH,
        )

    def landed(k):
        block = gs_s.at[lax.rem(chip - k + chips, chips)]
        return pltpu.make_async_remote_copy(
            src_ref=block, dst_ref=block, send_sem=send_h.at[2 * k], recv_sem=recv_h.at[k],
            device_id={"row": partner}, device_id_type=MESH,
        )

    @pl.when(core == 1)
    def _():
        total = sm_s[chip].astype(F32)
        arrived(0, 0).wait_recv()
        total = total + rm_s[0].astype(F32)
        for k in range(1, chips):
            for c in range(2):
                arrived(k, c).wait_recv()
                total = total + rm_s[2 * k + c].astype(F32)
        gs_s[chip] = total.astype(BF16)
        spread(0, 0).start()
        for k in range(1, chips):
            for c in range(2):
                spread(k, c).start()

    for copy in feat_pass:
        copy.wait_recv()
    feats = feat[...].reshape(devices * residues, lanes)
    gr2 = mm(gr2_s[...].astype(BF16), feats)
    gr = gr2[:width, :ch]
    for s in range(1, s_loc):
        gr = gr + gr2[s * width : (s + 1) * width, s * ch : (s + 1) * ch]

    pk_s[0] = jnp.concatenate([gl[:wide], gl[wide:]], axis=1)
    pk_s[1] = jnp.concatenate([gr[:wide], gr[wide:]], axis=1)
    twin = send(pk_s.at[half], pr_s, send_p.at[1], recv_p.at[1], partner)

    twin.wait_recv()
    ps_s[me] = (pk_s[core] + pr_s[...]).astype(BF16)
    last = []
    block = ps_s.at[me]
    for n in FAR_FIRST + (0,):
        to = other_chip(chip, n) * 2
        if n > 0:
            at = 2 * n + 1
            last.append(send(block, block, send_p.at[at], recv_p.at[at], to + core))
        at = 2 * n
        last.append(send(block, block, send_p.at[at], recv_p.at[at], to + 1 - core))

    def place(d):
        for t in range(2):
            go_ref[pl.ds(2 * d + t, width, stride=width), :] = gt_s[
                d, t * width : (t + 1) * width, :
            ].astype(F32)

    place(me)
    done2 = gather_finish(copies, gt_s, core, chip, chips, send_g, recv_g, place)
    for copy in last:
        copy.wait_recv()

    @pl.when(core == 0)
    def _():
        landed(0).wait_recv()
        portion(0).wait_send()

    for k in range(1, chips):
        landed(k).wait_recv()
        portion(k).wait_send()

    @pl.when(core == 1)
    def _():
        spread(0, 0).wait_send()
        for k in range(1, chips):
            for c in range(2):
                spread(k, c).wait_send()

    for k in range(chips):
        gg_ref[k * g_rows : (k + 1) * g_rows, :] = gs_s[k].astype(F32)
    gl, gr = ps_s[0].astype(F32), ps_s[1].astype(F32)
    for d in range(2, devices, 2):
        gl = gl + ps_s[d].astype(F32)
        gr = gr + ps_s[d + 1].astype(F32)
    for h in range(2):
        gl_ref[h * wide : (h + 1) * wide, :] = gl[:, h * ch : (h + 1) * ch]
        for t in range(2):
            gr_ref[pl.ds(2 * h + t, chips, stride=4), :] = gr[
                t * chips : (t + 1) * chips, h * ch : (h + 1) * ch
            ]
    for copy in (
        nears + [near_pass] + list(rights.values()) + [right_pass] + column + sideways + feat_pass + [crossing]
        + list(scatter.values()) + [twin] + done2 + last
    ):
        copy.wait_send()


def store_kernel(*refs):
    copies = [
        pltpu.make_async_copy(refs[n], refs[5 + n], refs[10].at[n]) for n in (3, 0, 4, 1, 2)
    ]
    for copy in copies:
        copy.start()
    for copy in copies:
        copy.wait()


def fused_device(
    alignment_state, pair_state, cotangent, sequence_row_mask, residue_mask, norm_gain_vector,
    left_matrix_weight, right_matrix_weight, output_weight, output_bias, gate_matrix,
):
    s_loc, residues, ch = alignment_state.shape
    rows, _, pc = pair_state.shape
    width = left_matrix_weight.shape[1]
    devices = lax.axis_size("row")
    seqs = s_loc * devices
    chips = devices // 2
    lanes = s_loc * ch
    top = (width // devices) * width
    smem = pl.BlockSpec(memory_space=pltpu.SMEM)
    vmem = pl.BlockSpec(memory_space=pltpu.VMEM)
    dma = pltpu.SemaphoreType.DMA
    inputs = (
        alignment_state.transpose(0, 2, 1),
        norm_gain_vector.reshape(1, ch),
        pair_state,
        gate_matrix,
        output_weight,
        residue_mask.reshape(1, residues),
        left_matrix_weight.T,
        right_matrix_weight.T,
        cotangent,
        output_bias.reshape(1, pc),
    )
    results = pl.pallas_call(
        fused_kernel,
        name="fused",
        out_shape=(
            pltpu.VMEM((rows, residues, pc), BF16),
            pltpu.VMEM((width, ch), F32),
            pltpu.VMEM((width, ch), F32),
            pltpu.VMEM((width * width, pc), F32),
            pltpu.VMEM((pc, pc), F32),
        ),
        in_specs=[smem, smem] + [pl.BlockSpec(memory_space=pltpu.HBM)] * 10,
        out_specs=(vmem,) * 5,
        scratch_shapes=[
            pltpu.VMEM((devices, top, pc), BF16),
            pltpu.VMEM((chips, pc // chips, pc), BF16),
            pltpu.VMEM((devices, width // 2, 2 * ch), BF16),
            pltpu.VMEM((2, chips, residues, lanes), BF16),
            pltpu.VMEM((2, chips, 2 * rows, lanes), BF16),
            pltpu.VMEM((rows, residues, pc), F32),
            pltpu.VMEM((2, width, width // 2 * pc), BF16),
            pltpu.VMEM((width * width, pc), F32),
            pltpu.VMEM((width, lanes), F32),
            pltpu.VMEM((2, s_loc * width // 2, residues), BF16),
            pltpu.VMEM((2, devices, s_loc * width // 2, residues), BF16),
            pltpu.VMEM((2, width // 2 * seqs, residues), F32),
            pltpu.VMEM((devices * 2 * rows, lanes), F32),
            pltpu.VMEM((2, width, rows * seqs), F32),
            pltpu.VMEM((width * seqs, rows * pc), BF16),
            pltpu.VMEM((2, residues, rows * pc), BF16),
            pltpu.VMEM((rows * residues, pc), BF16),
            pltpu.VMEM((2 * rows * seqs, width // 2 * pc), BF16),
            pltpu.VMEM((s_loc * width, devices * residues), F32),
            pltpu.VMEM((chips, top, pc), BF16),
            pltpu.VMEM((chips, top, pc), BF16),
            pltpu.VMEM((chips, pc // chips, pc), BF16),
            pltpu.VMEM((devices, pc // chips, pc), BF16),
            pltpu.VMEM((2, width // 2, 2 * ch), F32),
            pltpu.VMEM((width // 2, 2 * ch), F32),
            dma((devices,)),
            dma((devices,)),
            dma((chips + 1,)),
            dma((chips + 1,)),
            dma((chips + 1,)),
            dma((chips + 1,)),
            dma,
            dma,
            dma((chips,)),
            dma((chips,)),
            dma((chips,)),
            dma((devices,)),
            dma((2 * chips,)),
            dma((2 * chips,)),
            dma((devices,)),
            dma((chips,)),
            dma((devices,)),
            dma((devices,)),
        ]
        + [pltpu.VMEM(value.shape, value.dtype) for value in inputs]
        + [dma((len(inputs),))],
        compiler_params=pltpu.CompilerParams(
            collective_id=0, has_side_effects=True, vmem_limit_bytes=61 * 1024 * 1024
        ),
    )(sequence_row_mask, residue_mask, *inputs)
    update, left_t, right_t, grad_out, grad_gate = pl.pallas_call(
        store_kernel,
        name="store",
        out_shape=(
            jax.ShapeDtypeStruct((rows, residues, pc), BF16),
            jax.ShapeDtypeStruct((width, ch), F32),
            jax.ShapeDtypeStruct((width, ch), F32),
            jax.ShapeDtypeStruct((width * width, pc), F32),
            jax.ShapeDtypeStruct((pc, pc), F32),
        ),
        in_specs=[vmem] * 5,
        out_specs=(pl.BlockSpec(memory_space=pltpu.HBM),) * 5,
        scratch_shapes=[dma((5,))],
        compiler_params=pltpu.CompilerParams(vmem_limit_bytes=32 * 1024 * 1024),
    )(*results)
    return update, left_t.T, right_t.T, grad_out, grad_gate


def per_device(*arrays):
    alignment_state, pair_state = arrays[0], arrays[1]
    s_loc, residues, ch = alignment_state.shape
    rows, _, pc = pair_state.shape
    width = arrays[6].shape[1]
    devices = lax.axis_size("row")
    fits = (
        lax.axis_size("col") == 1
        and devices % 2 == 0
        and (s_loc * ch, pc, residues) == (128, 128, 128)
        and rows == 8
        and width % devices == 0
        and pc == devices * 8
        and s_loc * devices == 32
    )
    return fused_device(*arrays) if fits else general_device(*arrays)


def solution(mesh):
    return jax.shard_map(
        per_device,
        mesh=mesh,
        in_specs=(
            P(("grp", "row"), "col", None),
            P(("grp", "row"), "col", None),
            P(("grp", "row"), "col", None),
            P("grp"),
            P("grp"),
            P(),
            P(),
            P(),
            P(),
            P(),
            P(),
        ),
        out_specs=(
            P(("grp", "row"), "col", None),
            P("grp", None),
            P("grp", None),
            P("grp", None),
            P("grp", None),
        ),
        check_vma=False,
    )
```

```python
import jax
import jax.numpy as jnp
from jax import lax
from jax.experimental import pallas as pl
from jax.experimental.pallas import tpu as pltpu
from jax.sharding import PartitionSpec as P


def layer_normalize(alignment_state, norm_gain_vector):
    value_entries = alignment_state.astype(jnp.float32)
    average = jnp.mean(value_entries, axis=-1, keepdims=True)
    centred = value_entries - average
    variance = jnp.mean(centred * centred, axis=-1, keepdims=True)
    return (centred * lax.rsqrt(variance + 1e-05) * norm_gain_vector).astype(jnp.bfloat16)


def general_device(
    alignment_state,
    pair_state,
    cotangent,
    sequence_row_mask,
    residue_mask,
    norm_gain_vector,
    left_matrix_weight,
    right_matrix_weight,
    output_weight,
    output_bias,
    gate_matrix,
):
    sequence_resident, column_count, alignment_channel_count = alignment_state.shape
    count_of_rows = pair_state.shape[0]
    pair_chans = pair_state.shape[2]
    projection_width = left_matrix_weight.shape[1]
    every_sequence = sequence_row_mask.shape[0]
    row_at = lax.axis_index("row")
    col_at = lax.axis_index("col")
    number_of_rows = lax.axis_size("row")
    contract_first = (((0,), (0,)), ((), ()))
    contract_second = (((1,), (1,)), ((), ()))
    resident_features = layer_normalize(alignment_state, norm_gain_vector)
    seq_flags = sequence_row_mask.astype(jnp.float32)
    res_flags = residue_mask.astype(jnp.float32)
    my_cols = lax.dynamic_slice_in_dim(res_flags, col_at * column_count, column_count, 0)
    my_rows = lax.dynamic_slice_in_dim(res_flags, row_at * count_of_rows, count_of_rows, 0)
    panel_mask = seq_flags[:, None] * my_rows[None, :]
    column_mask = seq_flags[:, None] * my_cols[None, :]
    broadcast_features = lax.all_gather(
        resident_features.reshape(sequence_resident, column_count * alignment_channel_count),
        "col",
        axis=1,
        tiled=True,
    )
    row_portions = broadcast_features.reshape(
        sequence_resident, number_of_rows, count_of_rows * alignment_channel_count
    )
    row_feats = lax.all_to_all(
        row_portions, "row", split_axis=1, concat_axis=0, tiled=True
    ).reshape(every_sequence * count_of_rows, alignment_channel_count)
    left_panel = (
        jnp.dot(row_feats, left_matrix_weight, preferred_element_type=jnp.float32).reshape(
            every_sequence, count_of_rows, projection_width
        )
        * panel_mask[:, :, None]
    ).astype(jnp.bfloat16)
    left_matrix = left_panel.transpose(1, 2, 0).reshape(
        count_of_rows * projection_width, every_sequence
    )
    column_features = lax.all_gather(
        resident_features.reshape(sequence_resident, column_count * alignment_channel_count),
        "row",
        axis=0,
        tiled=True,
    ).reshape(every_sequence, column_count, alignment_channel_count)
    right_panel = (
        jnp.dot(
            column_features.reshape(every_sequence * column_count, alignment_channel_count),
            right_matrix_weight,
            preferred_element_type=jnp.float32,
        ).reshape(every_sequence, column_count, projection_width)
        * column_mask[:, :, None]
    ).astype(jnp.bfloat16)
    surplus_offset = jnp.zeros((alignment_channel_count, projection_width), jnp.float32)

    def absorb(extra, first_col, width_columns, right_part):
        feat_blk = (
            lax.dynamic_slice_in_dim(column_features, first_col, width_columns, 1)
            .reshape(every_sequence * width_columns, alignment_channel_count)
            .astype(jnp.float32)
        )
        mask_blk = lax.dynamic_slice_in_dim(column_mask, first_col, width_columns, 1)
        masked_part = (
            right_part.reshape(every_sequence, width_columns, projection_width)
            * mask_blk[:, :, None]
        ).reshape(every_sequence * width_columns, projection_width)
        return extra + jnp.dot(feat_blk.T, masked_part, precision=lax.Precision.HIGHEST)

    right_flat = right_panel.reshape(every_sequence, column_count * projection_width)
    row_total = jnp.sum(seq_flags)
    col_block = 128
    n_blocks = column_count // col_block

    def one_block(block_idx, carry):
        new_update, grad_out, grad_gate, left_acc, extra = carry
        first_col = block_idx * col_block
        right_blk = lax.dynamic_slice_in_dim(
            right_flat, first_col * projection_width, col_block * projection_width, 1
        )
        outer_prod = jnp.dot(left_matrix, right_blk, preferred_element_type=jnp.float32)
        outer_prod = outer_prod.reshape(
            count_of_rows, projection_width, col_block, projection_width
        ).transpose(0, 2, 1, 3)
        outer_prod = outer_prod.reshape(
            count_of_rows * col_block, projection_width * projection_width
        ).astype(jnp.bfloat16)
        linear = (
            jnp.dot(outer_prod, output_weight, preferred_element_type=jnp.float32) + output_bias
        )
        pair_blk = lax.dynamic_slice_in_dim(pair_state, first_col, col_block, 1).reshape(
            count_of_rows * col_block, pair_chans
        )
        gate_val = jax.nn.sigmoid(
            jnp.dot(pair_blk, gate_matrix, preferred_element_type=jnp.float32)
        )
        blk_flags = lax.dynamic_slice_in_dim(my_cols, first_col, col_block, 0)
        divisor = jnp.maximum(row_total * my_rows[:, None] * blk_flags[None, :], 1.0).reshape(
            count_of_rows * col_block, 1
        )
        cot_blk = (
            lax.dynamic_slice_in_dim(cotangent, first_col, col_block, 1)
            .reshape(count_of_rows * col_block, pair_chans)
            .astype(jnp.float32)
        )
        new_pair = (gate_val * linear / divisor).astype(jnp.bfloat16)
        new_update = lax.dynamic_update_slice_in_dim(
            new_update, new_pair.reshape(count_of_rows, col_block, pair_chans), first_col, 1
        )
        grad_lin = (cot_blk * gate_val / divisor).astype(jnp.bfloat16)
        grad_pre = (cot_blk * linear / divisor * gate_val * (1.0 - gate_val)).astype(jnp.bfloat16)
        grad_out = grad_out + lax.dot_general(
            outer_prod, grad_lin, contract_first, preferred_element_type=jnp.float32
        )
        grad_gate = grad_gate + lax.dot_general(
            pair_blk, grad_pre, contract_first, preferred_element_type=jnp.float32
        )
        grad_outer = lax.dot_general(
            grad_lin, output_weight, contract_second, preferred_element_type=jnp.float32
        ).astype(jnp.bfloat16)
        outer_turned = (
            grad_outer.reshape(count_of_rows, col_block, projection_width, projection_width)
            .transpose(0, 2, 1, 3)
            .reshape(count_of_rows * projection_width, col_block * projection_width)
        )
        left_acc = left_acc + lax.dot_general(
            outer_turned, right_blk, contract_second, preferred_element_type=jnp.float32
        )
        right_part = lax.dot_general(
            left_matrix, outer_turned, contract_first, preferred_element_type=jnp.float32
        )
        extra = absorb(extra, first_col, col_block, right_part)
        return (new_update, grad_out, grad_gate, left_acc, extra)

    start_carry = (
        jnp.zeros((count_of_rows, column_count, pair_chans), jnp.bfloat16),
        jnp.zeros((projection_width * projection_width, pair_chans), jnp.float32),
        jnp.zeros((pair_chans, pair_chans), jnp.float32),
        jnp.zeros((count_of_rows * projection_width, every_sequence), jnp.float32),
        surplus_offset,
    )
    new_update, grad_out, grad_gate, left_acc, extra = lax.fori_loop(
        0, n_blocks, one_block, start_carry
    )
    grad_left_act = (
        left_acc.reshape(count_of_rows, projection_width, every_sequence).transpose(2, 0, 1)
        * panel_mask[:, :, None]
    )
    grad_left = jnp.dot(
        row_feats.astype(jnp.float32).T,
        grad_left_act.reshape(every_sequence * count_of_rows, projection_width),
        precision=lax.Precision.HIGHEST,
    )
    summed_left, summed_right, summed_out, summed_gate = lax.psum(
        (grad_left, extra, grad_out, grad_gate), ("row", "col")
    )
    return (new_update, summed_left, summed_right, summed_out, summed_gate)


F32 = jnp.float32
BF16 = jnp.bfloat16
MESH = pl.DeviceIdType.MESH
NT = (((1,), (1,)), ((), ()))
TN = (((0,), (0,)), ((), ()))
NN = (((1,), (0,)), ((), ()))


def mm(a, b, dims=NN):
    return lax.dot_general(a, b, dims, preferred_element_type=F32)


def send(src, dst, send_sem, recv_sem, target):
    copy = pltpu.make_async_remote_copy(
        src_ref=src, dst_ref=dst, send_sem=send_sem, recv_sem=recv_sem,
        device_id={"row": target}, device_id_type=MESH,
    )
    copy.start()
    return copy


FAR_FIRST = (6, 7, 4, 5, 2, 3, 1)
NEAR_FIRST = (1, 2, 3, 4, 5, 6, 7)


def other_chip(chip, n):
    z_at, x_at = lax.div(chip, 2), lax.rem(chip, 2)
    z_to = (z_at, z_at + 1 - 2 * lax.rem(z_at, 2), lax.rem(z_at + 2, 4), 3 - z_at)[n // 2]
    return z_to * 2 + (1 - x_at if n % 2 else x_at)


def gather_start(buf, me, core, chip, send_sem, recv_sem):
    block = buf.at[me]
    return {
        n: send(
            block, block, send_sem.at[n], recv_sem.at[n], other_chip(chip, n) * 2 + 1 - core
        )
        for n in FAR_FIRST + (0,)
    }


def gather_finish(copies, buf, core, chip, chips, send_sem, recv_sem, use):
    partner = chip * 2 + 1 - core
    passed = []
    for n in NEAR_FIRST:
        copies[n].wait_recv()
        source = other_chip(chip, n) * 2 + 1 - core
        block = buf.at[source]
        at = chips + n
        passed.append(send(block, block, send_sem.at[at], recv_sem.at[at], partner))
        use(source)
    copies[0].wait_recv()
    use(partner)
    for n, copy in zip(NEAR_FIRST, passed):
        copy.wait_recv()
        use(other_chip(chip, n) * 2 + core)
    return list(copies.values()) + passed


def fused_kernel(
    seq_ref, res_ref, *inputs_and_rest,
):
    hbm, rest = inputs_and_rest[:10], inputs_and_rest[10:]
    outs_and_scratch, vmem, load_sem = rest[:-11], rest[-11:-1], rest[-1]
    loads = [
        pltpu.make_async_copy(src, dst, load_sem.at[n])
        for n, (src, dst) in enumerate(zip(hbm, vmem))
    ]
    for n in (0, 1, 5, 7, 2, 3, 8, 4, 6, 9):
        loads[n].start()
    fused_body(loads, seq_ref, res_ref, *vmem, *outs_and_scratch)


def fused_body(
    loads, seq_ref, res_ref, align_ref, gain_ref, pair_ref, gm_ref, w_ref, resrow_ref, wl_ref,
    wr_ref, cot_ref, bias_ref,
    upd_ref, gl_ref, gr_ref, go_ref, gg_ref,
    gt_s, gs_s, ps_s, feat, near, gate_s, w2_s, w32_s, wr32_s, own_s, rin_s, rt_s, fr_s, lt_s, m_s, g_s, pre_s, n2_s,
    gr2_s, sb_s, rb_s, sm_s, rm_s, pk_s, pr_s,
    send_r, recv_r, send_n, recv_n, send_f, recv_f, send_x, recv_x, send_b, recv_b, send_m, recv_m,
    send_g, recv_g, send_h, recv_h, send_p, recv_p,
):
    me = lax.axis_index("row")
    core = lax.rem(me, 2)
    chip = lax.div(me, 2)
    x_at = lax.rem(chip, 2)
    z_at = lax.div(chip, 2)
    half = 1 - core
    _, chips, residues, lanes = feat.shape
    devices = 2 * chips
    planes = chips // 2
    s_loc, ch, _ = align_ref.shape
    rows, _, pc = pair_ref.shape
    width = wl_ref.shape[0]
    seqs = s_loc * devices
    partner = chip * 2 + 1 - core
    across = (z_at * 2 + 1 - x_at) * 2 + core
    wide = width // 2
    mine_wide = rows * seqs

    barrier = pltpu.get_barrier_semaphore()
    for k in range(1, devices):
        pl.semaphore_signal(
            barrier, inc=1, device_id={"row": lax.rem(me + k, devices)}, device_id_type=MESH
        )

    for n in (0, 1, 5, 7):
        loads[n].wait()
    parts = []
    for s in range(s_loc):
        value = align_ref[s].astype(F32)
        centred = value - jnp.mean(value, axis=0, keepdims=True)
        variance = jnp.mean(centred * centred, axis=0, keepdims=True)
        parts.append(centred * lax.rsqrt(variance + 1e-05))
    gain = jnp.concatenate([gain_ref[...]] * s_loc, axis=1)
    own = (jnp.transpose(jnp.concatenate(parts, axis=0)) * gain).astype(BF16)
    feat[core, x_at * planes + z_at] = own

    resrow = resrow_ref[...].astype(F32)
    wr32_s[...] = jnp.concatenate([wr_ref[...].astype(F32)] * s_loc, axis=1)
    lane_s = lax.div(lax.broadcasted_iota(jnp.int32, (wide, lanes), 1), ch)
    wr_parts = []
    for h in range(2):
        block = jnp.concatenate(
            [wr32_s[pl.ds(2 * h + t, chips, stride=4), :] for t in range(2)], axis=0
        )
        for s in range(s_loc):
            wr_parts.append(jnp.where(lane_s == s, block, 0.0))
    right = mm(jnp.concatenate(wr_parts, axis=0).astype(BF16), own, NT)
    flags = [seq_ref[me * s_loc + s].astype(F32) * resrow for s in range(s_loc)]
    for h in range(2):
        for s in range(s_loc):
            at = (h * s_loc + s) * wide
            own_s[h, s * wide : (s + 1) * wide, :] = (
                right[at : at + wide] * flags[s]
            ).astype(BF16)
    rin_s[half, me] = own_s[half]
    pl.semaphore_wait(barrier, devices - 1)

    rights = {}
    nears = []
    mine_at = feat.at[core, x_at * planes + z_at]
    for n in FAR_FIRST + (0,):
        to = other_chip(chip, n)
        window = pl.ds(pl.multiple_of(to * 2 * rows, 2 * rows), 2 * rows)
        nears.append(
            send(
                mine_at.at[window], near.at[core, chip], send_n.at[n], recv_n.at[n],
                to * 2 + 1 - core,
            )
        )
    for n in FAR_FIRST + (0,):
        to = other_chip(chip, n)
        if n > 0:
            at = 2 * n + 1
            rights[at] = send(
                own_s.at[half], rin_s.at[half, me], send_r.at[at], recv_r.at[at], to * 2 + core
            )
        at = 2 * n
        rights[at] = send(
            own_s.at[core], rin_s.at[core, me], send_r.at[at], recv_r.at[at], to * 2 + 1 - core
        )
    column = []
    for k in range(1, planes):
        to = (lax.rem(z_at + k, planes) * 2 + x_at) * 2 + core
        column.append(send(mine_at, mine_at, send_f.at[k], recv_f.at[k], to))
    sideways = [send(mine_at, mine_at, send_f.at[0], recv_f.at[0], across)]

    for n in (2, 3, 4, 6, 8, 9):
        loads[n].wait()
    gm = gm_ref[...]
    rescol = jnp.transpose(jnp.broadcast_to(resrow, (pc, residues)))
    seq = [seq_ref[s].astype(F32) for s in range(seqs)]
    both_rows = [res_ref[chip * 2 * rows + i].astype(F32) for i in range(2 * rows)]
    mine = [res_ref[me * rows + i].astype(F32) for i in range(rows)]
    row_total = seq[0]
    for s in range(1, seqs):
        row_total = row_total + seq[s]
    present = 1.0 / jnp.maximum(row_total * rescol, 1.0)
    inverse = [present * mine[i] + (1.0 - mine[i]) for i in range(rows)]
    for i in range(rows):
        gate = jax.nn.sigmoid(mm(pair_ref[i], gm))
        gate_s[i] = gate
        g_s[core, :, i * pc : (i + 1) * pc] = (
            cot_ref[i].astype(F32) * (gate * inverse[i])
        ).astype(BF16)
    crossing = send(g_s.at[core], g_s.at[core], send_x, recv_x, partner)

    w32_s[...] = w_ref[...].astype(F32)
    for h in range(2):
        for t in range(2):
            for k in range(chips):
                e, q = 4 * k + 2 * h + t, t * chips + k
                w2_s[h, :, q * pc : (q + 1) * pc] = w32_s[
                    pl.ds(e, width, stride=width), :
                ].astype(BF16)
    lane = lax.broadcasted_iota(jnp.int32, (1, 2 * mine_wide), 1)
    maskrow = jnp.zeros((1, 2 * mine_wide), F32)
    for s in range(s_loc):
        for d in range(devices):
            maskrow = jnp.where(lax.rem(lane, seqs) == s * devices + d, seq[d * s_loc + s], maskrow)
    resl = jnp.zeros((1, 2 * mine_wide), F32)
    for i in range(2 * rows):
        resl = jnp.where(lax.div(lane, seqs) == i, both_rows[i], resl)
    maskrow = maskrow * resl
    wlt = wl_ref[...].astype(F32)
    wlt2 = jnp.concatenate([wlt] * s_loc, axis=1).astype(BF16)

    for copy in nears:
        copy.wait_recv()
    near_pass = send(near.at[half], near.at[half], send_n.at[chips], recv_n.at[chips], partner)
    near_pass.wait_recv()
    for d in range(devices):
        fr_s[d * 2 * rows : (d + 1) * 2 * rows, :] = near[d % 2, d // 2].astype(F32)
    lane_d = lax.div(lax.broadcasted_iota(jnp.int32, (devices, lanes), 1), ch)
    pieces = []
    for i in range(2 * rows):
        block = fr_s[pl.ds(i, devices, stride=2 * rows), :]
        for s in range(s_loc):
            pieces.append(jnp.where(lane_d == s, block, 0.0))
    fr = jnp.concatenate(pieces, axis=0).astype(BF16)
    left_t = mm(wlt2, fr, NT) * maskrow
    for c in range(2):
        lt_s[c] = left_t[:, c * mine_wide : (c + 1) * mine_wide]
    left_t = left_t.astype(BF16)

    left = jnp.transpose(lt_s[core]).astype(BF16)
    for h in range(2):
        for e in range(0, wide, 2):
            part = mm(left, w2_s[h, :, e * pc : (e + 2) * pc]).astype(BF16)
            for n in range(2):
                at = (h * wide + e + n) * seqs
                for i in range(rows):
                    m_s[at : at + seqs, i * pc : (i + 1) * pc] = part[
                        i * seqs : (i + 1) * seqs, n * pc : (n + 1) * pc
                    ]

    def lay_out(h, d):
        for s in range(s_loc):
            rt_s[h, pl.ds(s * devices + d, wide, stride=seqs), :] = rin_s[
                h, d, s * wide : (s + 1) * wide, :
            ].astype(F32)

    crossing.wait_recv()
    lay_out(half, me)
    for n in (0,) + NEAR_FIRST:
        source = other_chip(chip, n) * 2
        rights[2 * n].wait_recv()
        lay_out(half, source + 1 - core)
        if n > 0:
            rights[2 * n + 1].wait_recv()
            lay_out(half, source + core)
    right_pass = send(
        rin_s.at[half], rin_s.at[half], send_r.at[1], recv_r.at[1], partner
    )
    rtt = rt_s[half].astype(BF16)
    scatter = {}
    group = 4
    for first in range(0, chips, group):
        for t in range(2):
            at = t * chips + first
            for c in range(2):
                part = mm(rtt[at * seqs : (at + group) * seqs], g_s[c]).astype(BF16)
                for h in range(group):
                    for i in range(rows):
                        to = (c * rows + i) * seqs
                        n2_s[to : to + seqs, (at + h) * pc : (at + h + 1) * pc] = part[
                            h * seqs : (h + 1) * seqs, i * pc : (i + 1) * pc
                        ]
        for t in range(2):
            at = t * chips + first
            go = mm(left_t, n2_s[:, at * pc : (at + group) * pc])
            for h in range(group):
                sb_s[first + h, t * width : (t + 1) * width, :] = go[
                    :, h * pc : (h + 1) * pc
                ].astype(BF16)
        for h in (1, 0, 3, 2):
            k = first + h
            n = lax.rem(k - chip + chips, chips)
            scatter[k] = send(
                sb_s.at[k], rb_s.at[n], send_b.at[n], recv_b.at[n], k * 2 + 1 - core
            )

    for k in range(1, planes):
        column[k - 1].wait_recv()
        block = feat.at[core, x_at * planes + lax.rem(z_at - k + planes, planes)]
        at = planes + k
        sideways.append(send(block, block, send_f.at[at], recv_f.at[at], across))
    block = feat.at[core, pl.ds(x_at * planes, planes)]
    feat_pass = [send(block, block, send_f.at[planes], recv_f.at[planes], partner)]

    right_pass.wait_recv()
    for d in range(devices):
        lay_out(core, d)
    rt = jnp.transpose(rt_s[...].reshape(width * seqs, residues)).astype(BF16)

    bias = bias_ref[...]
    for i in range(0, rows, 2):
        lin2 = mm(rt, m_s[:, i * pc : (i + 2) * pc])
        for h in range(2):
            linear = lin2[:, h * pc : (h + 1) * pc] + bias
            gate = gate_s[i + h]
            scaled = gate * inverse[i + h]
            upd_ref[i + h] = (scaled * linear).astype(BF16)
            pre_s[(i + h) * residues : (i + h + 1) * residues, :] = (
                cot_ref[i + h].astype(F32) * scaled * linear * (1.0 - gate)
            ).astype(BF16)
    gg = mm(pair_ref[...].reshape(rows * residues, pc), pre_s[...], TN)
    g_rows = pc // chips
    sm_s[...] = gg.reshape(chips, g_rows, pc).astype(BF16)

    def portion(k):
        to = lax.rem(chip + k, chips)
        return pltpu.make_async_remote_copy(
            src_ref=sm_s.at[to], dst_ref=rm_s.at[2 * k + core], send_sem=send_m.at[k],
            recv_sem=recv_m.at[2 * k + core], device_id={"row": to * 2 + 1}, device_id_type=MESH,
        )

    def arrived(k, c):
        return pltpu.make_async_remote_copy(
            src_ref=sm_s.at[0], dst_ref=rm_s.at[2 * k + c], send_sem=send_m.at[k],
            recv_sem=recv_m.at[2 * k + c], device_id={"row": partner}, device_id_type=MESH,
        )

    @pl.when(core == 0)
    def _():
        portion(0).start()

    for k in range(1, chips):
        portion(k).start()

    act = mm(w2_s[half], n2_s[...], NT) * maskrow
    gl2 = mm(act.astype(BF16), fr)
    gl = gl2[:, :ch]
    for s in range(1, s_loc):
        gl = gl + gl2[:, s * ch : (s + 1) * ch]

    back = mm(m_s[...], g_s[core], NT)
    rt_s[...] = back.reshape(2, wide * seqs, residues)
    for p in range(2):
        for n in range(chips):
            b = p * chips + n
            d = (n % planes) * 4 + (n // planes) * 2 + p
            for s in range(s_loc):
                flag = seq[d * s_loc + s] * resrow
                for h in range(2):
                    at = s * width + h * wide
                    gr2_s[at : at + wide, b * residues : (b + 1) * residues] = (
                        rt_s[h, pl.ds(s * devices + d, wide, stride=seqs), :] * flag
                    )
    total = jnp.zeros(rb_s.shape[1:], F32)
    for n in range(chips):
        pltpu.make_async_remote_copy(
            src_ref=sb_s.at[0], dst_ref=rb_s.at[n], send_sem=send_b.at[n], recv_sem=recv_b.at[n],
            device_id={"row": partner}, device_id_type=MESH,
        ).wait_recv()
        total = total + rb_s[n].astype(F32)
    gt_s[me] = total.astype(BF16)
    copies = gather_start(gt_s, me, core, chip, send_g, recv_g)

    for copy in sideways:
        copy.wait_recv()
    block = feat.at[core, pl.ds((1 - x_at) * planes, planes)]
    at = 2 * planes
    feat_pass.append(send(block, block, send_f.at[at], recv_f.at[at], partner))

    def spread(k, c):
        block = gs_s.at[chip]
        return pltpu.make_async_remote_copy(
            src_ref=block, dst_ref=block, send_sem=send_h.at[2 * k + c], recv_sem=recv_h.at[k],
            device_id={"row": lax.rem(chip + k, chips) * 2 + c}, device_id_type=MESH,
        )

    def landed(k):
        block = gs_s.at[lax.rem(chip - k + chips, chips)]
        return pltpu.make_async_remote_copy(
            src_ref=block, dst_ref=block, send_sem=send_h.at[2 * k], recv_sem=recv_h.at[k],
            device_id={"row": partner}, device_id_type=MESH,
        )

    @pl.when(core == 1)
    def _():
        total = sm_s[chip].astype(F32)
        arrived(0, 0).wait_recv()
        total = total + rm_s[0].astype(F32)
        for k in range(1, chips):
            for c in range(2):
                arrived(k, c).wait_recv()
                total = total + rm_s[2 * k + c].astype(F32)
        gs_s[chip] = total.astype(BF16)
        spread(0, 0).start()
        for k in range(1, chips):
            for c in range(2):
                spread(k, c).start()

    for copy in feat_pass:
        copy.wait_recv()
    feats = feat[...].reshape(devices * residues, lanes)
    gr2 = mm(gr2_s[...].astype(BF16), feats)
    gr = gr2[:width, :ch]
    for s in range(1, s_loc):
        gr = gr + gr2[s * width : (s + 1) * width, s * ch : (s + 1) * ch]

    pk_s[0] = jnp.concatenate([gl[:wide], gl[wide:]], axis=1)
    pk_s[1] = jnp.concatenate([gr[:wide], gr[wide:]], axis=1)
    twin = send(pk_s.at[half], pr_s, send_p.at[1], recv_p.at[1], partner)

    twin.wait_recv()
    ps_s[me] = (pk_s[core] + pr_s[...]).astype(BF16)
    last = []
    block = ps_s.at[me]
    for n in FAR_FIRST + (0,):
        to = other_chip(chip, n) * 2
        if n > 0:
            at = 2 * n + 1
            last.append(send(block, block, send_p.at[at], recv_p.at[at], to + core))
        at = 2 * n
        last.append(send(block, block, send_p.at[at], recv_p.at[at], to + 1 - core))

    def place(d):
        for t in range(2):
            go_ref[pl.ds(2 * d + t, width, stride=width), :] = gt_s[
                d, t * width : (t + 1) * width, :
            ].astype(F32)

    place(me)
    done2 = gather_finish(copies, gt_s, core, chip, chips, send_g, recv_g, place)
    for copy in last:
        copy.wait_recv()

    @pl.when(core == 0)
    def _():
        landed(0).wait_recv()
        portion(0).wait_send()

    for k in range(1, chips):
        landed(k).wait_recv()
        portion(k).wait_send()

    @pl.when(core == 1)
    def _():
        spread(0, 0).wait_send()
        for k in range(1, chips):
            for c in range(2):
                spread(k, c).wait_send()

    for k in range(chips):
        gg_ref[k * g_rows : (k + 1) * g_rows, :] = gs_s[k].astype(F32)
    gl, gr = ps_s[0].astype(F32), ps_s[1].astype(F32)
    for d in range(2, devices, 2):
        gl = gl + ps_s[d].astype(F32)
        gr = gr + ps_s[d + 1].astype(F32)
    for h in range(2):
        gl_ref[h * wide : (h + 1) * wide, :] = gl[:, h * ch : (h + 1) * ch]
        for t in range(2):
            gr_ref[pl.ds(2 * h + t, chips, stride=4), :] = gr[
                t * chips : (t + 1) * chips, h * ch : (h + 1) * ch
            ]
    for copy in (
        nears + [near_pass] + list(rights.values()) + [right_pass] + column + sideways + feat_pass + [crossing]
        + list(scatter.values()) + [twin] + done2 + last
    ):
        copy.wait_send()


def store_kernel(*refs):
    copies = [
        pltpu.make_async_copy(refs[n], refs[5 + n], refs[10].at[n]) for n in (3, 0, 4, 1, 2)
    ]
    for copy in copies:
        copy.start()
    for copy in copies:
        copy.wait()


def fused_device(
    alignment_state, pair_state, cotangent, sequence_row_mask, residue_mask, norm_gain_vector,
    left_matrix_weight, right_matrix_weight, output_weight, output_bias, gate_matrix,
):
    s_loc, residues, ch = alignment_state.shape
    rows, _, pc = pair_state.shape
    width = left_matrix_weight.shape[1]
    devices = lax.axis_size("row")
    seqs = s_loc * devices
    chips = devices // 2
    lanes = s_loc * ch
    top = (width // devices) * width
    smem = pl.BlockSpec(memory_space=pltpu.SMEM)
    vmem = pl.BlockSpec(memory_space=pltpu.VMEM)
    dma = pltpu.SemaphoreType.DMA
    inputs = (
        alignment_state.transpose(0, 2, 1),
        norm_gain_vector.reshape(1, ch),
        pair_state,
        gate_matrix,
        output_weight,
        residue_mask.reshape(1, residues),
        left_matrix_weight.T,
        right_matrix_weight.T,
        cotangent,
        output_bias.reshape(1, pc),
    )
    results = pl.pallas_call(
        fused_kernel,
        name="fused",
        out_shape=(
            pltpu.VMEM((rows, residues, pc), BF16),
            pltpu.VMEM((width, ch), F32),
            pltpu.VMEM((width, ch), F32),
            pltpu.VMEM((width * width, pc), F32),
            pltpu.VMEM((pc, pc), F32),
        ),
        in_specs=[smem, smem] + [pl.BlockSpec(memory_space=pltpu.HBM)] * 10,
        out_specs=(vmem,) * 5,
        scratch_shapes=[
            pltpu.VMEM((devices, top, pc), BF16),
            pltpu.VMEM((chips, pc // chips, pc), BF16),
            pltpu.VMEM((devices, width // 2, 2 * ch), BF16),
            pltpu.VMEM((2, chips, residues, lanes), BF16),
            pltpu.VMEM((2, chips, 2 * rows, lanes), BF16),
            pltpu.VMEM((rows, residues, pc), F32),
            pltpu.VMEM((2, width, width // 2 * pc), BF16),
            pltpu.VMEM((width * width, pc), F32),
            pltpu.VMEM((width, lanes), F32),
            pltpu.VMEM((2, s_loc * width // 2, residues), BF16),
            pltpu.VMEM((2, devices, s_loc * width // 2, residues), BF16),
            pltpu.VMEM((2, width // 2 * seqs, residues), F32),
            pltpu.VMEM((devices * 2 * rows, lanes), F32),
            pltpu.VMEM((2, width, rows * seqs), F32),
            pltpu.VMEM((width * seqs, rows * pc), BF16),
            pltpu.VMEM((2, residues, rows * pc), BF16),
            pltpu.VMEM((rows * residues, pc), BF16),
            pltpu.VMEM((2 * rows * seqs, width // 2 * pc), BF16),
            pltpu.VMEM((s_loc * width, devices * residues), F32),
            pltpu.VMEM((chips, top, pc), BF16),
            pltpu.VMEM((chips, top, pc), BF16),
            pltpu.VMEM((chips, pc // chips, pc), BF16),
            pltpu.VMEM((devices, pc // chips, pc), BF16),
            pltpu.VMEM((2, width // 2, 2 * ch), F32),
            pltpu.VMEM((width // 2, 2 * ch), F32),
            dma((devices,)),
            dma((devices,)),
            dma((chips + 1,)),
            dma((chips + 1,)),
            dma((chips + 1,)),
            dma((chips + 1,)),
            dma,
            dma,
            dma((chips,)),
            dma((chips,)),
            dma((chips,)),
            dma((devices,)),
            dma((2 * chips,)),
            dma((2 * chips,)),
            dma((devices,)),
            dma((chips,)),
            dma((devices,)),
            dma((devices,)),
        ]
        + [pltpu.VMEM(value.shape, value.dtype) for value in inputs]
        + [dma((len(inputs),))],
        compiler_params=pltpu.CompilerParams(
            collective_id=0, has_side_effects=True, vmem_limit_bytes=61 * 1024 * 1024
        ),
    )(sequence_row_mask, residue_mask, *inputs)
    update, left_t, right_t, grad_out, grad_gate = pl.pallas_call(
        store_kernel,
        name="store",
        out_shape=(
            jax.ShapeDtypeStruct((rows, residues, pc), BF16),
            jax.ShapeDtypeStruct((width, ch), F32),
            jax.ShapeDtypeStruct((width, ch), F32),
            jax.ShapeDtypeStruct((width * width, pc), F32),
            jax.ShapeDtypeStruct((pc, pc), F32),
        ),
        in_specs=[vmem] * 5,
        out_specs=(pl.BlockSpec(memory_space=pltpu.HBM),) * 5,
        scratch_shapes=[dma((5,))],
        compiler_params=pltpu.CompilerParams(vmem_limit_bytes=32 * 1024 * 1024),
    )(*results)
    return update, left_t.T, right_t.T, grad_out, grad_gate


def per_device(*arrays):
    alignment_state, pair_state = arrays[0], arrays[1]
    s_loc, residues, ch = alignment_state.shape
    rows, _, pc = pair_state.shape
    width = arrays[6].shape[1]
    devices = lax.axis_size("row")
    fits = (
        lax.axis_size("col") == 1
        and devices % 2 == 0
        and (s_loc * ch, pc, residues) == (128, 128, 128)
        and rows == 8
        and width % devices == 0
        and pc == devices * 8
        and s_loc * devices == 32
    )
    return fused_device(*arrays) if fits else general_device(*arrays)


def solution(mesh):
    return jax.shard_map(
        per_device,
        mesh=mesh,
        in_specs=(
            P(("grp", "row"), "col", None),
            P(("grp", "row"), "col", None),
            P(("grp", "row"), "col", None),
            P("grp"),
            P("grp"),
            P(),
            P(),
            P(),
            P(),
            P(),
            P(),
        ),
        out_specs=(
            P(("grp", "row"), "col", None),
            P("grp", None),
            P("grp", None),
            P("grp", None),
            P("grp", None),
        ),
        check_vma=False,
    )
```

```python
import jax
import jax.numpy as jnp
from jax import lax
from jax.experimental import pallas as pl
from jax.experimental.pallas import tpu as pltpu
from jax.sharding import PartitionSpec as P


def layer_normalize(alignment_state, norm_gain_vector):
    value_entries = alignment_state.astype(jnp.float32)
    average = jnp.mean(value_entries, axis=-1, keepdims=True)
    centred = value_entries - average
    variance = jnp.mean(centred * centred, axis=-1, keepdims=True)
    return (centred * lax.rsqrt(variance + 1e-05) * norm_gain_vector).astype(jnp.bfloat16)


def general_device(
    alignment_state,
    pair_state,
    cotangent,
    sequence_row_mask,
    residue_mask,
    norm_gain_vector,
    left_matrix_weight,
    right_matrix_weight,
    output_weight,
    output_bias,
    gate_matrix,
):
    sequence_resident, column_count, alignment_channel_count = alignment_state.shape
    count_of_rows = pair_state.shape[0]
    pair_chans = pair_state.shape[2]
    projection_width = left_matrix_weight.shape[1]
    every_sequence = sequence_row_mask.shape[0]
    row_at = lax.axis_index("row")
    col_at = lax.axis_index("col")
    number_of_rows = lax.axis_size("row")
    contract_first = (((0,), (0,)), ((), ()))
    contract_second = (((1,), (1,)), ((), ()))
    resident_features = layer_normalize(alignment_state, norm_gain_vector)
    seq_flags = sequence_row_mask.astype(jnp.float32)
    res_flags = residue_mask.astype(jnp.float32)
    my_cols = lax.dynamic_slice_in_dim(res_flags, col_at * column_count, column_count, 0)
    my_rows = lax.dynamic_slice_in_dim(res_flags, row_at * count_of_rows, count_of_rows, 0)
    panel_mask = seq_flags[:, None] * my_rows[None, :]
    column_mask = seq_flags[:, None] * my_cols[None, :]
    broadcast_features = lax.all_gather(
        resident_features.reshape(sequence_resident, column_count * alignment_channel_count),
        "col",
        axis=1,
        tiled=True,
    )
    row_portions = broadcast_features.reshape(
        sequence_resident, number_of_rows, count_of_rows * alignment_channel_count
    )
    row_feats = lax.all_to_all(
        row_portions, "row", split_axis=1, concat_axis=0, tiled=True
    ).reshape(every_sequence * count_of_rows, alignment_channel_count)
    left_panel = (
        jnp.dot(row_feats, left_matrix_weight, preferred_element_type=jnp.float32).reshape(
            every_sequence, count_of_rows, projection_width
        )
        * panel_mask[:, :, None]
    ).astype(jnp.bfloat16)
    left_matrix = left_panel.transpose(1, 2, 0).reshape(
        count_of_rows * projection_width, every_sequence
    )
    column_features = lax.all_gather(
        resident_features.reshape(sequence_resident, column_count * alignment_channel_count),
        "row",
        axis=0,
        tiled=True,
    ).reshape(every_sequence, column_count, alignment_channel_count)
    right_panel = (
        jnp.dot(
            column_features.reshape(every_sequence * column_count, alignment_channel_count),
            right_matrix_weight,
            preferred_element_type=jnp.float32,
        ).reshape(every_sequence, column_count, projection_width)
        * column_mask[:, :, None]
    ).astype(jnp.bfloat16)
    surplus_offset = jnp.zeros((alignment_channel_count, projection_width), jnp.float32)

    def absorb(extra, first_col, width_columns, right_part):
        feat_blk = (
            lax.dynamic_slice_in_dim(column_features, first_col, width_columns, 1)
            .reshape(every_sequence * width_columns, alignment_channel_count)
            .astype(jnp.float32)
        )
        mask_blk = lax.dynamic_slice_in_dim(column_mask, first_col, width_columns, 1)
        masked_part = (
            right_part.reshape(every_sequence, width_columns, projection_width)
            * mask_blk[:, :, None]
        ).reshape(every_sequence * width_columns, projection_width)
        return extra + jnp.dot(feat_blk.T, masked_part, precision=lax.Precision.HIGHEST)

    right_flat = right_panel.reshape(every_sequence, column_count * projection_width)
    row_total = jnp.sum(seq_flags)
    col_block = 128
    n_blocks = column_count // col_block

    def one_block(block_idx, carry):
        new_update, grad_out, grad_gate, left_acc, extra = carry
        first_col = block_idx * col_block
        right_blk = lax.dynamic_slice_in_dim(
            right_flat, first_col * projection_width, col_block * projection_width, 1
        )
        outer_prod = jnp.dot(left_matrix, right_blk, preferred_element_type=jnp.float32)
        outer_prod = outer_prod.reshape(
            count_of_rows, projection_width, col_block, projection_width
        ).transpose(0, 2, 1, 3)
        outer_prod = outer_prod.reshape(
            count_of_rows * col_block, projection_width * projection_width
        ).astype(jnp.bfloat16)
        linear = (
            jnp.dot(outer_prod, output_weight, preferred_element_type=jnp.float32) + output_bias
        )
        pair_blk = lax.dynamic_slice_in_dim(pair_state, first_col, col_block, 1).reshape(
            count_of_rows * col_block, pair_chans
        )
        gate_val = jax.nn.sigmoid(
            jnp.dot(pair_blk, gate_matrix, preferred_element_type=jnp.float32)
        )
        blk_flags = lax.dynamic_slice_in_dim(my_cols, first_col, col_block, 0)
        divisor = jnp.maximum(row_total * my_rows[:, None] * blk_flags[None, :], 1.0).reshape(
            count_of_rows * col_block, 1
        )
        cot_blk = (
            lax.dynamic_slice_in_dim(cotangent, first_col, col_block, 1)
            .reshape(count_of_rows * col_block, pair_chans)
            .astype(jnp.float32)
        )
        new_pair = (gate_val * linear / divisor).astype(jnp.bfloat16)
        new_update = lax.dynamic_update_slice_in_dim(
            new_update, new_pair.reshape(count_of_rows, col_block, pair_chans), first_col, 1
        )
        grad_lin = (cot_blk * gate_val / divisor).astype(jnp.bfloat16)
        grad_pre = (cot_blk * linear / divisor * gate_val * (1.0 - gate_val)).astype(jnp.bfloat16)
        grad_out = grad_out + lax.dot_general(
            outer_prod, grad_lin, contract_first, preferred_element_type=jnp.float32
        )
        grad_gate = grad_gate + lax.dot_general(
            pair_blk, grad_pre, contract_first, preferred_element_type=jnp.float32
        )
        grad_outer = lax.dot_general(
            grad_lin, output_weight, contract_second, preferred_element_type=jnp.float32
        ).astype(jnp.bfloat16)
        outer_turned = (
            grad_outer.reshape(count_of_rows, col_block, projection_width, projection_width)
            .transpose(0, 2, 1, 3)
            .reshape(count_of_rows * projection_width, col_block * projection_width)
        )
        left_acc = left_acc + lax.dot_general(
            outer_turned, right_blk, contract_second, preferred_element_type=jnp.float32
        )
        right_part = lax.dot_general(
            left_matrix, outer_turned, contract_first, preferred_element_type=jnp.float32
        )
        extra = absorb(extra, first_col, col_block, right_part)
        return (new_update, grad_out, grad_gate, left_acc, extra)

    start_carry = (
        jnp.zeros((count_of_rows, column_count, pair_chans), jnp.bfloat16),
        jnp.zeros((projection_width * projection_width, pair_chans), jnp.float32),
        jnp.zeros((pair_chans, pair_chans), jnp.float32),
        jnp.zeros((count_of_rows * projection_width, every_sequence), jnp.float32),
        surplus_offset,
    )
    new_update, grad_out, grad_gate, left_acc, extra = lax.fori_loop(
        0, n_blocks, one_block, start_carry
    )
    grad_left_act = (
        left_acc.reshape(count_of_rows, projection_width, every_sequence).transpose(2, 0, 1)
        * panel_mask[:, :, None]
    )
    grad_left = jnp.dot(
        row_feats.astype(jnp.float32).T,
        grad_left_act.reshape(every_sequence * count_of_rows, projection_width),
        precision=lax.Precision.HIGHEST,
    )
    summed_left, summed_right, summed_out, summed_gate = lax.psum(
        (grad_left, extra, grad_out, grad_gate), ("row", "col")
    )
    return (new_update, summed_left, summed_right, summed_out, summed_gate)


F32 = jnp.float32
BF16 = jnp.bfloat16
MESH = pl.DeviceIdType.MESH
NT = (((1,), (1,)), ((), ()))
TN = (((0,), (0,)), ((), ()))
NN = (((1,), (0,)), ((), ()))


def mm(a, b, dims=NN):
    return lax.dot_general(a, b, dims, preferred_element_type=F32)


def send(src, dst, send_sem, recv_sem, target):
    copy = pltpu.make_async_remote_copy(
        src_ref=src, dst_ref=dst, send_sem=send_sem, recv_sem=recv_sem,
        device_id={"row": target}, device_id_type=MESH,
    )
    copy.start()
    return copy


FAR_FIRST = (6, 7, 4, 5, 2, 3, 1)
NEAR_FIRST = (1, 2, 3, 4, 5, 6, 7)


def other_chip(chip, n):
    z_at, x_at = lax.div(chip, 2), lax.rem(chip, 2)
    z_to = (z_at, z_at + 1 - 2 * lax.rem(z_at, 2), lax.rem(z_at + 2, 4), 3 - z_at)[n // 2]
    return z_to * 2 + (1 - x_at if n % 2 else x_at)


def gather_start(buf, me, core, chip, send_sem, recv_sem):
    block = buf.at[me]
    return {
        n: send(
            block, block, send_sem.at[n], recv_sem.at[n], other_chip(chip, n) * 2 + 1 - core
        )
        for n in FAR_FIRST + (0,)
    }


def gather_finish(copies, buf, core, chip, chips, send_sem, recv_sem, use):
    partner = chip * 2 + 1 - core
    passed = []
    for n in NEAR_FIRST:
        copies[n].wait_recv()
        source = other_chip(chip, n) * 2 + 1 - core
        block = buf.at[source]
        at = chips + n
        passed.append(send(block, block, send_sem.at[at], recv_sem.at[at], partner))
        use(source)
    copies[0].wait_recv()
    use(partner)
    for n, copy in zip(NEAR_FIRST, passed):
        copy.wait_recv()
        use(other_chip(chip, n) * 2 + core)
    return list(copies.values()) + passed


def fused_kernel(
    seq_ref, res_ref, *inputs_and_rest,
):
    hbm, rest = inputs_and_rest[:10], inputs_and_rest[10:]
    outs_and_scratch, vmem, load_sem = rest[:-11], rest[-11:-1], rest[-1]
    loads = [
        pltpu.make_async_copy(src, dst, load_sem.at[n])
        for n, (src, dst) in enumerate(zip(hbm, vmem))
    ]
    for n in (0, 1, 5, 7, 2, 3, 8, 4, 6, 9):
        loads[n].start()
    fused_body(loads, seq_ref, res_ref, *vmem, *outs_and_scratch)


def fused_body(
    loads, seq_ref, res_ref, align_ref, gain_ref, pair_ref, gm_ref, w_ref, resrow_ref, wl_ref,
    wr_ref, cot_ref, bias_ref,
    upd_ref, gl_ref, gr_ref, go_ref, gg_ref,
    gt_s, gs_s, ps_s, feat, near, gate_s, w2_s, w32_s, wr32_s, own_s, rin_s, rt_s, fr_s, lt_s, m_s, g_s, pre_s, n2_s,
    gr2_s, sb_s, rb_s, sm_s, rm_s, pk_s, pr_s,
    send_r, recv_r, send_n, recv_n, send_f, recv_f, send_x, recv_x, send_b, recv_b, send_m, recv_m,
    send_g, recv_g, send_h, recv_h, send_p, recv_p,
):
    me = lax.axis_index("row")
    core = lax.rem(me, 2)
    chip = lax.div(me, 2)
    x_at = lax.rem(chip, 2)
    z_at = lax.div(chip, 2)
    half = 1 - core
    _, chips, residues, lanes = feat.shape
    devices = 2 * chips
    planes = chips // 2
    s_loc, ch, _ = align_ref.shape
    rows, _, pc = pair_ref.shape
    width = wl_ref.shape[0]
    seqs = s_loc * devices
    partner = chip * 2 + 1 - core
    across = (z_at * 2 + 1 - x_at) * 2 + core
    wide = width // 2
    mine_wide = rows * seqs

    barrier = pltpu.get_barrier_semaphore()
    for k in range(1, devices):
        pl.semaphore_signal(
            barrier, inc=1, device_id={"row": lax.rem(me + k, devices)}, device_id_type=MESH
        )

    for n in (0, 1, 5, 7):
        loads[n].wait()
    parts = []
    for s in range(s_loc):
        value = align_ref[s].astype(F32)
        centred = value - jnp.mean(value, axis=0, keepdims=True)
        variance = jnp.mean(centred * centred, axis=0, keepdims=True)
        parts.append(centred * lax.rsqrt(variance + 1e-05))
    gain = jnp.concatenate([gain_ref[...]] * s_loc, axis=1)
    own = (jnp.transpose(jnp.concatenate(parts, axis=0)) * gain).astype(BF16)
    feat[core, x_at * planes + z_at] = own

    resrow = resrow_ref[...].astype(F32)
    wr32_s[...] = jnp.concatenate([wr_ref[...].astype(F32)] * s_loc, axis=1)
    lane_s = lax.div(lax.broadcasted_iota(jnp.int32, (wide, lanes), 1), ch)
    wr_parts = []
    for h in range(2):
        block = jnp.concatenate(
            [wr32_s[pl.ds(2 * h + t, chips, stride=4), :] for t in range(2)], axis=0
        )
        for s in range(s_loc):
            wr_parts.append(jnp.where(lane_s == s, block, 0.0))
    right = mm(jnp.concatenate(wr_parts, axis=0).astype(BF16), own, NT)
    flags = [seq_ref[me * s_loc + s].astype(F32) * resrow for s in range(s_loc)]
    for h in range(2):
        for s in range(s_loc):
            at = (h * s_loc + s) * wide
            own_s[h, s * wide : (s + 1) * wide, :] = (
                right[at : at + wide] * flags[s]
            ).astype(BF16)
    rin_s[half, me] = own_s[half]
    pl.semaphore_wait(barrier, devices - 1)

    rights = {}
    nears = []
    mine_at = feat.at[core, x_at * planes + z_at]
    for n in FAR_FIRST + (0,):
        to = other_chip(chip, n)
        window = pl.ds(pl.multiple_of(to * 2 * rows, 2 * rows), 2 * rows)
        nears.append(
            send(
                mine_at.at[window], near.at[core, chip], send_n.at[n], recv_n.at[n],
                to * 2 + 1 - core,
            )
        )
    for n in FAR_FIRST + (0,):
        to = other_chip(chip, n)
        if n > 0:
            at = 2 * n + 1
            rights[at] = send(
                own_s.at[half], rin_s.at[half, me], send_r.at[at], recv_r.at[at], to * 2 + core
            )
        at = 2 * n
        rights[at] = send(
            own_s.at[core], rin_s.at[core, me], send_r.at[at], recv_r.at[at], to * 2 + 1 - core
        )
    column = {}
    for n in (2, 4, 6):
        column[n] = send(
            mine_at, mine_at, send_f.at[n], recv_f.at[n], other_chip(chip, n) * 2 + core
        )
    sideways = [send(mine_at, mine_at, send_f.at[0], recv_f.at[0], across)]

    for n in (2, 3, 4, 6, 8, 9):
        loads[n].wait()
    gm = gm_ref[...]
    rescol = jnp.transpose(jnp.broadcast_to(resrow, (pc, residues)))
    seq = [seq_ref[s].astype(F32) for s in range(seqs)]
    both_rows = [res_ref[chip * 2 * rows + i].astype(F32) for i in range(2 * rows)]
    mine = [res_ref[me * rows + i].astype(F32) for i in range(rows)]
    row_total = seq[0]
    for s in range(1, seqs):
        row_total = row_total + seq[s]
    present = 1.0 / jnp.maximum(row_total * rescol, 1.0)
    inverse = [present * mine[i] + (1.0 - mine[i]) for i in range(rows)]
    for i in range(rows):
        gate = jax.nn.sigmoid(mm(pair_ref[i], gm))
        gate_s[i] = gate
        g_s[core, :, i * pc : (i + 1) * pc] = (
            cot_ref[i].astype(F32) * (gate * inverse[i])
        ).astype(BF16)
    crossing = send(g_s.at[core], g_s.at[core], send_x, recv_x, partner)

    w32_s[...] = w_ref[...].astype(F32)
    for h in range(2):
        for t in range(2):
            for k in range(chips):
                e, q = 4 * k + 2 * h + t, t * chips + k
                w2_s[h, :, q * pc : (q + 1) * pc] = w32_s[
                    pl.ds(e, width, stride=width), :
                ].astype(BF16)
    lane = lax.broadcasted_iota(jnp.int32, (1, 2 * mine_wide), 1)
    maskrow = jnp.zeros((1, 2 * mine_wide), F32)
    for s in range(s_loc):
        for d in range(devices):
            maskrow = jnp.where(lax.rem(lane, seqs) == s * devices + d, seq[d * s_loc + s], maskrow)
    resl = jnp.zeros((1, 2 * mine_wide), F32)
    for i in range(2 * rows):
        resl = jnp.where(lax.div(lane, seqs) == i, both_rows[i], resl)
    maskrow = maskrow * resl
    wlt = wl_ref[...].astype(F32)
    wlt2 = jnp.concatenate([wlt] * s_loc, axis=1).astype(BF16)

    for copy in nears:
        copy.wait_recv()
    near_pass = send(near.at[half], near.at[half], send_n.at[chips], recv_n.at[chips], partner)
    near_pass.wait_recv()
    for d in range(devices):
        fr_s[d * 2 * rows : (d + 1) * 2 * rows, :] = near[d % 2, d // 2].astype(F32)
    lane_d = lax.div(lax.broadcasted_iota(jnp.int32, (devices, lanes), 1), ch)
    pieces = []
    for i in range(2 * rows):
        block = fr_s[pl.ds(i, devices, stride=2 * rows), :]
        for s in range(s_loc):
            pieces.append(jnp.where(lane_d == s, block, 0.0))
    fr = jnp.concatenate(pieces, axis=0).astype(BF16)
    left_t = mm(wlt2, fr, NT) * maskrow
    for c in range(2):
        lt_s[c] = left_t[:, c * mine_wide : (c + 1) * mine_wide]
    left_t = left_t.astype(BF16)

    left = jnp.transpose(lt_s[core]).astype(BF16)
    for h in range(2):
        for e in range(0, wide, 2):
            part = mm(left, w2_s[h, :, e * pc : (e + 2) * pc]).astype(BF16)
            for n in range(2):
                at = (h * wide + e + n) * seqs
                for i in range(rows):
                    m_s[at : at + seqs, i * pc : (i + 1) * pc] = part[
                        i * seqs : (i + 1) * seqs, n * pc : (n + 1) * pc
                    ]

    def lay_out(h, d):
        for s in range(s_loc):
            rt_s[h, pl.ds(s * devices + d, wide, stride=seqs), :] = rin_s[
                h, d, s * wide : (s + 1) * wide, :
            ].astype(F32)

    crossing.wait_recv()
    lay_out(half, me)
    for n in (0,) + NEAR_FIRST:
        source = other_chip(chip, n) * 2
        rights[2 * n].wait_recv()
        lay_out(half, source + 1 - core)
        if n > 0:
            rights[2 * n + 1].wait_recv()
            lay_out(half, source + core)
    right_pass = send(
        rin_s.at[half], rin_s.at[half], send_r.at[1], recv_r.at[1], partner
    )
    rtt = rt_s[half].astype(BF16)
    scatter = {}
    group = 4
    for first in range(0, chips, group):
        for t in range(2):
            at = t * chips + first
            for c in range(2):
                part = mm(rtt[at * seqs : (at + group) * seqs], g_s[c]).astype(BF16)
                for h in range(group):
                    for i in range(rows):
                        to = (c * rows + i) * seqs
                        n2_s[to : to + seqs, (at + h) * pc : (at + h + 1) * pc] = part[
                            h * seqs : (h + 1) * seqs, i * pc : (i + 1) * pc
                        ]
        for t in range(2):
            at = t * chips + first
            go = mm(left_t, n2_s[:, at * pc : (at + group) * pc])
            for h in range(group):
                sb_s[first + h, t * width : (t + 1) * width, :] = go[
                    :, h * pc : (h + 1) * pc
                ].astype(BF16)
        for k in range(first, first + group):
            n = lax.rem(k - chip + chips, chips)
            scatter[k] = send(
                sb_s.at[k], rb_s.at[n], send_b.at[n], recv_b.at[n], k * 2 + 1 - core
            )

    right_pass.wait_recv()
    for d in range(devices):
        lay_out(core, d)
    rt = jnp.transpose(rt_s[...].reshape(width * seqs, residues)).astype(BF16)

    for n in (2, 4, 6):
        column[n].wait_recv()
        block = feat.at[core, x_at * planes + lax.div(other_chip(chip, n), 2)]
        at = n + 1
        sideways.append(send(block, block, send_f.at[at], recv_f.at[at], across))
    block = feat.at[core, pl.ds(x_at * planes, planes)]
    feat_pass = [send(block, block, send_f.at[1], recv_f.at[1], partner)]

    bias = bias_ref[...]
    for i in range(0, rows, 2):
        lin2 = mm(rt, m_s[:, i * pc : (i + 2) * pc])
        for h in range(2):
            linear = lin2[:, h * pc : (h + 1) * pc] + bias
            gate = gate_s[i + h]
            scaled = gate * inverse[i + h]
            upd_ref[i + h] = (scaled * linear).astype(BF16)
            pre_s[(i + h) * residues : (i + h + 1) * residues, :] = (
                cot_ref[i + h].astype(F32) * scaled * linear * (1.0 - gate)
            ).astype(BF16)
    gg = mm(pair_ref[...].reshape(rows * residues, pc), pre_s[...], TN)
    g_rows = pc // chips
    sm_s[...] = gg.reshape(chips, g_rows, pc).astype(BF16)

    def portion(k):
        to = lax.rem(chip + k, chips)
        return pltpu.make_async_remote_copy(
            src_ref=sm_s.at[to], dst_ref=rm_s.at[2 * k + core], send_sem=send_m.at[k],
            recv_sem=recv_m.at[2 * k + core], device_id={"row": to * 2 + 1}, device_id_type=MESH,
        )

    def arrived(k, c):
        return pltpu.make_async_remote_copy(
            src_ref=sm_s.at[0], dst_ref=rm_s.at[2 * k + c], send_sem=send_m.at[k],
            recv_sem=recv_m.at[2 * k + c], device_id={"row": partner}, device_id_type=MESH,
        )

    @pl.when(core == 0)
    def _():
        portion(0).start()

    for k in range(1, chips):
        portion(k).start()

    act = mm(w2_s[half], n2_s[...], NT) * maskrow
    gl2 = mm(act.astype(BF16), fr)
    gl = gl2[:, :ch]
    for s in range(1, s_loc):
        gl = gl + gl2[:, s * ch : (s + 1) * ch]

    back = mm(m_s[...], g_s[core], NT)
    rt_s[...] = back.reshape(2, wide * seqs, residues)
    for p in range(2):
        for n in range(chips):
            b = p * chips + n
            d = (n % planes) * 4 + (n // planes) * 2 + p
            for s in range(s_loc):
                flag = seq[d * s_loc + s] * resrow
                for h in range(2):
                    at = s * width + h * wide
                    gr2_s[at : at + wide, b * residues : (b + 1) * residues] = (
                        rt_s[h, pl.ds(s * devices + d, wide, stride=seqs), :] * flag
                    )
    total = jnp.zeros(rb_s.shape[1:], F32)
    for n in range(chips):
        pltpu.make_async_remote_copy(
            src_ref=sb_s.at[0], dst_ref=rb_s.at[n], send_sem=send_b.at[n], recv_sem=recv_b.at[n],
            device_id={"row": partner}, device_id_type=MESH,
        ).wait_recv()
        total = total + rb_s[n].astype(F32)
    gt_s[me] = total.astype(BF16)
    copies = gather_start(gt_s, me, core, chip, send_g, recv_g)

    for copy in sideways:
        copy.wait_recv()
    block = feat.at[core, pl.ds((1 - x_at) * planes, planes)]
    at = 2 * planes
    feat_pass.append(send(block, block, send_f.at[at], recv_f.at[at], partner))

    def spread(k, c):
        block = gs_s.at[chip]
        return pltpu.make_async_remote_copy(
            src_ref=block, dst_ref=block, send_sem=send_h.at[2 * k + c], recv_sem=recv_h.at[k],
            device_id={"row": lax.rem(chip + k, chips) * 2 + c}, device_id_type=MESH,
        )

    def landed(k):
        block = gs_s.at[lax.rem(chip - k + chips, chips)]
        return pltpu.make_async_remote_copy(
            src_ref=block, dst_ref=block, send_sem=send_h.at[2 * k], recv_sem=recv_h.at[k],
            device_id={"row": partner}, device_id_type=MESH,
        )

    @pl.when(core == 1)
    def _():
        total = sm_s[chip].astype(F32)
        arrived(0, 0).wait_recv()
        total = total + rm_s[0].astype(F32)
        for k in range(1, chips):
            for c in range(2):
                arrived(k, c).wait_recv()
                total = total + rm_s[2 * k + c].astype(F32)
        gs_s[chip] = total.astype(BF16)
        spread(0, 0).start()
        for k in range(1, chips):
            for c in range(2):
                spread(k, c).start()

    for copy in feat_pass:
        copy.wait_recv()
    feats = feat[...].reshape(devices * residues, lanes)
    gr2 = mm(gr2_s[...].astype(BF16), feats)
    gr = gr2[:width, :ch]
    for s in range(1, s_loc):
        gr = gr + gr2[s * width : (s + 1) * width, s * ch : (s + 1) * ch]

    pk_s[0] = jnp.concatenate([gl[:wide], gl[wide:]], axis=1)
    pk_s[1] = jnp.concatenate([gr[:wide], gr[wide:]], axis=1)
    twin = send(pk_s.at[half], pr_s, send_p.at[1], recv_p.at[1], partner)

    twin.wait_recv()
    ps_s[me] = (pk_s[core] + pr_s[...]).astype(BF16)
    last = []
    block = ps_s.at[me]
    for n in FAR_FIRST + (0,):
        to = other_chip(chip, n) * 2
        if n > 0:
            at = 2 * n + 1
            last.append(send(block, block, send_p.at[at], recv_p.at[at], to + core))
        at = 2 * n
        last.append(send(block, block, send_p.at[at], recv_p.at[at], to + 1 - core))

    def place(d):
        for t in range(2):
            go_ref[pl.ds(2 * d + t, width, stride=width), :] = gt_s[
                d, t * width : (t + 1) * width, :
            ].astype(F32)

    place(me)
    done2 = gather_finish(copies, gt_s, core, chip, chips, send_g, recv_g, place)
    for copy in last:
        copy.wait_recv()

    @pl.when(core == 0)
    def _():
        landed(0).wait_recv()
        portion(0).wait_send()

    for k in range(1, chips):
        landed(k).wait_recv()
        portion(k).wait_send()

    @pl.when(core == 1)
    def _():
        spread(0, 0).wait_send()
        for k in range(1, chips):
            for c in range(2):
                spread(k, c).wait_send()

    for k in range(chips):
        gg_ref[k * g_rows : (k + 1) * g_rows, :] = gs_s[k].astype(F32)
    gl, gr = ps_s[0].astype(F32), ps_s[1].astype(F32)
    for d in range(2, devices, 2):
        gl = gl + ps_s[d].astype(F32)
        gr = gr + ps_s[d + 1].astype(F32)
    for h in range(2):
        gl_ref[h * wide : (h + 1) * wide, :] = gl[:, h * ch : (h + 1) * ch]
        for t in range(2):
            gr_ref[pl.ds(2 * h + t, chips, stride=4), :] = gr[
                t * chips : (t + 1) * chips, h * ch : (h + 1) * ch
            ]
    for copy in (
        nears + [near_pass] + list(rights.values()) + [right_pass] + list(column.values()) + sideways + feat_pass + [crossing]
        + list(scatter.values()) + [twin] + done2 + last
    ):
        copy.wait_send()


def store_kernel(*refs):
    copies = [
        pltpu.make_async_copy(refs[n], refs[5 + n], refs[10].at[n]) for n in (3, 0, 4, 1, 2)
    ]
    for copy in copies:
        copy.start()
    for copy in copies:
        copy.wait()


def fused_device(
    alignment_state, pair_state, cotangent, sequence_row_mask, residue_mask, norm_gain_vector,
    left_matrix_weight, right_matrix_weight, output_weight, output_bias, gate_matrix,
):
    s_loc, residues, ch = alignment_state.shape
    rows, _, pc = pair_state.shape
    width = left_matrix_weight.shape[1]
    devices = lax.axis_size("row")
    seqs = s_loc * devices
    chips = devices // 2
    lanes = s_loc * ch
    top = (width // devices) * width
    smem = pl.BlockSpec(memory_space=pltpu.SMEM)
    vmem = pl.BlockSpec(memory_space=pltpu.VMEM)
    dma = pltpu.SemaphoreType.DMA
    inputs = (
        alignment_state.transpose(0, 2, 1),
        norm_gain_vector.reshape(1, ch),
        pair_state,
        gate_matrix,
        output_weight,
        residue_mask.reshape(1, residues),
        left_matrix_weight.T,
        right_matrix_weight.T,
        cotangent,
        output_bias.reshape(1, pc),
    )
    results = pl.pallas_call(
        fused_kernel,
        name="fused",
        out_shape=(
            pltpu.VMEM((rows, residues, pc), BF16),
            pltpu.VMEM((width, ch), F32),
            pltpu.VMEM((width, ch), F32),
            pltpu.VMEM((width * width, pc), F32),
            pltpu.VMEM((pc, pc), F32),
        ),
        in_specs=[smem, smem] + [pl.BlockSpec(memory_space=pltpu.HBM)] * 10,
        out_specs=(vmem,) * 5,
        scratch_shapes=[
            pltpu.VMEM((devices, top, pc), BF16),
            pltpu.VMEM((chips, pc // chips, pc), BF16),
            pltpu.VMEM((devices, width // 2, 2 * ch), BF16),
            pltpu.VMEM((2, chips, residues, lanes), BF16),
            pltpu.VMEM((2, chips, 2 * rows, lanes), BF16),
            pltpu.VMEM((rows, residues, pc), F32),
            pltpu.VMEM((2, width, width // 2 * pc), BF16),
            pltpu.VMEM((width * width, pc), F32),
            pltpu.VMEM((width, lanes), F32),
            pltpu.VMEM((2, s_loc * width // 2, residues), BF16),
            pltpu.VMEM((2, devices, s_loc * width // 2, residues), BF16),
            pltpu.VMEM((2, width // 2 * seqs, residues), F32),
            pltpu.VMEM((devices * 2 * rows, lanes), F32),
            pltpu.VMEM((2, width, rows * seqs), F32),
            pltpu.VMEM((width * seqs, rows * pc), BF16),
            pltpu.VMEM((2, residues, rows * pc), BF16),
            pltpu.VMEM((rows * residues, pc), BF16),
            pltpu.VMEM((2 * rows * seqs, width // 2 * pc), BF16),
            pltpu.VMEM((s_loc * width, devices * residues), F32),
            pltpu.VMEM((chips, top, pc), BF16),
            pltpu.VMEM((chips, top, pc), BF16),
            pltpu.VMEM((chips, pc // chips, pc), BF16),
            pltpu.VMEM((devices, pc // chips, pc), BF16),
            pltpu.VMEM((2, width // 2, 2 * ch), F32),
            pltpu.VMEM((width // 2, 2 * ch), F32),
            dma((devices,)),
            dma((devices,)),
            dma((chips + 1,)),
            dma((chips + 1,)),
            dma((chips + 1,)),
            dma((chips + 1,)),
            dma,
            dma,
            dma((chips,)),
            dma((chips,)),
            dma((chips,)),
            dma((devices,)),
            dma((2 * chips,)),
            dma((2 * chips,)),
            dma((devices,)),
            dma((chips,)),
            dma((devices,)),
            dma((devices,)),
        ]
        + [pltpu.VMEM(value.shape, value.dtype) for value in inputs]
        + [dma((len(inputs),))],
        compiler_params=pltpu.CompilerParams(
            collective_id=0, has_side_effects=True, vmem_limit_bytes=61 * 1024 * 1024
        ),
    )(sequence_row_mask, residue_mask, *inputs)
    update, left_t, right_t, grad_out, grad_gate = pl.pallas_call(
        store_kernel,
        name="store",
        out_shape=(
            jax.ShapeDtypeStruct((rows, residues, pc), BF16),
            jax.ShapeDtypeStruct((width, ch), F32),
            jax.ShapeDtypeStruct((width, ch), F32),
            jax.ShapeDtypeStruct((width * width, pc), F32),
            jax.ShapeDtypeStruct((pc, pc), F32),
        ),
        in_specs=[vmem] * 5,
        out_specs=(pl.BlockSpec(memory_space=pltpu.HBM),) * 5,
        scratch_shapes=[dma((5,))],
        compiler_params=pltpu.CompilerParams(vmem_limit_bytes=32 * 1024 * 1024),
    )(*results)
    return update, left_t.T, right_t.T, grad_out, grad_gate


def per_device(*arrays):
    alignment_state, pair_state = arrays[0], arrays[1]
    s_loc, residues, ch = alignment_state.shape
    rows, _, pc = pair_state.shape
    width = arrays[6].shape[1]
    devices = lax.axis_size("row")
    fits = (
        lax.axis_size("col") == 1
        and devices % 2 == 0
        and (s_loc * ch, pc, residues) == (128, 128, 128)
        and rows == 8
        and width % devices == 0
        and pc == devices * 8
        and s_loc * devices == 32
    )
    return fused_device(*arrays) if fits else general_device(*arrays)


def solution(mesh):
    return jax.shard_map(
        per_device,
        mesh=mesh,
        in_specs=(
            P(("grp", "row"), "col", None),
            P(("grp", "row"), "col", None),
            P(("grp", "row"), "col", None),
            P("grp"),
            P("grp"),
            P(),
            P(),
            P(),
            P(),
            P(),
            P(),
        ),
        out_specs=(
            P(("grp", "row"), "col", None),
            P("grp", None),
            P("grp", None),
            P("grp", None),
            P("grp", None),
        ),
        check_vma=False,
    )
```
